32 devices in a mesh: narrow: 4 (over x, core), wide: 8 (over z, y).
Axes of the slice: x: 2, y: 2, z: 4, core: 2. Of those that a mesh axis runs over, the one named last changes fastest.
Arguments:
- targets: bfloat16 [64, 288, 768], P(('narrow', 'wide')), may hold values from -6 to 6
- memory: bfloat16 [64, 1024, 768], P('narrow', 'wide'), may hold values from -6 to 6
- cotangent: bfloat16 [64, 288, 768], P(('narrow', 'wide')), may hold values from -6 to 6
- target_len: int32 [64], P(('narrow', 'wide')), may hold values from 1 to 288, 13824 in all
- memory_len: int32 [64], P(('narrow', 'wide')), may hold values from 1 to 1024, 49152 in all
- self_query: bfloat16 [768, 768], P(('narrow', 'wide')), may hold values from -0.109375 to 0.109375
- self_key: bfloat16 [768, 768], P(('narrow', 'wide')), may hold values from -0.109375 to 0.109375
- self_value: bfloat16 [768, 768], P(('narrow', 'wide')), may hold values from -0.21875 to 0.21875
- self_out: bfloat16 [768, 768], P(('narrow', 'wide')), may hold values from -0.625 to 0.625
- cross_query: bfloat16 [768, 768], P(('narrow', 'wide')), may hold values from -0.109375 to 0.109375
- cross_key: bfloat16 [768, 768], P(('narrow', 'wide')), may hold values from -0.109375 to 0.109375
- cross_value: bfloat16 [768, 768], P(('narrow', 'wide')), may hold values from -0.21875 to 0.21875
- cross_out: bfloat16 [768, 768], P(('narrow', 'wide')), may hold values from -0.875 to 0.875
- ff_gate: bfloat16 [768, 2048], P(('narrow', 'wide')), may hold values from -0.21875 to 0.21875
- ff_up: bfloat16 [768, 2048], P(('narrow', 'wide')), may hold values from -0.21875 to 0.21875
- ff_down: bfloat16 [2048, 768], P(('narrow', 'wide')), may hold values from -0.1875 to 0.1875
- self_gain: bfloat16 [768], P(('narrow', 'wide')), may hold values from 0.5 to 1.5
- cross_gain: bfloat16 [768], P(('narrow', 'wide')), may hold values from 0.5 to 1.5
- ff_gain: bfloat16 [768], P(('narrow', 'wide')), may hold values from 0.5 to 1.5
- position_bias: bfloat16 [32, 12], replicated, may hold values from -4 to 4
Outputs:
- layer_out: bfloat16 [64, 288, 768], P(('narrow', 'wide'))
- grad_targets: float32 [64, 288, 768], P(('narrow', 'wide'))
- grad_memory: float32 [64, 1024, 768], P('narrow', 'wide')
- grad_self_query: float32 [768, 768], P(('narrow', 'wide'))
- grad_self_key: float32 [768, 768], P(('narrow', 'wide'))
- grad_self_value: float32 [768, 768], P(('narrow', 'wide'))
- grad_self_out: float32 [768, 768], P(('narrow', 'wide'))
- grad_cross_query: float32 [768, 768], P(('narrow', 'wide'))
- grad_cross_key: float32 [768, 768], P(('narrow', 'wide'))
- grad_cross_value: float32 [768, 768], P(('narrow', 'wide'))
- grad_cross_out: float32 [768, 768], P(('narrow', 'wide'))
- grad_ff_gate: float32 [768, 2048], P(('narrow', 'wide'))
- grad_ff_up: float32 [768, 2048], P(('narrow', 'wide'))
- grad_ff_down: float32 [2048, 768], P(('narrow', 'wide'))
- grad_self_gain: float32 [768], P(('narrow', 'wide'))
- grad_cross_gain: float32 [768], P(('narrow', 'wide'))
- grad_ff_gain: float32 [768], P(('narrow', 'wide'))
- grad_position_bias: float32 [32, 12], replicated
The draws below stay inside these ranges and needn't reach their ends.
Inputs may be any that keep to these rules, and one draw needn't show every extreme that they name: `target_len`: at least one pair has 288 live target slots. `memory_len`: at least one pair has 1024 live memory rows.
All inputs are finite; a program needn't handle non-finite values. No bound on the sum of `target_len` or of `memory_len` on one device may be relied on, other than what follows from the above.
Results may differ from the reference program's by a relative error of at most 0.025.
The reference program's roundings to bfloat16 on the way count: a program that leaves them out, or rounds other values in their place, can miss the bound.
Values may be sent and summed in bfloat16 or wider, within the bound.
No kernel may reach another device: no remote copies, remote signals or barrier semaphores. Data moves between devices by JAX's collectives and lax.ppermute only.
A program may use at most 256 MiB of HBM per device.

```python
import math
import jax
import jax.numpy as jnp
import numpy as np
from jax import lax

D = 768
HEADS = 12
HEAD_DIM = 64
FF = 2048
BUCKETS = 32
REACH = 128
TGT = 288
MEM = 1024
PAIR_DEV = 2
PAIRS = 64


def levels(stream_key, extent, split, low, largest):
    def one(dim, parts):
        steps = jax.random.uniform(jax.random.fold_in(jax.random.fold_in(stream_key, 6), dim), (parts,), jnp.float32, low / len(split), largest / len(split))
        return jnp.repeat(jnp.exp(steps), extent[dim] // parts).reshape((-1,) + (1,) * (len(extent) - dim - 1))

    factor_of = one(*split[0])
    for cut in split[1:]:
        factor_of = factor_of * one(*cut)
    return factor_of


def split_up(number_of, total, most, lean):
    weights = [(1 << 20) // math.isqrt(standing ** lean) + 1 for standing in range(2, number_of + 1)]
    rest, given = total - most - (number_of - 1), [1] * (number_of - 1)
    while rest > 0:
        free = [i for i in range(number_of - 1) if given[i] < most]
        pool, budget = sum([weights[i] for i in free]), rest
        for i in free:
            more = min(most - given[i], max(1, budget * weights[i] // pool), rest)
            given[i] = given[i] + more
            rest = rest - more
    return np.array([most] + given)


def uneven(stream_key, amount, total, most, slope):
    if amount == 2:
        one = jax.random.randint(stream_key, (), max(1, total - most), min(most, total - 1) + 1)
        return jnp.stack([one, total - one])
    tallies = jnp.asarray(split_up(amount, total, most, slope), jnp.int32)
    couples = (amount - 1) // 2
    source_of, sink = tallies[1:1 + 2 * couples:2], tallies[2:2 + 2 * couples:2]
    room = jnp.minimum(source_of - 1, most - sink)
    shifted = jax.random.randint(jax.random.fold_in(stream_key, 1), (couples,), 0, 1 << 20) % (room + 1)
    tallies = tallies.at[1:1 + 2 * couples:2].set(source_of - shifted).at[2:2 + 2 * couples:2].set(sink + shifted)
    return tallies[jax.random.permutation(jax.random.fold_in(stream_key, 2), amount)]


def gaussian(key, dims, scale, limit, split=(), kind=jnp.bfloat16):
    array = jax.random.normal(key, dims, jnp.float32) * scale
    if len(split) > 0:
        array = levels(key, dims, split, -0.22, 0.18) * array
    return jnp.clip(array, min=-limit, max=limit).astype(kind)


def setup_inputs(seed: int = 0) -> dict:
    key_of = jax.random.split(jax.random.key(seed), 21)
    return {
        "targets": gaussian(key_of[0], (PAIRS, TGT, D), 1.0, 6.0, ((0, 32),)),
        "memory": gaussian(key_of[1], (PAIRS, MEM, D), 1.0, 6.0, ((0, 4), (1, 8))),
        "cotangent": gaussian(key_of[2], (PAIRS, TGT, D), 1.0, 6.0, ((0, 32),)),
        "target_len": uneven(key_of[3], PAIRS, PAIRS * TGT * 3 // 4, TGT, 0).astype(jnp.int32),
        "memory_len": uneven(key_of[4], PAIRS, PAIRS * MEM * 3 // 4, MEM, 0).astype(jnp.int32),
        "self_query": gaussian(key_of[5], (D, D), (4 * D) ** -0.5, 0.109375, ((0, 32),)),
        "self_key": gaussian(key_of[6], (D, D), (4 * D) ** -0.5, 0.109375, ((0, 32),)),
        "self_value": gaussian(key_of[7], (D, D), D ** -0.5, 0.21875, ((0, 32),)),
        "self_out": gaussian(key_of[8], (D, D), (D // 8) ** -0.5, 0.625, ((0, 32),)),
        "cross_query": gaussian(key_of[9], (D, D), (4 * D) ** -0.5, 0.109375, ((0, 32),)),
        "cross_key": gaussian(key_of[10], (D, D), (4 * D) ** -0.5, 0.109375, ((0, 32),)),
        "cross_value": gaussian(key_of[11], (D, D), D ** -0.5, 0.21875, ((0, 32),)),
        "cross_out": gaussian(key_of[12], (D, D), (D // 16) ** -0.5, 0.875, ((0, 32),)),
        "ff_gate": gaussian(key_of[13], (D, FF), D ** -0.5, 0.21875, ((0, 32),)),
        "ff_up": gaussian(key_of[14], (D, FF), D ** -0.5, 0.21875, ((0, 32),)),
        "ff_down": gaussian(key_of[15], (FF, D), (FF // 2) ** -0.5, 0.1875, ((0, 32),)),
        "self_gain": jnp.clip(1.0 + 0.1 * jax.random.normal(key_of[16], (D,), jnp.float32), 0.5, 1.5).astype(jnp.bfloat16),
        "cross_gain": jnp.clip(1.0 + 0.1 * jax.random.normal(key_of[17], (D,), jnp.float32), 0.5, 1.5).astype(jnp.bfloat16),
        "ff_gain": jnp.clip(1.0 + 0.1 * jax.random.normal(key_of[18], (D,), jnp.float32), 0.5, 1.5).astype(jnp.bfloat16),
        "position_bias": gaussian(key_of[19], (BUCKETS, HEADS), 1.0, 4.0),
    }


negative = -1e+30
epsilon = 1e-06

@jax.custom_vjp
def low(v):
    return lax.optimization_barrier(v.astype(jnp.bfloat16)).astype(jnp.float32)

@jax.custom_vjp
def low_back(v):
    return v

def low_keep(v):
    return (low(v), None)

def low_pass(kept, grad):
    return (grad,)

def back_keep(v):
    return (v, None)

def back_low(kept, grad):
    return (low(grad),)
low.defvjp(low_keep, low_pass)
low_back.defvjp(back_keep, back_low)

def bucket_matrix(length, buckets, reach):
    rows = np.arange(length)[:, None]
    cols = np.arange(length)[None, :]
    apart = np.maximum(rows - cols, 0)
    exact = buckets // 2
    safe = np.maximum(apart, 1)
    far = exact + (np.log(safe / exact) / np.log(reach / exact) * (buckets - exact)).astype(np.int64)
    far = np.minimum(far, buckets - 1)
    return np.where(apart < exact, apart, far).astype(np.int32)

def both(value):
    return low_back(low(value))

def matmul(left, weight):
    return jnp.einsum('pld,de->ple', left, weight, precision=lax.Precision.HIGHEST)

def rms_norm(value, gain):
    return value * lax.rsqrt(lax.optimization_barrier(jnp.mean(value * value, axis=-1, keepdims=True)) + epsilon) * gain

def attend(query, keys, values, bias, mask):
    pairs, rows_q, _ = query.shape
    rows_k = keys.shape[1]
    query_h = query.reshape(pairs, rows_q, HEADS, HEAD_DIM)
    keys_h = keys.reshape(pairs, rows_k, HEADS, HEAD_DIM)
    values_h = values.reshape(pairs, rows_k, HEADS, HEAD_DIM)
    scores = jnp.einsum('pqhd,pkhd->phqk', query_h, keys_h, precision=lax.Precision.HIGHEST) + bias
    scores = low_back(scores)
    scores = jnp.where(mask, scores, negative)
    probs = jax.nn.softmax(scores, axis=-1)
    mixed = jnp.einsum('phqk,pkhd->pqhd', low(probs), values_h, precision=lax.Precision.HIGHEST)
    return both(mixed.reshape(pairs, rows_q, HEADS * HEAD_DIM))

def layer(params, targets, memory, target_len, memory_len):
    s_query, s_key, s_value, s_out, c_query, c_key, c_value, c_out, f_gate, f_up, f_down, gain_one, gain_two, gain_three, pos_bias = params
    places = jnp.arange(TGT)
    causal = (places[:, None] >= places[None, :])[None, None]
    table = jnp.asarray(bucket_matrix(TGT, BUCKETS, REACH))
    bias = jnp.transpose(pos_bias[table], (2, 0, 1))[None]
    normed_one = low(rms_norm(targets, gain_one))
    mixed_one = attend(both(matmul(normed_one, s_query)), both(matmul(normed_one, s_key)), both(matmul(normed_one, s_value)), bias, causal)
    first = targets + low_back(matmul(mixed_one, s_out))
    normed_two = low(rms_norm(first, gain_two))
    mem_mask = (jnp.arange(MEM)[None, :] < memory_len[:, None])[:, None, None, :]
    mixed_two = attend(both(matmul(normed_two, c_query)), both(matmul(memory, c_key)), both(matmul(memory, c_value)), 0.0, mem_mask)
    second = first + low_back(matmul(mixed_two, c_out))
    third_normalized_rows = low(rms_norm(second, gain_three))
    gate = low_back(matmul(third_normalized_rows, f_gate))
    upward = low_back(matmul(third_normalized_rows, f_up))
    hidden = low(jax.nn.gelu(gate, approximate=True) * upward)
    third = second + low_back(matmul(hidden, f_down))
    live = (places[None, :] < target_len[:, None]).astype(jnp.float32)[:, :, None]
    return third * live

def reference(targets, memory, cotangent, target_len, memory_len, self_query, self_key, self_value, self_out, cross_query, cross_key, cross_value, cross_out, ff_gate, ff_up, ff_down, self_gain, cross_gain, ff_gain, position_bias):
    params = tuple((w.astype(jnp.float32) for w in (self_query, self_key, self_value, self_out, cross_query, cross_key, cross_value, cross_out, ff_gate, ff_up, ff_down, self_gain, cross_gain, ff_gain, position_bias)))
    groups = PAIRS // PAIR_DEV

    def grouped(value):
        return value.reshape((groups, PAIR_DEV) + value.shape[1:])

    def step(carry, items):
        inputs, rows, grads_in, t_len, m_len = items

        def forward(weights, values, mem):
            return layer(weights, values, mem, t_len, m_len)
        result, pull = jax.vjp(forward, params, inputs, rows)
        d_params, d_inputs, d_rows = pull(grads_in)
        carry = jax.tree.map(lambda a, b: a + b, carry, d_params)
        return (carry, (result.astype(jnp.bfloat16), d_inputs, d_rows))
    start = jax.tree.map(jnp.zeros_like, params)
    items = (grouped(targets.astype(jnp.float32)), grouped(memory.astype(jnp.float32)), grouped(cotangent.astype(jnp.float32)), grouped(target_len), grouped(memory_len))
    totals, (outputs, d_targets, d_memory) = lax.scan(step, start, items)
    layer_out = outputs.reshape(PAIRS, TGT, D)
    grad_targets = d_targets.reshape(PAIRS, TGT, D).astype(jnp.float32)
    grad_memory = d_memory.reshape(PAIRS, MEM, D).astype(jnp.float32)
    grads = tuple((g.astype(jnp.float32) for g in totals))
    return (layer_out, grad_targets, grad_memory, grads[0], grads[1], grads[2], grads[3], grads[4], grads[5], grads[6], grads[7], grads[8], grads[9], grads[10], grads[11], grads[12], grads[13], grads[14])
```

```python
import jax
import jax.numpy as jnp
import numpy as np
from jax import lax
from jax.experimental import pallas as pl
from jax.experimental.pallas import tpu as pltpu
from jax.sharding import PartitionSpec as P

HEADS = 12
HEAD_DIM = 64
BUCKETS = 32
REACH = 128
LANES = 128
BOTH = ("narrow", "wide")

negative = -1e30
epsilon = 1e-06
bf16 = jnp.bfloat16
f32 = jnp.float32

NT = (((1,), (1,)), ((), ()))
NN = (((1,), (0,)), ((), ()))
TN = (((0,), (0,)), ((), ()))


def dot(left, right, dims):
    return lax.dot_general(left, right, dims, preferred_element_type=f32)


def bucket_of_distance(length, buckets, reach):
    apart = np.arange(length)
    exact = buckets // 2
    safe = np.maximum(apart, 1)
    far = exact + (np.log(safe / exact) / np.log(reach / exact) * (buckets - exact)).astype(
        np.int64
    )
    far = np.minimum(far, buckets - 1)
    return np.where(apart < exact, apart, far).astype(np.int32)


def of_head(h, first, value):
    return jnp.where(first if h == 0 else ~first, value, jnp.zeros_like(value))


def self_forward_kernel(q_ref, k_ref, v_ref, bias_ref, mixed_ref, total_ref):
    q, k, v = q_ref[0], k_ref[0], v_ref[0]
    first = lax.broadcasted_iota(jnp.int32, q.shape, 1) < HEAD_DIM
    mixed, totals = [], []
    for h in range(2):
        scores = dot(of_head(h, first, q), k, NT) + bias_ref[h].astype(f32)
        top = jnp.max(scores, axis=1, keepdims=True)
        grown = jnp.exp(scores - top)
        total = jnp.sum(grown, axis=1, keepdims=True)
        mixed.append(dot((grown * (1.0 / total)).astype(bf16), v, NN))
        totals.append(top + jnp.log(total))
    mixed_ref[0] = jnp.where(first, mixed[0], mixed[1]).astype(bf16)
    total_ref[0] = jnp.where(first, totals[0], totals[1])


def self_forward(qkv, bias):
    pairs, length, width = qkv.shape
    width //= 3
    steps = width // LANES
    part = lambda c: pl.BlockSpec((1, length, LANES), lambda p, h: (p, 0, h + c * steps))
    return pl.pallas_call(
        self_forward_kernel,
        out_shape=(
            jax.ShapeDtypeStruct((pairs, length, width), bf16),
            jax.ShapeDtypeStruct((pairs, length, width), f32),
        ),
        grid=(pairs, steps),
        in_specs=[
            part(0),
            part(1),
            part(2),
            pl.BlockSpec((2, length, length), lambda p, h: (h, 0, 0)),
        ],
        out_specs=[part(0), part(0)],
        cost_estimate=pl.CostEstimate(
            flops=pairs * HEADS * length * length * HEAD_DIM * 4,
            transcendentals=pairs * HEADS * length * length,
            bytes_accessed=pairs * length * width * 12,
        ),
        name="self_forward",
    )(qkv, qkv, qkv, bias)


def self_backward_kernel(
    q_ref, k_ref, v_ref, bias_ref, total_ref, grad_ref, grads_ref, diagonal_ref, sum_ref
):
    p, hp = pl.program_id(0), pl.program_id(1)
    steps = pl.num_programs(1)
    q, k, v, grad, total = q_ref[0], k_ref[0], v_ref[0], grad_ref[0], total_ref[0]
    length, padded = q.shape[0], sum_ref.shape[-1]
    first = lax.broadcasted_iota(jnp.int32, q.shape, 1) < HEAD_DIM

    @pl.when(p == 0)
    def _():
        sum_ref[hp] = jnp.zeros(sum_ref.shape[1:], f32)

    found = []
    for h in range(2):
        scores = dot(of_head(h, first, q), k, NT) + bias_ref[h].astype(f32)
        probs = jnp.exp(scores - total[:, HEAD_DIM * h : HEAD_DIM * h + 1])
        grad_probs = dot(of_head(h, first, grad), v, NT)
        inner = jnp.sum(probs * grad_probs, axis=1, keepdims=True)
        grad_scores = (probs * (grad_probs - inner)).astype(bf16)
        sum_ref[hp, h, :, :length] += grad_scores.astype(f32)
        found.append(
            (
                dot(grad_scores, k, NN),
                dot(grad_scores, q, TN),
                dot(probs.astype(bf16), grad, TN),
            )
        )
    for c in range(3):
        grads_ref[0, :, pl.ds(pl.multiple_of((hp + c * steps) * LANES, LANES), LANES)] = (
            jnp.where(first, found[0][c], found[1][c]).astype(bf16)
        )

    @pl.when(p == pl.num_programs(0) - 1)
    def _():
        rows = lax.broadcasted_iota(jnp.int32, (8, padded), 0)
        for h in range(2):
            held = sum_ref[hp, h, 0:8, :]
            for i in range(8, length, 8):
                held = held + pltpu.roll(sum_ref[hp, h, i : i + 8, :], padded - i, 1)
            for bit in (1, 2, 4):
                held = jnp.where(
                    (rows // bit) % 2 == 1, pltpu.roll(held, padded - bit, 1), held
                )
            diagonal_ref[0, h] = held


def self_backward(qkv, bias, total, grad):
    pairs, length, width = qkv.shape
    width //= 3
    steps = width // LANES
    padded = -(-length // LANES) * LANES
    part = lambda c: pl.BlockSpec((1, length, LANES), lambda p, h: (p, 0, h + c * steps))
    return pl.pallas_call(
        self_backward_kernel,
        out_shape=(
            jax.ShapeDtypeStruct(qkv.shape, bf16),
            jax.ShapeDtypeStruct((steps, 2, 8, padded), f32),
        ),
        grid=(pairs, steps),
        in_specs=[
            part(0),
            part(1),
            part(2),
            pl.BlockSpec((2, length, length), lambda p, h: (h, 0, 0)),
            part(0),
            part(0),
        ],
        out_specs=[
            pl.BlockSpec((1, length, 3 * width), lambda p, h: (p, 0, 0)),
            pl.BlockSpec((1, 2, 8, padded), lambda p, h: (h, 0, 0, 0)),
        ],
        scratch_shapes=[pltpu.VMEM((steps, 2, length, padded), f32)],
        cost_estimate=pl.CostEstimate(
            flops=pairs * HEADS * length * length * HEAD_DIM * 10,
            transcendentals=pairs * HEADS * length * length,
            bytes_accessed=pairs * length * width * 18,
        ),
        name="self_backward",
    )(qkv, qkv, qkv, bias, total, grad)


def dead_rows(len_ref, rows):
    places = lax.broadcasted_iota(jnp.int32, (1, rows), 1)
    return jnp.where(places < len_ref[pl.program_id(0)], 0.0, negative)


def cross_forward_kernel(len_ref, q_ref, k_ref, v_ref, mixed_ref, total_ref):
    q, k, v = q_ref[0], k_ref[0], v_ref[0]
    first = lax.broadcasted_iota(jnp.int32, q.shape, 1) < HEAD_DIM
    dead = dead_rows(len_ref, k.shape[0])
    mixed, totals = [], []
    for h in range(2):
        scores = dot(of_head(h, first, q), k, NT) + dead
        top = jnp.max(scores, axis=1, keepdims=True)
        grown = jnp.exp(scores - top)
        total = jnp.sum(grown, axis=1, keepdims=True)
        mixed.append(dot((grown * (1.0 / total)).astype(bf16), v, NN))
        totals.append(top + jnp.log(total))
    mixed_ref[0] = jnp.where(first, mixed[0], mixed[1]).astype(bf16)
    total_ref[0] = jnp.where(first, totals[0], totals[1])


def cross_forward(query, kv, lens):
    pairs, length, width = query.shape
    rows = kv.shape[1]
    steps = width // LANES
    target = pl.BlockSpec((1, length, LANES), lambda p, h, n: (p, 0, h))
    source = lambda c: pl.BlockSpec((1, rows, LANES), lambda p, h, n: (p, 0, h + c * steps))
    return pl.pallas_call(
        cross_forward_kernel,
        out_shape=(
            jax.ShapeDtypeStruct(query.shape, bf16),
            jax.ShapeDtypeStruct(query.shape, f32),
        ),
        grid_spec=pltpu.PrefetchScalarGridSpec(
            num_scalar_prefetch=1,
            grid=(pairs, steps),
            in_specs=[target, source(0), source(1)],
            out_specs=[target, target],
        ),
        cost_estimate=pl.CostEstimate(
            flops=pairs * HEADS * length * rows * HEAD_DIM * 4,
            transcendentals=pairs * HEADS * length * rows,
            bytes_accessed=pairs * (length * width * 8 + rows * width * 4),
        ),
        name="cross_forward",
    )(lens, query, kv, kv)


def cross_backward_kernel(
    len_ref, q_ref, k_ref, v_ref, total_ref, grad_ref, grad_query_ref, grad_kv_ref
):
    hp, steps = pl.program_id(1), pl.num_programs(1)
    q, k, v, grad, total = q_ref[0], k_ref[0], v_ref[0], grad_ref[0], total_ref[0]
    first = lax.broadcasted_iota(jnp.int32, q.shape, 1) < HEAD_DIM
    first_row = lax.broadcasted_iota(jnp.int32, k.shape, 1) < HEAD_DIM
    dead = dead_rows(len_ref, k.shape[0])
    found = []
    for h in range(2):
        scores = dot(of_head(h, first, q), k, NT) + dead
        probs = jnp.exp(scores - total[:, HEAD_DIM * h : HEAD_DIM * h + 1])
        grad_probs = dot(of_head(h, first, grad), v, NT)
        inner = jnp.sum(probs * grad_probs, axis=1, keepdims=True)
        grad_scores = (probs * (grad_probs - inner)).astype(bf16)
        found.append(
            (
                dot(grad_scores, k, NN),
                dot(grad_scores, q, TN),
                dot(probs.astype(bf16), grad, TN),
            )
        )
    grad_query_ref[0] = jnp.where(first, found[0][0], found[1][0]).astype(bf16)
    for c in range(2):
        grad_kv_ref[0, :, pl.ds(pl.multiple_of((hp + c * steps) * LANES, LANES), LANES)] = (
            jnp.where(first_row, found[0][c + 1], found[1][c + 1]).astype(bf16)
        )


def cross_backward(query, kv, lens, total, grad):
    pairs, length, width = query.shape
    rows = kv.shape[1]
    steps = width // LANES
    target = pl.BlockSpec((1, length, LANES), lambda p, h, n: (p, 0, h))
    source = lambda c: pl.BlockSpec((1, rows, LANES), lambda p, h, n: (p, 0, h + c * steps))
    return pl.pallas_call(
        cross_backward_kernel,
        out_shape=(
            jax.ShapeDtypeStruct(query.shape, bf16),
            jax.ShapeDtypeStruct(kv.shape, bf16),
        ),
        grid_spec=pltpu.PrefetchScalarGridSpec(
            num_scalar_prefetch=1,
            grid=(pairs, steps),
            in_specs=[target, source(0), source(1), target, target],
            out_specs=[target, pl.BlockSpec((1, rows, 2 * width), lambda p, h, n: (p, 0, 0))],
        ),
        cost_estimate=pl.CostEstimate(
            flops=pairs * HEADS * length * rows * HEAD_DIM * 10,
            transcendentals=pairs * HEADS * length * rows,
            bytes_accessed=pairs * (length * width * 10 + rows * width * 8),
        ),
        name="cross_backward",
    )(lens, query, kv, kv, total, grad)


class Cube:
    def __init__(self, narrow, wide):
        self.size = narrow * wide
        self.bits = self.size.bit_length() - 1
        self.core = wide.bit_length() - 1
        self.index = lax.axis_index(BOTH)

    def swap(self, value, bit):
        pairs = [(i, i ^ (1 << bit)) for i in range(self.size)]
        return lax.ppermute(value, BOTH, pairs)

    def side(self, bit):
        return (self.index >> bit) & 1

    def total(self, value):
        for bit in range(self.bits):
            value = value + self.swap(value, bit)
        return value

    def scatter(self, value, order):
        rows, width = value.shape
        value = value.reshape((2,) * self.bits + (rows // self.size, width))
        left = list(range(self.bits))[::-1]
        for bit in order:
            axis, side = left.index(bit), self.side(bit)
            send = lax.dynamic_index_in_dim(value, 1 - side, axis, keepdims=False)
            keep = lax.dynamic_index_in_dim(value, side, axis, keepdims=False)
            left.remove(bit)
            value = keep.astype(f32) + self.swap(send, bit).astype(f32)
            if left:
                value = value.astype(bf16)
        return value

    def orders(self):
        rest = [b for b in range(self.bits) if b != self.core]
        one = [self.core, rest[-1], rest[0]] + rest[1:-1][::-1]
        two = [self.core, rest[0], rest[-1]] + rest[1:-1][::-1]
        return one, two

    def scatter_both(self, value):
        half = value.shape[1] // 2 // LANES * LANES
        one, two = self.orders()
        return jnp.concatenate(
            [self.scatter(value[:, :half], one), self.scatter(value[:, half:], two)], axis=1
        )


def rms_norm(value, gain):
    return value * lax.rsqrt(jnp.mean(value * value, axis=-1, keepdims=True) + epsilon) * gain


def gelu_tanh(value):
    return jax.nn.gelu(value, approximate=True)


def on_device(
    targets,
    memory,
    cotangent,
    target_len,
    memory_len,
    self_query,
    self_key,
    self_value,
    self_out,
    cross_query,
    cross_key,
    cross_value,
    cross_out,
    ff_gate,
    ff_up,
    ff_down,
    self_gain,
    cross_gain,
    ff_gain,
    position_bias,
    narrow,
    wide,
):
    cube = Cube(narrow, wide)
    pairs, length, width = targets.shape
    slots = pairs * length
    own, own_ff = self_query.shape[0], ff_down.shape[0]
    inner = ff_gate.shape[1]
    devices = cube.size

    gains = jnp.stack([self_gain, cross_gain, ff_gain], axis=1)
    gains = jnp.pad(gains, ((0, 0), (0, LANES - 3)))
    attention_shard = jnp.concatenate(
        [
            self_query,
            self_key,
            self_value,
            self_out,
            cross_query,
            cross_key,
            cross_value,
            cross_out,
            gains,
        ],
        axis=1,
    )
    attention = lax.all_gather(attention_shard, BOTH, axis=0, tiled=True)
    stack = -(-own_ff // own)
    down_shard = jnp.pad(ff_down, ((0, stack * own - own_ff), (0, 0)))
    down_shard = [down_shard[c * own : (c + 1) * own] for c in range(stack)]
    ff_shard = jnp.concatenate([ff_gate, ff_up] + down_shard, axis=1)
    ff = lax.all_gather(ff_shard, BOTH, axis=0, tiled=True)

    w_qkv = attention[:, : 3 * width]
    s_out = attention[:, 3 * width : 4 * width]
    c_query = attention[:, 4 * width : 5 * width]
    c_kv = attention[:, 5 * width : 7 * width]
    c_out = attention[:, 7 * width : 8 * width]
    gains = attention[:, 8 * width : 8 * width + 3].astype(f32).T
    gain_one, gain_two, gain_three = gains[0], gains[1], gains[2]
    f_gate_up = ff[:, : 2 * inner]
    f_down = jnp.concatenate(
        [
            ff[:, 2 * inner + c * width : 2 * inner + (c + 1) * width].reshape(devices, own, width)
            for c in range(stack)
        ],
        axis=1,
    )[:, :own_ff].reshape(inner, width)

    places = jnp.arange(length)
    apart = places[:, None] - places[None, :]
    bucket = bucket_of_distance(length, BUCKETS, REACH)
    starts = [int(np.argmax(bucket >= b)) for b in range(1, int(bucket[-1]) + 1)]
    bucket_matrix = sum((apart >= start).astype(jnp.int32) for start in starts)
    onehot = (bucket_matrix[:, :, None] == jnp.arange(BUCKETS)[None, None, :]).astype(bf16)
    bias = jnp.einsum("ijb,bh->hij", onehot, position_bias, preferred_element_type=f32)
    bias = jnp.where((apart >= 0)[None], bias, negative).astype(bf16)

    live = (places[None, :] < target_len[:, None]).astype(f32).reshape(slots, 1)
    inputs = targets.astype(f32).reshape(slots, width)

    memory_rows = lax.all_to_all(memory, "wide", split_axis=0, concat_axis=1, tiled=True)
    memory_rows = memory_rows.reshape(-1, width)
    normed_one = rms_norm(inputs, gain_one).astype(bf16)
    qkv_one = dot(normed_one, w_qkv, NN).astype(bf16).reshape(pairs, length, 3 * width)
    mixed_one, total_one = self_forward(qkv_one, bias)
    mixed_one = mixed_one.reshape(slots, width)
    first = inputs + dot(mixed_one, s_out, NN)
    normed_two = rms_norm(first, gain_two).astype(bf16)
    query_two = dot(normed_two, c_query, NN).astype(bf16).reshape(pairs, length, width)
    kv_two = dot(memory_rows, c_kv, NN).astype(bf16).reshape(pairs, -1, 2 * width)
    mixed_two, total_two = cross_forward(query_two, kv_two, memory_len)
    mixed_two = mixed_two.reshape(slots, width)
    second = first + dot(mixed_two, c_out, NN)
    normed_three = rms_norm(second, gain_three).astype(bf16)
    gate = dot(normed_three, f_gate_up[:, :inner], NN)
    upward = dot(normed_three, f_gate_up[:, inner:], NN)
    activated, gelu_pull = jax.vjp(gelu_tanh, gate)
    hidden = (activated * upward).astype(bf16)
    third = second + dot(hidden, f_down, NN)
    layer_out = (third * live).astype(bf16).reshape(pairs, length, width)

    grad_third = cotangent.astype(f32).reshape(slots, width) * live
    branch_ff = grad_third.astype(bf16)
    d_down = dot(hidden, branch_ff, TN).astype(bf16)
    grad_hidden = dot(branch_ff, f_down, NT)
    grad_gate = gelu_pull(grad_hidden * upward)[0].astype(bf16)
    grad_up = (grad_hidden * activated).astype(bf16)
    d_gate = dot(normed_three, grad_gate, TN).astype(bf16)
    d_up = dot(normed_three, grad_up, TN).astype(bf16)
    grad_normed_three = dot(grad_gate, f_gate_up[:, :inner], NT) + dot(
        grad_up, f_gate_up[:, inner:], NT
    )
    d_down = d_down.reshape(devices, own_ff, width)
    d_down = jnp.pad(d_down, ((0, 0), (0, stack * own - own_ff), (0, 0)))
    d_down = [
        d_down[:, c * own : (c + 1) * own].reshape(devices * own, width) for c in range(stack)
    ]
    ff_grads = lax.psum_scatter(
        jnp.concatenate([d_gate, d_up] + d_down, axis=1),
        BOTH,
        scatter_dimension=0,
        tiled=True,
    ).astype(f32)
    _, norm_three = jax.vjp(rms_norm, second, gain_three)
    back_three, d_gain_three = norm_three(grad_normed_three)
    grad_second = grad_third + back_three

    branch_cross = grad_second.astype(bf16)
    d_cross_out = dot(mixed_two, branch_cross, TN).astype(bf16)
    grad_mixed_two = dot(branch_cross, c_out, NT).astype(bf16).reshape(pairs, length, width)
    grad_query_two, grad_kv_two = cross_backward(
        query_two, kv_two, memory_len, total_two, grad_mixed_two
    )
    grad_query_two = grad_query_two.reshape(slots, width)
    grad_kv_two = grad_kv_two.reshape(-1, 2 * width)
    rows_grad = dot(grad_kv_two, c_kv, NT).astype(bf16).reshape(pairs, -1, width)
    grad_memory = lax.all_to_all(
        rows_grad, "wide", split_axis=1, concat_axis=0, tiled=True
    ).astype(f32)
    d_cross_query = dot(normed_two, grad_query_two, TN).astype(bf16)
    d_cross_kv = dot(memory_rows, grad_kv_two, TN).astype(bf16)
    cross_grads = cube.scatter_both(
        jnp.concatenate([d_cross_query, d_cross_kv, d_cross_out], axis=1)
    )
    _, norm_two = jax.vjp(rms_norm, first, gain_two)
    back_two, d_gain_two = norm_two(dot(grad_query_two, c_query, NT))
    grad_first = grad_second + back_two

    branch_self = grad_first.astype(bf16)
    d_self_out = dot(mixed_one, branch_self, TN).astype(bf16)
    grad_mixed_one = dot(branch_self, s_out, NT).astype(bf16).reshape(pairs, length, width)
    grad_qkv_one, diagonals = self_backward(qkv_one, bias, total_one, grad_mixed_one)
    grad_qkv_one = grad_qkv_one.reshape(slots, 3 * width)
    d_qkv = dot(normed_one, grad_qkv_one, TN).astype(bf16)
    self_grads = cube.scatter_both(jnp.concatenate([d_qkv, d_self_out], axis=1))
    grad_normed_one = dot(grad_qkv_one, w_qkv, NT)
    _, norm_one = jax.vjp(rms_norm, inputs, gain_one)
    back_one, d_gain_one = norm_one(grad_normed_one)
    grad_targets = (grad_first + back_one).reshape(pairs, length, width)

    padded = diagonals.shape[-1]
    column = (padded - np.arange(length)) % padded
    to_bucket = np.zeros((padded, BUCKETS), np.float32)
    to_bucket[column, bucket_of_distance(length, BUCKETS, REACH)] = 1.0
    diagonals = jnp.sum(diagonals, axis=2).reshape(HEADS, padded)
    d_position = jnp.einsum(
        "hc,cb->bh", diagonals, jnp.asarray(to_bucket), precision=lax.Precision.HIGHEST
    )
    small = jnp.concatenate(
        [d_gain_one, d_gain_two, d_gain_three, d_position.reshape(-1)]
    ).reshape(-1, LANES)
    small = jnp.pad(small, ((0, -small.shape[0] % 8), (0, 0)))
    small = cube.total(small).reshape(-1)
    gain_grads = small[: 3 * width].reshape(3, devices, width // devices)
    gain_grads = lax.dynamic_index_in_dim(gain_grads, cube.index, 1, keepdims=False)
    grad_position = small[3 * width : 3 * width + BUCKETS * HEADS].reshape(BUCKETS, HEADS)

    g_down = jnp.concatenate(
        [ff_grads[:, 2 * inner + c * width : 2 * inner + (c + 1) * width] for c in range(stack)],
        axis=0,
    )[:own_ff]
    cut = lambda value, c: value[:, c * width : (c + 1) * width]
    return (
        layer_out,
        grad_targets,
        grad_memory,
        cut(self_grads, 0),
        cut(self_grads, 1),
        cut(self_grads, 2),
        cut(self_grads, 3),
        cut(cross_grads, 0),
        cut(cross_grads, 1),
        cut(cross_grads, 2),
        cut(cross_grads, 3),
        ff_grads[:, :inner],
        ff_grads[:, inner : 2 * inner],
        g_down,
        gain_grads[0],
        gain_grads[1],
        gain_grads[2],
        grad_position,
    )


def solution(mesh):
    rows = P(BOTH, None)
    slots = P(BOTH, None, None)
    one = P(BOTH)
    source = P("narrow", "wide", None)
    in_specs = (slots, source, slots, one, one) + (rows,) * 11 + (one,) * 3 + (P(),)
    out_specs = (slots, slots, source) + (rows,) * 11 + (one,) * 3 + (P(),)
    narrow, wide = mesh.shape["narrow"], mesh.shape["wide"]

    def body(*args):
        return on_device(*args, narrow=narrow, wide=wide)

    return jax.shard_map(body, mesh=mesh, in_specs=in_specs, out_specs=out_specs, check_vma=False)
```

```python
import functools

import jax
import jax.numpy as jnp
import numpy as np
from jax import lax
from jax.experimental import pallas as pl
from jax.experimental.pallas import tpu as pltpu
from jax.sharding import PartitionSpec as P

HEADS = 12
HEAD_DIM = 64
BUCKETS = 32
REACH = 128
LANES = 128
BOTH = ("narrow", "wide")
SHARE = 8

negative = -1e30
epsilon = 1e-06
bf16 = jnp.bfloat16
f32 = jnp.float32

NT = (((1,), (1,)), ((), ()))
NN = (((1,), (0,)), ((), ()))
TN = (((0,), (0,)), ((), ()))


def cost(flops=0, transcendentals=0, bytes_accessed=0):
    return pl.CostEstimate(
        flops=flops // SHARE,
        transcendentals=transcendentals // SHARE,
        bytes_accessed=bytes_accessed // SHARE,
    )


def dot(left, right, dims):
    return lax.dot_general(left, right, dims, preferred_element_type=f32)


def bucket_of_distance(length, buckets, reach):
    apart = np.arange(length)
    exact = buckets // 2
    safe = np.maximum(apart, 1)
    far = exact + (np.log(safe / exact) / np.log(reach / exact) * (buckets - exact)).astype(
        np.int64
    )
    far = np.minimum(far, buckets - 1)
    return np.where(apart < exact, apart, far).astype(np.int32)


def of_head(h, first, value):
    return jnp.where(first if h == 0 else ~first, value, jnp.zeros_like(value))


def self_forward_kernel(q_ref, k_ref, v_ref, bias_ref, mixed_ref, total_ref):
    q, k, v = q_ref[0], k_ref[0], v_ref[0]
    first = lax.broadcasted_iota(jnp.int32, q.shape, 1) < HEAD_DIM
    mixed, totals = [], []
    for h in range(2):
        scores = dot(of_head(h, first, q), k, NT) + bias_ref[h].astype(f32)
        top = jnp.max(scores, axis=1, keepdims=True)
        grown = jnp.exp(scores - top)
        total = jnp.sum(grown, axis=1, keepdims=True)
        mixed.append(dot((grown * (1.0 / total)).astype(bf16), v, NN))
        totals.append(top + jnp.log(total))
    mixed_ref[0] = jnp.where(first, mixed[0], mixed[1]).astype(bf16)
    total_ref[0] = jnp.where(first, totals[0], totals[1])


def self_forward(qkv, bias):
    pairs, length, width = qkv.shape
    width //= 3
    steps = width // LANES
    part = lambda c: pl.BlockSpec((1, length, LANES), lambda p, h: (p, 0, h + c * steps))
    return pl.pallas_call(
        self_forward_kernel,
        out_shape=(
            jax.ShapeDtypeStruct((pairs, length, width), bf16),
            jax.ShapeDtypeStruct((pairs, length, width), f32),
        ),
        grid=(pairs, steps),
        in_specs=[
            part(0),
            part(1),
            part(2),
            pl.BlockSpec((2, length, length), lambda p, h: (h, 0, 0)),
        ],
        out_specs=[part(0), part(0)],
        cost_estimate=cost(
            flops=pairs * HEADS * length * length * HEAD_DIM * 4,
            transcendentals=pairs * HEADS * length * length,
            bytes_accessed=pairs * length * width * 12,
        ),
        name="self_forward",
    )(qkv, qkv, qkv, bias)


def self_backward_kernel(
    q_ref, k_ref, v_ref, bias_ref, total_ref, grad_ref, grads_ref, diagonal_ref, sum_ref
):
    p, hp = pl.program_id(0), pl.program_id(1)
    steps = pl.num_programs(1)
    q, k, v, grad, total = q_ref[0], k_ref[0], v_ref[0], grad_ref[0], total_ref[0]
    length, padded = q.shape[0], sum_ref.shape[-1]
    first = lax.broadcasted_iota(jnp.int32, q.shape, 1) < HEAD_DIM

    @pl.when(p == 0)
    def _():
        sum_ref[hp] = jnp.zeros(sum_ref.shape[1:], f32)

    found = []
    for h in range(2):
        scores = dot(of_head(h, first, q), k, NT) + bias_ref[h].astype(f32)
        probs = jnp.exp(scores - total[:, HEAD_DIM * h : HEAD_DIM * h + 1])
        grad_probs = dot(of_head(h, first, grad), v, NT)
        inner = jnp.sum(probs * grad_probs, axis=1, keepdims=True)
        grad_scores = (probs * (grad_probs - inner)).astype(bf16)
        sum_ref[hp, h, :, :length] += grad_scores.astype(f32)
        found.append(
            (
                dot(grad_scores, k, NN),
                dot(grad_scores, q, TN),
                dot(probs.astype(bf16), grad, TN),
            )
        )
    for c in range(3):
        grads_ref[0, :, pl.ds(pl.multiple_of((hp + c * steps) * LANES, LANES), LANES)] = (
            jnp.where(first, found[0][c], found[1][c]).astype(bf16)
        )

    @pl.when(p == pl.num_programs(0) - 1)
    def _():
        rows = lax.broadcasted_iota(jnp.int32, (8, padded), 0)
        for h in range(2):
            held = sum_ref[hp, h, 0:8, :]
            for i in range(8, length, 8):
                held = held + pltpu.roll(sum_ref[hp, h, i : i + 8, :], padded - i, 1)
            for bit in (1, 2, 4):
                held = jnp.where(
                    (rows // bit) % 2 == 1, pltpu.roll(held, padded - bit, 1), held
                )
            diagonal_ref[0, h] = held


def self_backward(qkv, bias, total, grad):
    pairs, length, width = qkv.shape
    width //= 3
    steps = width // LANES
    padded = -(-length // LANES) * LANES
    part = lambda c: pl.BlockSpec((1, length, LANES), lambda p, h: (p, 0, h + c * steps))
    return pl.pallas_call(
        self_backward_kernel,
        out_shape=(
            jax.ShapeDtypeStruct(qkv.shape, bf16),
            jax.ShapeDtypeStruct((steps, 2, 8, padded), f32),
        ),
        grid=(pairs, steps),
        in_specs=[
            part(0),
            part(1),
            part(2),
            pl.BlockSpec((2, length, length), lambda p, h: (h, 0, 0)),
            part(0),
            part(0),
        ],
        out_specs=[
            pl.BlockSpec((1, length, 3 * width), lambda p, h: (p, 0, 0)),
            pl.BlockSpec((1, 2, 8, padded), lambda p, h: (h, 0, 0, 0)),
        ],
        scratch_shapes=[pltpu.VMEM((steps, 2, length, padded), f32)],
        cost_estimate=cost(
            flops=pairs * HEADS * length * length * HEAD_DIM * 10,
            transcendentals=pairs * HEADS * length * length,
            bytes_accessed=pairs * length * width * 18,
        ),
        name="self_backward",
    )(qkv, qkv, qkv, bias, total, grad)


def dead_rows(live_rows, rows):
    places = lax.broadcasted_iota(jnp.int32, (1, rows), 1)
    return jnp.where(places < live_rows, 0.0, negative)


def cross_forward_kernel(pair, len_ref, q_ref, memory_ref, wk_ref, wv_ref, *refs):
    mixed_ref, total_ref, k_ref, v_ref = refs[-4:]
    q = q_ref[0]
    rows = k_ref.shape[1]
    memory = memory_ref[...].reshape(rows, -1)
    kv = dot(memory, jnp.concatenate([wk_ref[...], wv_ref[...]], axis=1), NN).astype(bf16)
    k, v = kv[:, :LANES], kv[:, LANES:]
    k_ref[0], v_ref[0] = k, v
    first = lax.broadcasted_iota(jnp.int32, q.shape, 1) < HEAD_DIM
    dead = dead_rows(len_ref[pair], rows)
    mixed, totals = [], []
    for h in range(2):
        scores = dot(of_head(h, first, q), k, NT) + dead
        top = jnp.max(scores, axis=1, keepdims=True)
        grown = jnp.exp(scores - top)
        total = jnp.sum(grown, axis=1, keepdims=True)
        mixed.append(dot((grown * (1.0 / total)).astype(bf16), v, NN))
        totals.append(top + jnp.log(total))
    mixed_ref[0] = jnp.where(first, mixed[0], mixed[1]).astype(bf16)
    total_ref[0] = jnp.where(first, totals[0], totals[1])


def cross_forward(pair, query, memory, query_key, value_out, lens, before):
    pairs, length, width = query.shape
    sources, _, part, _ = memory.shape
    rows = sources * part
    steps = width // LANES
    target = pl.BlockSpec((1, length, LANES), lambda h, n: (pair, 0, h))
    source = pl.BlockSpec((1, rows, LANES), lambda h, n: (pair, 0, h))
    weight = lambda c: pl.BlockSpec((width, LANES), lambda h, n: (0, h + c * steps))
    return pl.pallas_call(
        functools.partial(cross_forward_kernel, pair),
        out_shape=(
            jax.ShapeDtypeStruct(query.shape, bf16),
            jax.ShapeDtypeStruct(query.shape, f32),
            jax.ShapeDtypeStruct((pairs, rows, width), bf16),
            jax.ShapeDtypeStruct((pairs, rows, width), bf16),
        ),
        grid_spec=pltpu.PrefetchScalarGridSpec(
            num_scalar_prefetch=1,
            grid=(steps,),
            in_specs=[
                target,
                pl.BlockSpec((sources, 1, part, width), lambda h, n: (0, pair, 0, 0)),
                weight(1),
                weight(0),
            ]
            + [pl.BlockSpec(memory_space=pl.ANY)] * len(before),
            out_specs=[target, target, source, source],
        ),
        input_output_aliases={5 + i: i for i in range(len(before))},
        cost_estimate=cost(
            flops=rows * width * (length * 4 + width * 4),
            transcendentals=HEADS * length * rows,
            bytes_accessed=length * width * 8 + rows * width * 6,
        ),
        name="cross_forward",
    )(lens, query, memory, query_key, value_out, *before)


def cross_backward_kernel(
    pair, last, len_ref, q_ref, k_ref, v_ref, total_ref, grad_ref, memory_ref, wk_ref, wv_ref, *refs
):
    turned_ref, rows_ref = refs[-2:]
    hp, steps = pl.program_id(0), pl.num_programs(0)
    q, k, v, grad, total = q_ref[0], k_ref[0], v_ref[0], grad_ref[0], total_ref[0]
    rows = k.shape[0]
    first = lax.broadcasted_iota(jnp.int32, q.shape, 1) < HEAD_DIM
    first_row = lax.broadcasted_iota(jnp.int32, k.shape, 1) < HEAD_DIM
    dead = dead_rows(len_ref[pair], rows)
    if pair:
        before_ref, _, *refs = refs
    if last:
        grad_query_ref, grad_memory_ref, d_key_ref, d_value_ref = refs[:4]
    else:
        grad_query_ref, grad_memory_ref, sum_ref = refs[:3]

    @pl.when(hp == 0)
    def _():
        turned_ref[...] = memory_ref[...].reshape(rows, -1).T

    found = []
    for h in range(2):
        scores = dot(of_head(h, first, q), k, NT) + dead
        probs = jnp.exp(scores - total[:, HEAD_DIM * h : HEAD_DIM * h + 1])
        grad_probs = dot(of_head(h, first, grad), v, NT)
        inner = jnp.sum(probs * grad_probs, axis=1, keepdims=True)
        grad_scores = (probs * (grad_probs - inner)).astype(bf16)
        found.append(
            (
                dot(grad_scores, k, NN),
                dot(grad_scores, q, TN),
                dot(probs.astype(bf16), grad, TN),
            )
        )
    grad_query_ref[0] = jnp.where(first, found[0][0], found[1][0]).astype(bf16)
    grad_kv = jnp.concatenate(
        [jnp.where(first_row, found[0][c], found[1][c]).astype(bf16) for c in (1, 2)], axis=1
    )
    weight = jnp.concatenate([wk_ref[...], wv_ref[...]], axis=1)
    back = dot(grad_kv, weight, NT)

    @pl.when(hp == 0)
    def _():
        rows_ref[...] = back

    @pl.when(hp > 0)
    def _():
        rows_ref[...] += back

    @pl.when(hp == steps - 1)
    def _():
        grad_memory_ref[...] = rows_ref[...].astype(bf16).reshape(grad_memory_ref.shape)

    d_kv = dot(turned_ref[...], grad_kv, NN)
    if pair:
        d_kv = d_kv + before_ref[0]
    if last:
        d_key_ref[...] = d_kv[:, :LANES].astype(bf16)
        d_value_ref[...] = d_kv[:, LANES:].astype(bf16)
    else:
        sum_ref[0] = d_kv


def cross_backward(
    pair, query, key, value, lens, total, grad, memory, query_key, value_out, before
):
    pairs, length, width = query.shape
    sources, _, part, _ = memory.shape
    rows = sources * part
    steps = width // LANES
    last = pair == pairs - 1
    target = pl.BlockSpec((1, length, LANES), lambda h, n: (pair, 0, h))
    source = pl.BlockSpec((1, rows, LANES), lambda h, n: (pair, 0, h))
    weight = lambda c: pl.BlockSpec((width, LANES), lambda h, n: (0, h + c * steps))
    held = pl.BlockSpec((sources, 1, part, width), lambda h, n: (0, pair, 0, 0))
    given = pl.BlockSpec((sources, part, width), lambda h, n: (0, 0, 0))
    sums = pl.BlockSpec((1, width, 2 * LANES), lambda h, n: (h, 0, 0))
    out_shape = [jax.ShapeDtypeStruct(query.shape, bf16), jax.ShapeDtypeStruct((sources, part, width), bf16)]
    if last:
        out_shape += [jax.ShapeDtypeStruct((width, width), bf16)] * 2
    else:
        out_shape += [jax.ShapeDtypeStruct((steps, width, 2 * LANES), f32)]
    return pl.pallas_call(
        functools.partial(cross_backward_kernel, pair, last),
        out_shape=out_shape,
        grid_spec=pltpu.PrefetchScalarGridSpec(
            num_scalar_prefetch=1,
            grid=(steps,),
            in_specs=[target, source, source, target, target, held, weight(1), weight(0)]
            + [sums, pl.BlockSpec(memory_space=pl.ANY)][: len(before)],
            out_specs=[target, given] + ([weight(0)] * 2 if last else [sums]),
            scratch_shapes=[pltpu.VMEM((width, rows), bf16), pltpu.VMEM((rows, width), f32)],
        ),
        input_output_aliases={10: 0} if pair else {},
        cost_estimate=cost(
            flops=rows * width * (length * 10 + width * 8),
            transcendentals=HEADS * length * rows,
            bytes_accessed=length * width * 10 + rows * width * 8,
        ),
        name="cross_backward",
    )(lens, query, key, value, total, grad, memory, query_key, value_out, *before)


class Cube:
    def __init__(self, narrow, wide):
        self.narrow, self.wide = narrow, wide
        self.size = narrow * wide
        self.bits = self.size.bit_length() - 1
        self.index = lax.axis_index(BOTH)

    def swap(self, value, mask):
        pairs = [(i, i ^ mask) for i in range(self.size)]
        return lax.ppermute(value, BOTH, pairs)

    def total(self, value, bits):
        for bit in bits:
            value = value + self.swap(value, 1 << bit)
        return value


def merge_four(cube, pieces, split):
    r, n = pieces[0].shape

    def kernel(place_ref, *refs):
        ins, (left_ref, right_ref) = refs[:4], refs[4:]
        for m, ref in enumerate(ins):
            at = place_ref[0] ^ m
            left_ref[at] = ref[:, :split]
            right_ref[at] = ref[:, split:]

    return pl.pallas_call(
        kernel,
        out_shape=(
            jax.ShapeDtypeStruct((4, r, split), bf16),
            jax.ShapeDtypeStruct((4, r, n - split), bf16),
        ),
        grid_spec=pltpu.PrefetchScalarGridSpec(
            num_scalar_prefetch=1,
            grid=(1,),
            in_specs=[pl.BlockSpec((r, n), lambda i, s: (0, 0))] * 4,
            out_specs=[
                pl.BlockSpec((4, r, split), lambda i, s: (0, 0, 0)),
                pl.BlockSpec((4, r, n - split), lambda i, s: (0, 0, 0)),
            ],
        ),
        cost_estimate=cost(flops=0, transcendentals=0, bytes_accessed=16 * r * n),
        name="merge_four",
    )(((cube.index >> 1) & 3).reshape(1), *pieces)


def merge_two(side, mine, come, chunks):
    a, rows, n = mine.shape
    piece = pl.BlockSpec((1, rows, n // chunks), lambda i, c, s: (i, 0, c))

    def kernel(side_ref, mine_ref, come_ref, out_ref):
        out_ref[0, side_ref[0]] = mine_ref[0]
        out_ref[0, 1 - side_ref[0]] = come_ref[0]

    return pl.pallas_call(
        kernel,
        out_shape=jax.ShapeDtypeStruct((a, 2, rows, n), bf16),
        grid_spec=pltpu.PrefetchScalarGridSpec(
            num_scalar_prefetch=1,
            grid=(a, chunks),
            in_specs=[piece, piece],
            out_specs=pl.BlockSpec((1, 2, rows, n // chunks), lambda i, c, s: (i, 0, 0, c)),
        ),
        cost_estimate=cost(
            flops=0, transcendentals=0, bytes_accessed=8 * a * rows * n
        ),
        name="merge_two",
    )(side.reshape(1), mine, come)


class Gather:
    def __init__(self, cube, shard, split):
        self.cube = cube
        pieces = [shard] + [cube.swap(shard, m << 1) for m in (1, 2, 3)]
        self.start = merge_four(cube, pieces, split)

    def half(self, filler):
        cube = self.cube
        one, two = self.start
        r = one.shape[1]
        come_one, come_two = cube.swap(one, 1), cube.swap(two.reshape(1, 4 * r, -1), 16)
        come_one, come_two, filler = tie(come_one, come_two, filler)
        one = merge_two(self.side(0), one, come_one, 1)
        two = merge_two(self.side(4), two.reshape(1, 4 * r, -1), come_two, 1)
        return one.reshape(1, 8 * r, -1), two.reshape(8, r, -1), filler

    def side(self, bit):
        return (self.cube.index >> bit) & 1

    def most(self, one, two):
        cube = self.cube
        r = two.shape[1]
        one = merge_two(self.side(4), one, cube.swap(one, 16), 2 - one.shape[2] // LANES % 2)
        two = merge_two(self.side(0), two, cube.swap(two, 1), 1)
        return [one.reshape(2, 8 * r, -1), two.reshape(2, 8 * r, -1)]

    def finish(self, values):
        core = self.side(3)
        chunks = lambda value: 2 - value.shape[2] // LANES % 2
        return [
            merge_two(core, value, self.cube.swap(value, 8), chunks(value)).reshape(
                -1, value.shape[2]
            )
            for value in values
        ]


class Scatter:
    def __init__(self, cube, grads):
        self.cube = cube
        self.shapes = [(grad.shape[0] // cube.size, grad.shape[1]) for grad in grads]
        self.own = self.shapes[0][0]
        self.flat = [i for i, (r, _) in enumerate(self.shapes) if r == self.own]
        self.tall = [i for i, (r, _) in enumerate(self.shapes) if r != self.own]
        self.grads = [
            grad.reshape(2, 2, cube.wide * r, n)
            for grad, (r, n) in zip(grads, self.shapes, strict=True)
        ]
        self.sides = jnp.stack([cube.index >> 4, (cube.index >> 3) & 1, cube.index & 1])
        self.groups = [(self.own, sum(self.shapes[i][1] for i in self.flat))]
        self.groups += [self.shapes[i] for i in self.tall]

    def message(self, come, own, places, lead=1, packed=0):
        wide = self.cube.wide
        split = 2
        n_grads, n_groups = len(self.grads), len(self.groups)
        n_ins = n_grads + len(come)
        widths = [n for _, n in self.groups]
        stack = [-(-r // self.own) for r, _ in self.groups]

        def kernel(sides_ref, *refs):
            ins, outs = refs[:n_ins], refs[n_ins:]
            flat = [ins[i][0, 0] for i in self.flat]
            values = [flat[0] if len(flat) == 1 else jnp.concatenate(flat, axis=1)]
            values += [ins[i][0, 0] for i in self.tall]
            for k, ref in enumerate(ins[n_grads:]):
                got = ref[...]
                got = got.reshape(got.shape[-2:])
                i = k % n_groups
                values[i] = values[i].astype(f32) + got.astype(f32)
            if not packed:
                for out_ref, value in zip(outs, values, strict=True):
                    out_ref[...] = value.astype(bf16).reshape(out_ref.shape)
                return
            at = 0
            for value, (r, n), high in zip(values, self.groups, stack, strict=True):
                value = value.astype(f32).reshape(wide // split, r, n)
                for c in range(high):
                    part = value[:, c * self.own : (c + 1) * self.own].astype(bf16)
                    if packed == 1:
                        outs[0][:, : part.shape[1], at : at + n] = part
                    else:
                        side = sides_ref[2]
                        for i in range(0, part.shape[0], 2):
                            for flip, out_ref in enumerate(outs):
                                out_ref[i // 2, : part.shape[1], at : at + n] = jnp.where(
                                    side == flip, part[i], part[i + 1]
                                )
                    at += n

        in_specs = [
            pl.BlockSpec((1, 1, wide * r // split, n), lambda i, j, s: (*own(i, s), j, 0))
            for r, n in self.shapes
        ]
        for k, value in enumerate(come):
            at = places[k // n_groups]
            r, n = self.groups[k % n_groups]
            in_specs.append(
                pl.BlockSpec(
                    (1,) * (value.ndim - 2) + (wide * r // split, n),
                    lambda i, j, s, at=at: (*at(s), j, 0),
                )
            )
        if packed:
            n = sum(w * high for w, high in zip(widths, stack, strict=True))
            high = wide // packed
            out_shape = [jax.ShapeDtypeStruct((high, self.own, n), bf16)] * packed
            out_specs = [
                pl.BlockSpec((high // split, self.own, n), lambda i, j, s: (j, 0, 0))
            ] * packed
        else:
            out_shape = [jax.ShapeDtypeStruct((lead, wide * r, n), bf16) for r, n in self.groups]
            out_specs = [
                pl.BlockSpec((1, wide * r // split, n), lambda i, j, s: (i, j, 0))
                for r, n in self.groups
            ]
        size = sum(int(np.prod(out.shape)) for out in out_shape)
        return pl.pallas_call(
            kernel,
            out_shape=out_shape,
            grid_spec=pltpu.PrefetchScalarGridSpec(
                num_scalar_prefetch=1,
                grid=(lead, split),
                in_specs=in_specs,
                out_specs=out_specs,
            ),
            cost_estimate=cost(
                flops=size, transcendentals=0, bytes_accessed=4 * size
            ),
            name="message",
        )(self.sides, *self.grads, *come)

    def swap(self, values, mask):
        return [self.cube.swap(value, mask) for value in values]

    def to_core(self):
        return self.message([], lambda i, s: (i, 1 - s[1]), [], lead=2)

    def to_x(self, one):
        return self.message(one, lambda i, s: (1 - s[0], s[1]), [lambda s: (1 - s[0],)])

    def to_wide(self, one, two, halved=False):
        places = [lambda s: (s[0],), lambda s: (0,)]
        return self.message(
            [*one, *two], lambda i, s: (s[0], s[1]), places, packed=1 + halved
        )

    def step(self, bit, mine, come):
        blocks, r, n = mine.shape

        def kernel(side_ref, *refs):
            keep_ref, send_ref = refs[-2:]
            side = side_ref[0]
            for i in range(blocks // 2):
                for out_ref, at in ((keep_ref, 2 * i + side), (send_ref, 2 * i + 1 - side)):
                    value = refs[0][at].astype(f32) + refs[1][at].astype(f32)
                    out_ref[i] = value.astype(bf16)

        whole = pl.BlockSpec(mine.shape, lambda i, s: (0, 0, 0))
        half = pl.BlockSpec((blocks // 2, r, n), lambda i, s: (0, 0, 0))
        return pl.pallas_call(
            kernel,
            out_shape=[jax.ShapeDtypeStruct((blocks // 2, r, n), bf16)] * 2,
            grid_spec=pltpu.PrefetchScalarGridSpec(
                num_scalar_prefetch=1,
                grid=(1,),
                in_specs=[whole, whole],
                out_specs=[half, half],
            ),
            cost_estimate=cost(
                flops=mine.size, transcendentals=0, bytes_accessed=6 * mine.size
            ),
            name="step",
        )(((self.cube.index >> bit) & 1).reshape(1), mine, come)

    def finish(self, *come):
        def kernel(*refs):
            ins, outs = refs[: len(come)], refs[len(come) :]
            blocks = [ref[i] for ref in ins for i in range(ref.shape[0])]
            value = blocks[0].astype(f32)
            for block in blocks[1:]:
                value = value + block.astype(f32)
            at = 0
            for i in self.flat:
                n = self.shapes[i][1]
                outs[i][...] = value[:, at : at + n]
                at += n
            for i in self.tall:
                r, n = self.shapes[i]
                for c in range(0, r, self.own):
                    high = min(self.own, r - c)
                    outs[i][c : c + high] = value[:high, at : at + n]
                    at += n

        size = sum(value.size for value in come)
        return pl.pallas_call(
            kernel,
            out_shape=tuple(jax.ShapeDtypeStruct(shape, f32) for shape in self.shapes),
            cost_estimate=cost(
                flops=size, transcendentals=0, bytes_accessed=4 * size
            ),
            name="finish",
        )(*come)


def tie(*values):
    return lax.optimization_barrier(values)


def pack_shards(parts, widths, rows):
    flat = [part for group in parts for part in group]

    def kernel(*refs):
        ins, outs = refs[: len(flat)], refs[len(flat) :]
        refs_of = iter(ins)
        for out_ref, group in zip(outs, parts, strict=True):
            at = 0
            for array, start, count in group:
                ref, n = next(refs_of), array.shape[1]
                out_ref[:count, at : at + n] = ref[start : start + count, :]
                if count < rows:
                    out_ref[count:, at : at + n] = jnp.zeros((rows - count, n), bf16)
                at += n

    return pl.pallas_call(
        kernel,
        out_shape=tuple(jax.ShapeDtypeStruct((rows, n), bf16) for n in widths),
        name="pack",
    )(*[part[0] for part in flat])


def rms_norm(value, gain):
    return value * lax.rsqrt(jnp.mean(value * value, axis=-1, keepdims=True) + epsilon) * gain


def gelu_tanh(value):
    return jax.nn.gelu(value, approximate=True)


def on_device(
    targets,
    memory,
    cotangent,
    target_len,
    memory_len,
    self_query,
    self_key,
    self_value,
    self_out,
    cross_query,
    cross_key,
    cross_value,
    cross_out,
    ff_gate,
    ff_up,
    ff_down,
    self_gain,
    cross_gain,
    ff_gain,
    position_bias,
    narrow,
    wide,
):
    cube = Cube(narrow, wide)
    pairs, length, width = targets.shape
    slots = pairs * length
    own, own_ff = self_query.shape[0], ff_down.shape[0]
    inner = ff_gate.shape[1]
    devices = cube.size
    stepped = narrow == 4 and wide == 8 and own % 8 == 0

    gains = jnp.stack([self_gain, cross_gain, ff_gain], axis=1)
    gains = jnp.pad(gains, ((0, 0), (0, LANES - 3)))
    stack = -(-own_ff // own)
    whole = lambda *arrays: [(array, 0, own) for array in arrays]
    self_shard, cross_shard, ff_shard = pack_shards(
        [
            whole(self_query, self_key, self_value, self_out, gains),
            whole(cross_query, cross_key, cross_value, cross_out),
            whole(ff_gate, ff_up)
            + [(ff_down, c * own, min(own, own_ff - c * own)) for c in range(stack)],
        ],
        [4 * width + LANES, 4 * width, 2 * inner + stack * width],
        own,
    )
    places = jnp.arange(length)
    apart = places[:, None] - places[None, :]
    bucket = bucket_of_distance(length, BUCKETS, REACH)
    starts = [int(np.argmax(bucket >= b)) for b in range(1, int(bucket[-1]) + 1)]
    bucket_matrix = sum((apart >= start).astype(jnp.int32) for start in starts)
    onehot = (bucket_matrix[:, :, None] == jnp.arange(BUCKETS)[None, None, :]).astype(bf16)
    bias = jnp.einsum("ijb,bh->hij", onehot, position_bias, preferred_element_type=f32)
    bias = jnp.where((apart >= 0)[None], bias, negative).astype(bf16)

    exchange = lambda value: lax.all_to_all(
        value, "wide", split_axis=0, concat_axis=0, tiled=True
    )
    gathered = lax.all_gather(self_shard, BOTH, axis=0, tiled=True)
    ff = lax.all_gather(ff_shard, BOTH, axis=0, tiled=True)
    if stepped:
        cross_gather = Gather(cube, cross_shard, 2 * width)
        one, two, bias = cross_gather.half(bias)
        most = cross_gather.most(one, two)
        memory, most[0] = tie(memory, most[0])
        gathered, *most = tie(gathered, *most)
        c_query_key, c_value_out = cross_gather.finish(most)
    else:
        cross = lax.all_gather(cross_shard, BOTH, axis=0, tiled=True)
        c_query_key, c_value_out = cross[:, : 2 * width], cross[:, 2 * width :]
    memory_rows = exchange(memory).reshape(wide, pairs, -1, width)
    w_qkv, s_out = gathered[:, : 3 * width], gathered[:, 3 * width : 4 * width]
    c_query, c_out = c_query_key[:, :width], c_value_out[:, width:]

    gains = gathered[:, 4 * width : 4 * width + 3].astype(f32).T
    gain_one, gain_two, gain_three = gains[0], gains[1], gains[2]
    f_gate_up = ff[:, : 2 * inner]
    f_down = jnp.concatenate(
        [
            ff[:, 2 * inner + c * width : 2 * inner + (c + 1) * width].reshape(devices, own, width)
            for c in range(stack)
        ],
        axis=1,
    )[:, :own_ff].reshape(inner, width)

    live = (places[None, :] < target_len[:, None]).astype(f32).reshape(slots, 1)
    inputs = targets.astype(f32).reshape(slots, width)

    normed_one = rms_norm(inputs, gain_one).astype(bf16)
    cube_of = lambda value: value.reshape(pairs, length, -1)
    qkv_one = cube_of(dot(normed_one, w_qkv, NN).astype(bf16))
    mixed_one, total_one = self_forward(qkv_one, bias)
    mixed_one = mixed_one.reshape(slots, width)
    first = inputs + dot(mixed_one, s_out, NN)
    normed_two = rms_norm(first, gain_two).astype(bf16)
    query_two = cube_of(dot(normed_two, c_query, NN).astype(bf16))
    held = ()
    for p in range(pairs):
        held = cross_forward(
            p, query_two, memory_rows, c_query_key, c_value_out, memory_len, held
        )
    mixed_two, total_two, key_two, value_two = held
    mixed_two = mixed_two.reshape(slots, width)
    second = first + dot(mixed_two, c_out, NN)
    normed_three = rms_norm(second, gain_three).astype(bf16)
    gate = dot(normed_three, f_gate_up[:, :inner], NN)
    upward = dot(normed_three, f_gate_up[:, inner:], NN)
    activated, gelu_pull = jax.vjp(gelu_tanh, gate)
    hidden = (activated * upward).astype(bf16)
    third = second + dot(hidden, f_down, NN)
    layer_out = (third * live).astype(bf16).reshape(pairs, length, width)

    grad_third = cotangent.astype(f32).reshape(slots, width) * live
    branch_ff = grad_third.astype(bf16)
    d_down = dot(hidden, branch_ff, TN).astype(bf16)
    grad_hidden = dot(branch_ff, f_down, NT)
    grad_gate = gelu_pull(grad_hidden * upward)[0].astype(bf16)
    grad_up = (grad_hidden * activated).astype(bf16)
    d_gate = dot(normed_three, grad_gate, TN).astype(bf16)
    d_up = dot(normed_three, grad_up, TN).astype(bf16)
    grad_normed_three = dot(grad_gate, f_gate_up[:, :inner], NT) + dot(
        grad_up, f_gate_up[:, inner:], NT
    )
    d_down = d_down.reshape(devices, own_ff, width)
    d_down = jnp.pad(d_down, ((0, 0), (0, stack * own - own_ff), (0, 0)))
    d_down = [
        d_down[:, c * own : (c + 1) * own].reshape(devices * own, width) for c in range(stack)
    ]
    ff_grads = lax.psum_scatter(
        jnp.concatenate([d_gate, d_up] + d_down, axis=1),
        BOTH,
        scatter_dimension=0,
        tiled=True,
    )
    _, norm_three = jax.vjp(rms_norm, second, gain_three)
    back_three, d_gain_three = norm_three(grad_normed_three)
    grad_second = grad_third + back_three

    branch_cross = grad_second.astype(bf16)
    d_cross_out = dot(mixed_two, branch_cross, TN).astype(bf16)
    grad_mixed_two = cube_of(dot(branch_cross, c_out, NT).astype(bf16))
    held, grad_memory = (), []
    for p in range(pairs):
        grad_query_two, rows_grad, *sums = cross_backward(
            p,
            query_two,
            key_two,
            value_two,
            memory_len,
            total_two,
            grad_mixed_two,
            memory_rows,
            c_query_key,
            c_value_out,
            held,
        )
        held = (*sums, grad_query_two)
        if p < pairs - 1:
            grad_memory.append(exchange(rows_grad))
    d_cross_key, d_cross_value = sums
    if stepped:
        grad_query_two, *grad_memory = tie(grad_query_two, *grad_memory)
    grad_memory.append(exchange(rows_grad))
    grad_query_two = grad_query_two.reshape(slots, width)
    d_cross_query = dot(normed_two, grad_query_two, TN).astype(bf16)
    _, norm_two = jax.vjp(rms_norm, first, gain_two)
    back_two, d_gain_two = norm_two(dot(grad_query_two, c_query, NT))
    grad_first = grad_second + back_two

    branch_self = grad_first.astype(bf16)
    d_self_out = dot(mixed_one, branch_self, TN).astype(bf16)
    grad_mixed_one = cube_of(dot(branch_self, s_out, NT).astype(bf16))
    middle = [d_cross_query, d_cross_key, d_cross_value, d_cross_out, d_self_out]
    if stepped:
        middle_sum = Scatter(cube, middle)
        middle_one = middle_sum.swap(middle_sum.to_core(), 8)
        middle_send = middle_sum.to_x(middle_one)
        grad_mixed_one, *middle_send = tie(grad_mixed_one, *middle_send)
        middle_two = middle_sum.swap(middle_send, 16)
    grads_one, diagonals = self_backward(qkv_one, bias, total_one, grad_mixed_one)
    grads_one = grads_one.reshape(slots, 3 * width)
    if stepped:
        grads_one, diagonals, *middle_two = tie(grads_one, diagonals, *middle_two)
        middle_keep, middle_send = middle_sum.to_wide(middle_one, middle_two, halved=True)
        grads_one, middle_send = tie(grads_one, middle_send)
        middle_come = cube.swap(middle_send, 1)
    d_qkv = dot(normed_one, grads_one, TN).astype(bf16)
    if stepped:
        last_sum = Scatter(cube, [d_qkv])
        last_send = last_sum.to_core()
        grads_one, *last_send = tie(grads_one, *last_send)
        last_one = last_sum.swap(last_send, 8)
    grad_normed_one = dot(grads_one, w_qkv, NT)
    _, norm_one = jax.vjp(rms_norm, inputs, gain_one)
    back_one, d_gain_one = norm_one(grad_normed_one)
    if stepped:
        last_one[0], d_gain_one = tie(last_one[0], d_gain_one)
        last_send = last_sum.to_x(last_one)
        middle_come, grad_memory[-1], *last_send = tie(
            middle_come, grad_memory[-1], *last_send
        )
        last_two = last_sum.swap(last_send, 16)
        middle_keep, middle_send = middle_sum.step(1, middle_keep, middle_come)
        middle_come = cube.swap(middle_send, 2)
    grad_targets = (grad_first + back_one).reshape(pairs, length, width)

    padded = diagonals.shape[-1]
    column = (padded - np.arange(length)) % padded
    to_bucket = np.zeros((padded, BUCKETS), np.float32)
    to_bucket[column, bucket] = 1.0
    diagonals = jnp.sum(diagonals, axis=2).reshape(HEADS, padded)
    d_position = jnp.einsum(
        "hc,cb->bh", diagonals, jnp.asarray(to_bucket), precision=lax.Precision.HIGHEST
    )
    small = jnp.concatenate(
        [d_gain_one, d_gain_two, d_gain_three, d_position.reshape(-1)]
    ).reshape(-1, LANES)
    small = jnp.pad(small, ((0, -small.shape[0] % 8), (0, 0)))
    far = [b for b in range(cube.bits) if 0 < b < wide.bit_length() - 1]
    near = [b for b in range(cube.bits) if b not in far]
    small = cube.total(small, far)
    if stepped:
        middle_keep, middle_send = middle_sum.step(2, middle_keep, middle_come)
        last_two[0], middle_send = tie(last_two[0], middle_send)
        middle_come = cube.swap(middle_send, 4)
        (last_send,) = last_sum.to_wide(last_one, last_two)
        last_send, small, middle_come, ff_grads = tie(last_send, small, middle_come, ff_grads)
        last_three = exchange(last_send)
        middle_grads = middle_sum.finish(middle_keep, middle_come)
        (d_qkv,) = last_sum.finish(last_three)
    else:
        scatter = lambda value: lax.psum_scatter(
            value, BOTH, scatter_dimension=0, tiled=True
        ).astype(f32)
        middle_grads = [scatter(value) for value in middle]
        d_qkv = scatter(d_qkv)
    small = cube.total(small, near).reshape(-1)
    gain_grads = small[: 3 * width].reshape(3, devices, width // devices)
    gain_grads = lax.dynamic_index_in_dim(gain_grads, cube.index, 1, keepdims=False)
    grad_position = small[3 * width : 3 * width + BUCKETS * HEADS].reshape(BUCKETS, HEADS)

    ff_grads = ff_grads.astype(f32)
    d_down = jnp.concatenate(
        [ff_grads[:, 2 * inner + c * width : 2 * inner + (c + 1) * width] for c in range(stack)],
        axis=0,
    )[:own_ff]
    return (
        layer_out,
        grad_targets,
        jnp.stack(grad_memory, axis=1).reshape(memory.shape).astype(f32),
        d_qkv[:, :width],
        d_qkv[:, width : 2 * width],
        d_qkv[:, 2 * width :],
        middle_grads[4],
        *middle_grads[:4],
        ff_grads[:, :inner],
        ff_grads[:, inner : 2 * inner],
        d_down,
        gain_grads[0],
        gain_grads[1],
        gain_grads[2],
        grad_position,
    )


def solution(mesh):
    rows = P(BOTH, None)
    slots = P(BOTH, None, None)
    one = P(BOTH)
    source = P("narrow", "wide", None)
    in_specs = (slots, source, slots, one, one) + (rows,) * 11 + (one,) * 3 + (P(),)
    out_specs = (slots, slots, source) + (rows,) * 11 + (one,) * 3 + (P(),)
    narrow, wide = mesh.shape["narrow"], mesh.shape["wide"]

    def body(*args):
        return on_device(*args, narrow=narrow, wide=wide)

    return jax.shard_map(body, mesh=mesh, in_specs=in_specs, out_specs=out_specs, check_vma=False)
```

```python
import functools

import jax
import jax.numpy as jnp
import numpy as np
from jax import lax
from jax.experimental import pallas as pl
from jax.experimental.pallas import tpu as pltpu
from jax.sharding import PartitionSpec as P

HEADS = 12
HEAD_DIM = 64
BUCKETS = 32
REACH = 128
LANES = 128
BOTH = ("narrow", "wide")
SHARE = 8

negative = -1e30
epsilon = 1e-06
bf16 = jnp.bfloat16
f32 = jnp.float32

NT = (((1,), (1,)), ((), ()))
NN = (((1,), (0,)), ((), ()))
TN = (((0,), (0,)), ((), ()))


def cost(flops=0, transcendentals=0, bytes_accessed=0):
    return pl.CostEstimate(
        flops=flops // SHARE,
        transcendentals=transcendentals // SHARE,
        bytes_accessed=bytes_accessed // SHARE,
    )


def dot(left, right, dims):
    return lax.dot_general(left, right, dims, preferred_element_type=f32)


def bucket_of_distance(length, buckets, reach):
    apart = np.arange(length)
    exact = buckets // 2
    safe = np.maximum(apart, 1)
    far = exact + (np.log(safe / exact) / np.log(reach / exact) * (buckets - exact)).astype(
        np.int64
    )
    far = np.minimum(far, buckets - 1)
    return np.where(apart < exact, apart, far).astype(np.int32)


def stack_heads(value):
    first = lax.broadcasted_iota(jnp.int32, value.shape, 1) < HEAD_DIM
    zero = jnp.zeros_like(value)
    return jnp.concatenate([jnp.where(first, value, zero), jnp.where(first, zero, value)], axis=0)


def join_heads(value):
    half = value.shape[0] // 2
    first = lax.broadcasted_iota(jnp.int32, (half, value.shape[1]), 1) < HEAD_DIM
    return jnp.where(first, value[:half], value[half:])


def stack_columns(total):
    return jnp.concatenate([total[:, :1], total[:, HEAD_DIM : HEAD_DIM + 1]], axis=0)


def attend(scores, v, mixed_ref, total_ref):
    top = jnp.max(scores, axis=1, keepdims=True)
    grown = jnp.exp(scores - top)
    total = jnp.sum(grown, axis=1, keepdims=True)
    mixed = dot(grown.astype(bf16), v, NN) * (1.0 / total)
    mixed_ref[0] = join_heads(mixed).astype(bf16)
    total_ref[0] = join_heads(jnp.broadcast_to(top + jnp.log(total), mixed.shape))


def attend_back(scores, total, grad, v):
    probs = jnp.exp(scores - stack_columns(total))
    grad_probs = dot(grad, v, NT)
    inner = jnp.sum(probs * grad_probs, axis=1, keepdims=True)
    return probs.astype(bf16), (probs * (grad_probs - inner)).astype(bf16)


def self_forward_kernel(q_ref, k_ref, v_ref, bias_ref, mixed_ref, total_ref):
    length = q_ref.shape[1]
    bias = bias_ref[...].reshape(2 * length, length).astype(f32)
    scores = dot(stack_heads(q_ref[0]), k_ref[0], NT) + bias
    attend(scores, v_ref[0], mixed_ref, total_ref)


def self_forward(qkv, bias):
    pairs, length, width = qkv.shape
    width //= 3
    steps = width // LANES
    part = lambda c: pl.BlockSpec((1, length, LANES), lambda p, h: (p, 0, h + c * steps))
    return pl.pallas_call(
        self_forward_kernel,
        out_shape=(
            jax.ShapeDtypeStruct((pairs, length, width), bf16),
            jax.ShapeDtypeStruct((pairs, length, width), f32),
        ),
        grid=(pairs, steps),
        in_specs=[
            part(0),
            part(1),
            part(2),
            pl.BlockSpec((2, length, length), lambda p, h: (h, 0, 0)),
        ],
        out_specs=[part(0), part(0)],
        cost_estimate=cost(
            flops=pairs * HEADS * length * length * HEAD_DIM * 4,
            transcendentals=pairs * HEADS * length * length,
            bytes_accessed=pairs * length * width * 12,
        ),
        name="self_forward",
    )(qkv, qkv, qkv, bias)


def self_backward_kernel(
    q_ref, k_ref, v_ref, bias_ref, total_ref, grad_ref, grads_ref, diagonal_ref, sum_ref
):
    p, hp = pl.program_id(0), pl.program_id(1)
    steps = pl.num_programs(1)
    length, padded = q_ref.shape[1], sum_ref.shape[-1]
    q, grad, k = stack_heads(q_ref[0]), stack_heads(grad_ref[0]), k_ref[0]

    @pl.when(p == 0)
    def _():
        sum_ref[hp] = jnp.zeros(sum_ref.shape[1:], f32)

    bias = bias_ref[...].reshape(2 * length, length).astype(f32)
    scores = dot(q, k, NT) + bias
    probs, grad_scores = attend_back(scores, total_ref[0], grad, v_ref[0])
    sum_ref[hp, :, :, :length] += grad_scores.astype(f32).reshape(2, length, length)
    found = join_heads(dot(grad_scores, k, NN)), dot(grad_scores, q, TN), dot(probs, grad, TN)
    for c in range(3):
        grads_ref[0, :, pl.ds(pl.multiple_of((hp + c * steps) * LANES, LANES), LANES)] = found[
            c
        ].astype(bf16)

    @pl.when(p == pl.num_programs(0) - 1)
    def _():
        rows = lax.broadcasted_iota(jnp.int32, (8, padded), 0)
        for h in range(2):
            held = sum_ref[hp, h, 0:8, :]
            for i in range(8, length, 8):
                held = held + pltpu.roll(sum_ref[hp, h, i : i + 8, :], padded - i, 1)
            for bit in (1, 2, 4):
                held = jnp.where(
                    (rows // bit) % 2 == 1, pltpu.roll(held, padded - bit, 1), held
                )
            diagonal_ref[0, h] = held


def self_backward(qkv, bias, total, grad):
    pairs, length, width = qkv.shape
    width //= 3
    steps = width // LANES
    padded = -(-length // LANES) * LANES
    part = lambda c: pl.BlockSpec((1, length, LANES), lambda p, h: (p, 0, h + c * steps))
    return pl.pallas_call(
        self_backward_kernel,
        out_shape=(
            jax.ShapeDtypeStruct(qkv.shape, bf16),
            jax.ShapeDtypeStruct((steps, 2, 8, padded), f32),
        ),
        grid=(pairs, steps),
        in_specs=[
            part(0),
            part(1),
            part(2),
            pl.BlockSpec((2, length, length), lambda p, h: (h, 0, 0)),
            part(0),
            part(0),
        ],
        out_specs=[
            pl.BlockSpec((1, length, 3 * width), lambda p, h: (p, 0, 0)),
            pl.BlockSpec((1, 2, 8, padded), lambda p, h: (h, 0, 0, 0)),
        ],
        scratch_shapes=[pltpu.VMEM((steps, 2, length, padded), f32)],
        cost_estimate=cost(
            flops=pairs * HEADS * length * length * HEAD_DIM * 10,
            transcendentals=pairs * HEADS * length * length,
            bytes_accessed=pairs * length * width * 18,
        ),
        name="self_backward",
    )(qkv, qkv, qkv, bias, total, grad)


def dead_rows(live_rows, rows):
    places = lax.broadcasted_iota(jnp.int32, (1, rows), 1)
    return jnp.where(places < live_rows, 0.0, negative)


def cross_forward_kernel(pair, len_ref, q_ref, memory_ref, wk_ref, wv_ref, *refs):
    mixed_ref, total_ref, k_ref, v_ref = refs[-4:]
    rows = k_ref.shape[1]
    memory = memory_ref[...].reshape(rows, -1)
    kv = dot(memory, jnp.concatenate([wk_ref[...], wv_ref[...]], axis=1), NN).astype(bf16)
    k, v = kv[:, :LANES], kv[:, LANES:]
    k_ref[0], v_ref[0] = k, v
    scores = dot(stack_heads(q_ref[0]), k, NT) + dead_rows(len_ref[pair], rows)
    attend(scores, v, mixed_ref, total_ref)


def cross_forward(pair, query, memory, query_key, value_out, lens, before):
    pairs, length, width = query.shape
    sources, _, part, _ = memory.shape
    rows = sources * part
    steps = width // LANES
    target = pl.BlockSpec((1, length, LANES), lambda h, n: (pair, 0, h))
    source = pl.BlockSpec((1, rows, LANES), lambda h, n: (pair, 0, h))
    weight = lambda c: pl.BlockSpec((width, LANES), lambda h, n: (0, h + c * steps))
    return pl.pallas_call(
        functools.partial(cross_forward_kernel, pair),
        out_shape=(
            jax.ShapeDtypeStruct(query.shape, bf16),
            jax.ShapeDtypeStruct(query.shape, f32),
            jax.ShapeDtypeStruct((pairs, rows, width), bf16),
            jax.ShapeDtypeStruct((pairs, rows, width), bf16),
        ),
        grid_spec=pltpu.PrefetchScalarGridSpec(
            num_scalar_prefetch=1,
            grid=(steps,),
            in_specs=[
                target,
                pl.BlockSpec((sources, 1, part, width), lambda h, n: (0, pair, 0, 0)),
                weight(1),
                weight(0),
            ]
            + [pl.BlockSpec(memory_space=pl.ANY)] * len(before),
            out_specs=[target, target, source, source],
        ),
        input_output_aliases={5 + i: i for i in range(len(before))},
        cost_estimate=cost(
            flops=rows * width * (length * 4 + width * 4),
            transcendentals=HEADS * length * rows,
            bytes_accessed=length * width * 8 + rows * width * 6,
        ),
        name="cross_forward",
    )(lens, query, memory, query_key, value_out, *before)


def cross_backward_kernel(
    pair, last, len_ref, q_ref, k_ref, v_ref, total_ref, grad_ref, memory_ref, qk_ref, vo_ref, *refs
):
    *refs, grads_ref, held_ref, weight_ref, sems = refs
    hp, steps = pl.program_id(0), pl.num_programs(0)
    rows, width = k_ref.shape[1], weight_ref.shape[0]
    before = pair if last else 0
    before_refs, refs = refs[:before], refs[pair + (pair > 0) :]
    grad_query_ref, grad_memory_ref, *outs = refs

    moves = [
        (qk_ref.at[:, width:], weight_ref.at[:, :width]),
        (vo_ref.at[:, :width], weight_ref.at[:, width:]),
    ]
    if last:
        moves += [(memory_ref.at[:, p], held_ref.at[p]) for p in range(pair + 1)]
        moves += [(ref, grads_ref.at[p]) for p, ref in enumerate(before_refs)]
    copies = [pltpu.make_async_copy(*move, sems.at[i]) for i, move in enumerate(moves)]

    @pl.when(hp == 0)
    def _():
        for copy in copies:
            copy.start()

    q, grad, k = stack_heads(q_ref[0]), stack_heads(grad_ref[0]), k_ref[0]
    scores = dot(q, k, NT) + dead_rows(len_ref[pair], rows)
    probs, grad_scores = attend_back(scores, total_ref[0], grad, v_ref[0])
    grad_query_ref[0] = join_heads(dot(grad_scores, k, NN)).astype(bf16)
    for c, value in enumerate((dot(grad_scores, q, TN), dot(probs, grad, TN))):
        at = pl.ds(pl.multiple_of((hp + c * steps) * LANES, LANES), LANES)
        grads_ref[before, :, at] = value.astype(bf16)

    @pl.when(hp == steps - 1)
    def _():
        for copy in copies:
            copy.wait()
        back = dot(grads_ref[before], weight_ref[...], NT).astype(bf16)
        grad_memory_ref[...] = back.reshape(grad_memory_ref.shape)
        if last:
            d_kv = sum(
                dot(held_ref[p].reshape(rows, width), grads_ref[p], TN) for p in range(pair + 1)
            )
            outs[0][...] = d_kv[:, :width].astype(bf16)
            outs[1][...] = d_kv[:, width:].astype(bf16)
        else:
            outs[0][...] = grads_ref[0]


def cross_backward(
    pair, query, key, value, lens, total, grad, memory, query_key, value_out, before
):
    pairs, length, width = query.shape
    sources, _, part, _ = memory.shape
    rows = sources * part
    steps = width // LANES
    last = pair == pairs - 1
    held = pairs if last else 1
    target = pl.BlockSpec((1, length, LANES), lambda h, n: (pair, 0, h))
    source = pl.BlockSpec((1, rows, LANES), lambda h, n: (pair, 0, h))
    anywhere = pl.BlockSpec(memory_space=pl.ANY)
    whole = lambda *shape: pl.BlockSpec(shape, lambda h, n: (0,) * len(shape))
    out_shape = [
        jax.ShapeDtypeStruct(query.shape, bf16),
        jax.ShapeDtypeStruct((sources, part, width), bf16),
    ]
    if last:
        out_shape += [jax.ShapeDtypeStruct((width, width), bf16)] * 2
    else:
        out_shape += [jax.ShapeDtypeStruct((rows, 2 * width), bf16)]
    return pl.pallas_call(
        functools.partial(cross_backward_kernel, pair, last),
        out_shape=out_shape,
        grid_spec=pltpu.PrefetchScalarGridSpec(
            num_scalar_prefetch=1,
            grid=(steps,),
            in_specs=[target, source, source, target, target] + [anywhere] * (3 + len(before)),
            out_specs=[target] + [whole(*out.shape) for out in out_shape[1:]],
            scratch_shapes=[
                pltpu.VMEM((held, rows, 2 * width), bf16),
                pltpu.VMEM((held, sources, part, width), bf16),
                pltpu.VMEM((width, 2 * width), bf16),
                pltpu.SemaphoreType.DMA((2 + 2 * pairs,)),
            ],
        ),
        input_output_aliases={8 + len(before): 0} if pair else {},
        cost_estimate=cost(
            flops=rows * width * (length * 10 + width * 8),
            transcendentals=HEADS * length * rows,
            bytes_accessed=length * width * 10 + rows * width * 8,
        ),
        name="cross_backward",
    )(lens, query, key, value, total, grad, memory, query_key, value_out, *before)


class Cube:
    def __init__(self, narrow, wide):
        self.narrow, self.wide = narrow, wide
        self.size = narrow * wide
        self.bits = self.size.bit_length() - 1
        self.index = lax.axis_index(BOTH)

    def swap(self, value, mask):
        pairs = [(i, i ^ mask) for i in range(self.size)]
        return lax.ppermute(value, BOTH, pairs)

    def total(self, value, bits):
        for bit in bits:
            value = value + self.swap(value, 1 << bit)
        return value


def merge_four(cube, pieces, split):
    r, n = pieces[0].shape

    def kernel(place_ref, *refs):
        ins, (left_ref, right_ref) = refs[:4], refs[4:]
        for m, ref in enumerate(ins):
            at = place_ref[0] ^ m
            left_ref[at] = ref[:, :split]
            right_ref[at] = ref[:, split:]

    return pl.pallas_call(
        kernel,
        out_shape=(
            jax.ShapeDtypeStruct((4, r, split), bf16),
            jax.ShapeDtypeStruct((4, r, n - split), bf16),
        ),
        grid_spec=pltpu.PrefetchScalarGridSpec(
            num_scalar_prefetch=1,
            grid=(1,),
            in_specs=[pl.BlockSpec((r, n), lambda i, s: (0, 0))] * 4,
            out_specs=[
                pl.BlockSpec((4, r, split), lambda i, s: (0, 0, 0)),
                pl.BlockSpec((4, r, n - split), lambda i, s: (0, 0, 0)),
            ],
        ),
        cost_estimate=cost(flops=0, transcendentals=0, bytes_accessed=16 * r * n),
        name="merge_four",
    )(((cube.index >> 1) & 3).reshape(1), *pieces)


def merge_two(side, mine, come, chunks):
    a, rows, n = mine.shape
    piece = pl.BlockSpec((1, rows, n // chunks), lambda i, c, s: (i, 0, c))

    def kernel(side_ref, mine_ref, come_ref, out_ref):
        out_ref[0, side_ref[0]] = mine_ref[0]
        out_ref[0, 1 - side_ref[0]] = come_ref[0]

    return pl.pallas_call(
        kernel,
        out_shape=jax.ShapeDtypeStruct((a, 2, rows, n), bf16),
        grid_spec=pltpu.PrefetchScalarGridSpec(
            num_scalar_prefetch=1,
            grid=(a, chunks),
            in_specs=[piece, piece],
            out_specs=pl.BlockSpec((1, 2, rows, n // chunks), lambda i, c, s: (i, 0, 0, c)),
        ),
        cost_estimate=cost(
            flops=0, transcendentals=0, bytes_accessed=8 * a * rows * n
        ),
        name="merge_two",
    )(side.reshape(1), mine, come)


class Gather:
    def __init__(self, cube, shard, split):
        self.cube = cube
        pieces = [shard] + [cube.swap(shard, m << 1) for m in (1, 2, 3)]
        self.start = merge_four(cube, pieces, split)

    def half(self, filler):
        cube = self.cube
        one, two = self.start
        r = one.shape[1]
        come_one, come_two = cube.swap(one, 1), cube.swap(two.reshape(1, 4 * r, -1), 16)
        come_one, come_two, filler = tie(come_one, come_two, filler)
        one = merge_two(self.side(0), one, come_one, 1)
        two = merge_two(self.side(4), two.reshape(1, 4 * r, -1), come_two, 1)
        return one.reshape(1, 8 * r, -1), two.reshape(8, r, -1), filler

    def side(self, bit):
        return (self.cube.index >> bit) & 1

    def most(self, one, two):
        cube = self.cube
        r = two.shape[1]
        one = merge_two(self.side(4), one, cube.swap(one, 16), 2 - one.shape[2] // LANES % 2)
        two = merge_two(self.side(0), two, cube.swap(two, 1), 1)
        return [one.reshape(2, 8 * r, -1), two.reshape(2, 8 * r, -1)]

    def finish(self, values):
        core = self.side(3)
        chunks = lambda value: 2 - value.shape[2] // LANES % 2
        return [
            merge_two(core, value, self.cube.swap(value, 8), chunks(value)).reshape(
                -1, value.shape[2]
            )
            for value in values
        ]


class Scatter:
    def __init__(self, cube, grads):
        self.cube = cube
        self.shapes = [(grad.shape[0] // cube.size, grad.shape[1]) for grad in grads]
        self.own = self.shapes[0][0]
        self.flat = [i for i, (r, _) in enumerate(self.shapes) if r == self.own]
        self.tall = [i for i, (r, _) in enumerate(self.shapes) if r != self.own]
        self.grads = [
            grad.reshape(2, 2, cube.wide * r, n)
            for grad, (r, n) in zip(grads, self.shapes, strict=True)
        ]
        self.sides = jnp.stack([cube.index >> 4, (cube.index >> 3) & 1, cube.index & 1])
        self.groups = [(self.own, sum(self.shapes[i][1] for i in self.flat))]
        self.groups += [self.shapes[i] for i in self.tall]

    def message(self, come, own, places, lead=1, packed=0):
        wide = self.cube.wide
        split = 2
        n_grads, n_groups = len(self.grads), len(self.groups)
        n_ins = n_grads + len(come)
        widths = [n for _, n in self.groups]
        stack = [-(-r // self.own) for r, _ in self.groups]

        def kernel(sides_ref, *refs):
            ins, outs = refs[:n_ins], refs[n_ins:]
            flat = [ins[i][0, 0] for i in self.flat]
            values = [flat[0] if len(flat) == 1 else jnp.concatenate(flat, axis=1)]
            values += [ins[i][0, 0] for i in self.tall]
            for k, ref in enumerate(ins[n_grads:]):
                got = ref[...]
                got = got.reshape(got.shape[-2:])
                i = k % n_groups
                values[i] = values[i].astype(f32) + got.astype(f32)
            if not packed:
                for out_ref, value in zip(outs, values, strict=True):
                    out_ref[...] = value.astype(bf16).reshape(out_ref.shape)
                return
            at = 0
            for value, (r, n), high in zip(values, self.groups, stack, strict=True):
                value = value.astype(f32).reshape(wide // split, r, n)
                for c in range(high):
                    part = value[:, c * self.own : (c + 1) * self.own].astype(bf16)
                    if packed == 1:
                        outs[0][:, : part.shape[1], at : at + n] = part
                    else:
                        side = sides_ref[2]
                        for i in range(0, part.shape[0], 2):
                            for flip, out_ref in enumerate(outs):
                                out_ref[i // 2, : part.shape[1], at : at + n] = jnp.where(
                                    side == flip, part[i], part[i + 1]
                                )
                    at += n

        in_specs = [
            pl.BlockSpec((1, 1, wide * r // split, n), lambda i, j, s: (*own(i, s), j, 0))
            for r, n in self.shapes
        ]
        for k, value in enumerate(come):
            at = places[k // n_groups]
            r, n = self.groups[k % n_groups]
            in_specs.append(
                pl.BlockSpec(
                    (1,) * (value.ndim - 2) + (wide * r // split, n),
                    lambda i, j, s, at=at: (*at(s), j, 0),
                )
            )
        if packed:
            n = sum(w * high for w, high in zip(widths, stack, strict=True))
            high = wide // packed
            out_shape = [jax.ShapeDtypeStruct((high, self.own, n), bf16)] * packed
            out_specs = [
                pl.BlockSpec((high // split, self.own, n), lambda i, j, s: (j, 0, 0))
            ] * packed
        else:
            out_shape = [jax.ShapeDtypeStruct((lead, wide * r, n), bf16) for r, n in self.groups]
            out_specs = [
                pl.BlockSpec((1, wide * r // split, n), lambda i, j, s: (i, j, 0))
                for r, n in self.groups
            ]
        size = sum(int(np.prod(out.shape)) for out in out_shape)
        return pl.pallas_call(
            kernel,
            out_shape=out_shape,
            grid_spec=pltpu.PrefetchScalarGridSpec(
                num_scalar_prefetch=1,
                grid=(lead, split),
                in_specs=in_specs,
                out_specs=out_specs,
            ),
            cost_estimate=cost(
                flops=size, transcendentals=0, bytes_accessed=4 * size
            ),
            name="message",
        )(self.sides, *self.grads, *come)

    def swap(self, values, mask):
        return [self.cube.swap(value, mask) for value in values]

    def to_core(self):
        return self.message([], lambda i, s: (i, 1 - s[1]), [], lead=2)

    def to_x(self, one):
        return self.message(one, lambda i, s: (1 - s[0], s[1]), [lambda s: (1 - s[0],)])

    def to_wide(self, one, two, halved=False):
        places = [lambda s: (s[0],), lambda s: (0,)]
        return self.message(
            [*one, *two], lambda i, s: (s[0], s[1]), places, packed=1 + halved
        )

    def step(self, bit, mine, come):
        blocks, r, n = mine.shape

        def kernel(side_ref, *refs):
            keep_ref, send_ref = refs[-2:]
            side = side_ref[0]
            for i in range(blocks // 2):
                for out_ref, at in ((keep_ref, 2 * i + side), (send_ref, 2 * i + 1 - side)):
                    value = refs[0][at].astype(f32) + refs[1][at].astype(f32)
                    out_ref[i] = value.astype(bf16)

        whole = pl.BlockSpec(mine.shape, lambda i, s: (0, 0, 0))
        half = pl.BlockSpec((blocks // 2, r, n), lambda i, s: (0, 0, 0))
        return pl.pallas_call(
            kernel,
            out_shape=[jax.ShapeDtypeStruct((blocks // 2, r, n), bf16)] * 2,
            grid_spec=pltpu.PrefetchScalarGridSpec(
                num_scalar_prefetch=1,
                grid=(1,),
                in_specs=[whole, whole],
                out_specs=[half, half],
            ),
            cost_estimate=cost(
                flops=mine.size, transcendentals=0, bytes_accessed=6 * mine.size
            ),
            name="step",
        )(((self.cube.index >> bit) & 1).reshape(1), mine, come)

    def finish(self, *come):
        def kernel(*refs):
            ins, outs = refs[: len(come)], refs[len(come) :]
            blocks = [ref[i] for ref in ins for i in range(ref.shape[0])]
            value = blocks[0].astype(f32)
            for block in blocks[1:]:
                value = value + block.astype(f32)
            at = 0
            for i in self.flat:
                n = self.shapes[i][1]
                outs[i][...] = value[:, at : at + n]
                at += n
            for i in self.tall:
                r, n = self.shapes[i]
                for c in range(0, r, self.own):
                    high = min(self.own, r - c)
                    outs[i][c : c + high] = value[:high, at : at + n]
                    at += n

        size = sum(value.size for value in come)
        return pl.pallas_call(
            kernel,
            out_shape=tuple(jax.ShapeDtypeStruct(shape, f32) for shape in self.shapes),
            cost_estimate=cost(
                flops=size, transcendentals=0, bytes_accessed=4 * size
            ),
            name="finish",
        )(*come)


def tie(*values):
    return lax.optimization_barrier(values)


def pack_shards(parts, widths, rows):
    flat = [part for group in parts for part in group]

    def kernel(*refs):
        ins, outs = refs[: len(flat)], refs[len(flat) :]
        refs_of = iter(ins)
        for out_ref, group in zip(outs, parts, strict=True):
            at = 0
            for array, start, count in group:
                ref, n = next(refs_of), array.shape[1]
                out_ref[:count, at : at + n] = ref[start : start + count, :]
                if count < rows:
                    out_ref[count:, at : at + n] = jnp.zeros((rows - count, n), bf16)
                at += n

    return pl.pallas_call(
        kernel,
        out_shape=tuple(jax.ShapeDtypeStruct((rows, n), bf16) for n in widths),
        name="pack",
    )(*[part[0] for part in flat])


def rms_norm(value, gain):
    return value * lax.rsqrt(jnp.mean(value * value, axis=-1, keepdims=True) + epsilon) * gain


def gelu_tanh(value):
    return jax.nn.gelu(value, approximate=True)


def on_device(
    targets,
    memory,
    cotangent,
    target_len,
    memory_len,
    self_query,
    self_key,
    self_value,
    self_out,
    cross_query,
    cross_key,
    cross_value,
    cross_out,
    ff_gate,
    ff_up,
    ff_down,
    self_gain,
    cross_gain,
    ff_gain,
    position_bias,
    narrow,
    wide,
):
    cube = Cube(narrow, wide)
    pairs, length, width = targets.shape
    slots = pairs * length
    own, own_ff = self_query.shape[0], ff_down.shape[0]
    inner = ff_gate.shape[1]
    devices = cube.size
    stepped = narrow == 4 and wide == 8 and own % 8 == 0

    gains = jnp.stack([self_gain, cross_gain, ff_gain], axis=1)
    gains = jnp.pad(gains, ((0, 0), (0, LANES - 3)))
    stack = -(-own_ff // own)
    whole = lambda *arrays: [(array, 0, own) for array in arrays]
    self_shard, cross_shard, ff_shard = pack_shards(
        [
            whole(self_query, self_key, self_value, self_out, gains),
            whole(cross_query, cross_key, cross_value, cross_out),
            whole(ff_gate, ff_up)
            + [(ff_down, c * own, min(own, own_ff - c * own)) for c in range(stack)],
        ],
        [4 * width + LANES, 4 * width, 2 * inner + stack * width],
        own,
    )
    places = jnp.arange(length)
    apart = places[:, None] - places[None, :]
    bucket = bucket_of_distance(length, BUCKETS, REACH)
    starts = [int(np.argmax(bucket >= b)) for b in range(1, int(bucket[-1]) + 1)]
    bucket_matrix = sum((apart >= start).astype(jnp.int32) for start in starts)
    onehot = (bucket_matrix[:, :, None] == jnp.arange(BUCKETS)[None, None, :]).astype(bf16)
    bias = jnp.einsum("ijb,bh->hij", onehot, position_bias, preferred_element_type=f32)
    bias = jnp.where((apart >= 0)[None], bias, negative).astype(bf16)

    exchange = lambda value: lax.all_to_all(
        value, "wide", split_axis=0, concat_axis=0, tiled=True
    )
    gathered = lax.all_gather(self_shard, BOTH, axis=0, tiled=True)
    ff = lax.all_gather(ff_shard, BOTH, axis=0, tiled=True)
    if stepped:
        cross_gather = Gather(cube, cross_shard, 2 * width)
        one, two, bias = cross_gather.half(bias)
        most = cross_gather.most(one, two)
        memory, most[0] = tie(memory, most[0])
        gathered, *most = tie(gathered, *most)
        c_query_key, c_value_out = cross_gather.finish(most)
    else:
        cross = lax.all_gather(cross_shard, BOTH, axis=0, tiled=True)
        c_query_key, c_value_out = cross[:, : 2 * width], cross[:, 2 * width :]
    memory_rows = exchange(memory).reshape(wide, pairs, -1, width)
    w_qkv, s_out = gathered[:, : 3 * width], gathered[:, 3 * width : 4 * width]
    c_query, c_out = c_query_key[:, :width], c_value_out[:, width:]

    gains = gathered[:, 4 * width : 4 * width + 3].astype(f32).T
    gain_one, gain_two, gain_three = gains[0], gains[1], gains[2]
    f_gate_up = ff[:, : 2 * inner]
    f_down = jnp.concatenate(
        [
            ff[:, 2 * inner + c * width : 2 * inner + (c + 1) * width].reshape(devices, own, width)
            for c in range(stack)
        ],
        axis=1,
    )[:, :own_ff].reshape(inner, width)

    live = (places[None, :] < target_len[:, None]).astype(f32).reshape(slots, 1)
    inputs = targets.astype(f32).reshape(slots, width)

    normed_one = rms_norm(inputs, gain_one).astype(bf16)
    cube_of = lambda value: value.reshape(pairs, length, -1)
    qkv_one = cube_of(dot(normed_one, w_qkv, NN).astype(bf16))
    mixed_one, total_one = self_forward(qkv_one, bias)
    mixed_one = mixed_one.reshape(slots, width)
    first = inputs + dot(mixed_one, s_out, NN)
    normed_two = rms_norm(first, gain_two).astype(bf16)
    query_two = cube_of(dot(normed_two, c_query, NN).astype(bf16))
    held = ()
    for p in range(pairs):
        held = cross_forward(
            p, query_two, memory_rows, c_query_key, c_value_out, memory_len, held
        )
    mixed_two, total_two, key_two, value_two = held
    mixed_two = mixed_two.reshape(slots, width)
    second = first + dot(mixed_two, c_out, NN)
    normed_three = rms_norm(second, gain_three).astype(bf16)
    gate = dot(normed_three, f_gate_up[:, :inner], NN)
    upward = dot(normed_three, f_gate_up[:, inner:], NN)
    activated, gelu_pull = jax.vjp(gelu_tanh, gate)
    hidden = (activated * upward).astype(bf16)
    third = second + dot(hidden, f_down, NN)
    layer_out = (third * live).astype(bf16).reshape(pairs, length, width)

    grad_third = cotangent.astype(f32).reshape(slots, width) * live
    branch_ff = grad_third.astype(bf16)
    d_down = dot(hidden, branch_ff, TN).astype(bf16)
    grad_hidden = dot(branch_ff, f_down, NT)
    grad_gate = gelu_pull(grad_hidden * upward)[0].astype(bf16)
    grad_up = (grad_hidden * activated).astype(bf16)
    d_gate = dot(normed_three, grad_gate, TN).astype(bf16)
    d_up = dot(normed_three, grad_up, TN).astype(bf16)
    grad_normed_three = dot(grad_gate, f_gate_up[:, :inner], NT) + dot(
        grad_up, f_gate_up[:, inner:], NT
    )
    d_down = d_down.reshape(devices, own_ff, width)
    d_down = jnp.pad(d_down, ((0, 0), (0, stack * own - own_ff), (0, 0)))
    d_down = [
        d_down[:, c * own : (c + 1) * own].reshape(devices * own, width) for c in range(stack)
    ]
    ff_grads = lax.psum_scatter(
        jnp.concatenate([d_gate, d_up] + d_down, axis=1),
        BOTH,
        scatter_dimension=0,
        tiled=True,
    )
    _, norm_three = jax.vjp(rms_norm, second, gain_three)
    back_three, d_gain_three = norm_three(grad_normed_three)
    grad_second = grad_third + back_three

    branch_cross = grad_second.astype(bf16)
    d_cross_out = dot(mixed_two, branch_cross, TN).astype(bf16)
    grad_mixed_two = cube_of(dot(branch_cross, c_out, NT).astype(bf16))
    held, grad_memory = (), []
    for p in range(pairs):
        grad_query_two, rows_grad, *found = cross_backward(
            p,
            query_two,
            key_two,
            value_two,
            memory_len,
            total_two,
            grad_mixed_two,
            memory_rows,
            c_query_key,
            c_value_out,
            held,
        )
        held = (*held[:-1], *found, grad_query_two)
        if p < pairs - 1:
            grad_memory.append(exchange(rows_grad))
    d_cross_key, d_cross_value = found
    grad_query_two = grad_query_two.reshape(slots, width)
    d_cross_query = dot(normed_two, grad_query_two, TN).astype(bf16)
    _, norm_two = jax.vjp(rms_norm, first, gain_two)
    back_two, d_gain_two = norm_two(dot(grad_query_two, c_query, NT))
    if stepped:
        back_two, *grad_memory = tie(back_two, *grad_memory)
    grad_memory.append(exchange(rows_grad))
    grad_first = grad_second + back_two

    branch_self = grad_first.astype(bf16)
    d_self_out = dot(mixed_one, branch_self, TN).astype(bf16)
    grad_mixed_one = cube_of(dot(branch_self, s_out, NT).astype(bf16))
    middle = [d_cross_query, d_cross_key, d_cross_value, d_cross_out, d_self_out]
    if stepped:
        middle_sum = Scatter(cube, middle)
        middle_one = middle_sum.swap(middle_sum.to_core(), 8)
        middle_send = middle_sum.to_x(middle_one)
        grad_mixed_one, *middle_send = tie(grad_mixed_one, *middle_send)
        middle_two = middle_sum.swap(middle_send, 16)
    grads_one, diagonals = self_backward(qkv_one, bias, total_one, grad_mixed_one)
    grads_one = grads_one.reshape(slots, 3 * width)
    d_qkv = dot(normed_one, grads_one, TN).astype(bf16)
    if stepped:
        last_sum = Scatter(cube, [d_qkv])
        last_send = last_sum.to_core()
        grads_one, diagonals, *tied = tie(grads_one, diagonals, *middle_two, *last_send)
        middle_two, last_send = tied[: len(middle_two)], tied[len(middle_two) :]
        last_one = last_sum.swap(last_send, 8)
        (middle_send,) = middle_sum.to_wide(middle_one, middle_two)
        grads_one, middle_send = tie(grads_one, middle_send)
        middle_three = exchange(middle_send)
    grad_normed_one = dot(grads_one, w_qkv, NT)
    _, norm_one = jax.vjp(rms_norm, inputs, gain_one)
    back_one, d_gain_one = norm_one(grad_normed_one)
    if stepped:
        last_one[0], d_gain_one = tie(last_one[0], d_gain_one)
        last_send = last_sum.to_x(last_one)
        grad_memory[-1], *last_send = tie(grad_memory[-1], *last_send)
        last_two = last_sum.swap(last_send, 16)
    grad_targets = (grad_first + back_one).reshape(pairs, length, width)

    padded = diagonals.shape[-1]
    column = (padded - np.arange(length)) % padded
    to_bucket = np.zeros((padded, BUCKETS), np.float32)
    to_bucket[column, bucket] = 1.0
    diagonals = jnp.sum(diagonals, axis=2).reshape(HEADS, padded)
    d_position = jnp.einsum(
        "hc,cb->bh", diagonals, jnp.asarray(to_bucket), precision=lax.Precision.HIGHEST
    )
    small = jnp.concatenate(
        [d_gain_one, d_gain_two, d_gain_three, d_position.reshape(-1)]
    ).reshape(-1, LANES)
    small = jnp.pad(small, ((0, -small.shape[0] % 8), (0, 0)))
    far = [b for b in range(cube.bits) if 0 < b < wide.bit_length() - 1]
    near = [b for b in range(cube.bits) if b not in far]
    small = cube.total(small, far)
    if stepped:
        last_two[0], middle_three = tie(last_two[0], middle_three)
        (last_send,) = last_sum.to_wide(last_one, last_two)
        last_send, ff_grads = tie(last_send, ff_grads)
        last_three = exchange(last_send)
        middle_grads = middle_sum.finish(middle_three)
        (d_qkv,) = last_sum.finish(last_three)
    else:
        scatter = lambda value: lax.psum_scatter(
            value, BOTH, scatter_dimension=0, tiled=True
        ).astype(f32)
        middle_grads = [scatter(value) for value in middle]
        d_qkv = scatter(d_qkv)
    small = cube.total(small, near).reshape(-1)
    gain_grads = small[: 3 * width].reshape(3, devices, width // devices)
    gain_grads = lax.dynamic_index_in_dim(gain_grads, cube.index, 1, keepdims=False)
    grad_position = small[3 * width : 3 * width + BUCKETS * HEADS].reshape(BUCKETS, HEADS)

    ff_grads = ff_grads.astype(f32)
    d_down = jnp.concatenate(
        [ff_grads[:, 2 * inner + c * width : 2 * inner + (c + 1) * width] for c in range(stack)],
        axis=0,
    )[:own_ff]
    return (
        layer_out,
        grad_targets,
        jnp.stack(grad_memory, axis=1).reshape(memory.shape).astype(f32),
        d_qkv[:, :width],
        d_qkv[:, width : 2 * width],
        d_qkv[:, 2 * width :],
        middle_grads[4],
        *middle_grads[:4],
        ff_grads[:, :inner],
        ff_grads[:, inner : 2 * inner],
        d_down,
        gain_grads[0],
        gain_grads[1],
        gain_grads[2],
        grad_position,
    )


def solution(mesh):
    rows = P(BOTH, None)
    slots = P(BOTH, None, None)
    one = P(BOTH)
    source = P("narrow", "wide", None)
    in_specs = (slots, source, slots, one, one) + (rows,) * 11 + (one,) * 3 + (P(),)
    out_specs = (slots, slots, source) + (rows,) * 11 + (one,) * 3 + (P(),)
    narrow, wide = mesh.shape["narrow"], mesh.shape["wide"]

    def body(*args):
        return on_device(*args, narrow=narrow, wide=wide)

    return jax.shard_map(body, mesh=mesh, in_specs=in_specs, out_specs=out_specs, check_vma=False)
```

```python
import functools

import jax
import jax.numpy as jnp
import numpy as np
from jax import lax
from jax.experimental import pallas as pl
from jax.experimental.pallas import tpu as pltpu
from jax.sharding import PartitionSpec as P

HEADS = 12
HEAD_DIM = 64
BUCKETS = 32
REACH = 128
LANES = 128
BOTH = ("narrow", "wide")
SHARE = 8

negative = -1e30
epsilon = 1e-06
bf16 = jnp.bfloat16
f32 = jnp.float32

NT = (((1,), (1,)), ((), ()))
NN = (((1,), (0,)), ((), ()))
TN = (((0,), (0,)), ((), ()))


def cost(flops=0, transcendentals=0, bytes_accessed=0):
    return pl.CostEstimate(
        flops=flops // SHARE,
        transcendentals=transcendentals // SHARE,
        bytes_accessed=bytes_accessed // SHARE,
    )


def dot(left, right, dims):
    return lax.dot_general(left, right, dims, preferred_element_type=f32)


def bucket_of_distance(length, buckets, reach):
    apart = np.arange(length)
    exact = buckets // 2
    safe = np.maximum(apart, 1)
    far = exact + (np.log(safe / exact) / np.log(reach / exact) * (buckets - exact)).astype(
        np.int64
    )
    far = np.minimum(far, buckets - 1)
    return np.where(apart < exact, apart, far).astype(np.int32)


def stack_heads(value):
    first = lax.broadcasted_iota(jnp.int32, value.shape, 1) < HEAD_DIM
    zero = jnp.zeros_like(value)
    return jnp.concatenate([jnp.where(first, value, zero), jnp.where(first, zero, value)], axis=0)


def join_heads(value):
    half = value.shape[0] // 2
    first = lax.broadcasted_iota(jnp.int32, (half, value.shape[1]), 1) < HEAD_DIM
    return jnp.where(first, value[:half], value[half:])


def stack_columns(total):
    return jnp.concatenate([total[:, :1], total[:, HEAD_DIM : HEAD_DIM + 1]], axis=0)


def attend(scores, v, mixed_ref, total_ref):
    top = jnp.max(scores, axis=1, keepdims=True)
    grown = jnp.exp(scores - top)
    total = jnp.sum(grown, axis=1, keepdims=True)
    mixed = dot(grown.astype(bf16), v, NN) * (1.0 / total)
    mixed_ref[0] = join_heads(mixed).astype(bf16)
    total_ref[0] = join_heads(jnp.broadcast_to(top + jnp.log(total), mixed.shape))


def attend_back(scores, total, grad, v):
    probs = jnp.exp(scores - stack_columns(total))
    grad_probs = dot(grad, v, NT)
    inner = jnp.sum(probs * grad_probs, axis=1, keepdims=True)
    return probs.astype(bf16), (probs * (grad_probs - inner)).astype(bf16)


def self_forward_kernel(q_ref, k_ref, v_ref, bias_ref, mixed_ref, total_ref):
    length = q_ref.shape[1]
    bias = bias_ref[...].reshape(2 * length, length).astype(f32)
    scores = dot(stack_heads(q_ref[0]), k_ref[0], NT) + bias
    attend(scores, v_ref[0], mixed_ref, total_ref)


def self_forward(qkv, bias):
    pairs, length, width = qkv.shape
    width //= 3
    steps = width // LANES
    part = lambda c: pl.BlockSpec((1, length, LANES), lambda p, h: (p, 0, h + c * steps))
    return pl.pallas_call(
        self_forward_kernel,
        out_shape=(
            jax.ShapeDtypeStruct((pairs, length, width), bf16),
            jax.ShapeDtypeStruct((pairs, length, width), f32),
        ),
        grid=(pairs, steps),
        in_specs=[
            part(0),
            part(1),
            part(2),
            pl.BlockSpec((2, length, length), lambda p, h: (h, 0, 0)),
        ],
        out_specs=[part(0), part(0)],
        cost_estimate=cost(
            flops=pairs * HEADS * length * length * HEAD_DIM * 4,
            transcendentals=pairs * HEADS * length * length,
            bytes_accessed=pairs * length * width * 12,
        ),
        name="self_forward",
    )(qkv, qkv, qkv, bias)


def self_backward_kernel(
    q_ref, k_ref, v_ref, bias_ref, total_ref, grad_ref, grads_ref, diagonal_ref, sum_ref
):
    p, hp = pl.program_id(0), pl.program_id(1)
    steps = pl.num_programs(1)
    length, padded = q_ref.shape[1], sum_ref.shape[-1]
    q, grad, k = stack_heads(q_ref[0]), stack_heads(grad_ref[0]), k_ref[0]

    @pl.when(p == 0)
    def _():
        sum_ref[hp] = jnp.zeros(sum_ref.shape[1:], f32)

    bias = bias_ref[...].reshape(2 * length, length).astype(f32)
    scores = dot(q, k, NT) + bias
    probs, grad_scores = attend_back(scores, total_ref[0], grad, v_ref[0])
    sum_ref[hp, :, :, :length] += grad_scores.astype(f32).reshape(2, length, length)
    found = join_heads(dot(grad_scores, k, NN)), dot(grad_scores, q, TN), dot(probs, grad, TN)
    for c in range(3):
        grads_ref[0, :, pl.ds(pl.multiple_of((hp + c * steps) * LANES, LANES), LANES)] = found[
            c
        ].astype(bf16)

    @pl.when(p == pl.num_programs(0) - 1)
    def _():
        rows = lax.broadcasted_iota(jnp.int32, (8, padded), 0)
        for h in range(2):
            held = sum_ref[hp, h, 0:8, :]
            for i in range(8, length, 8):
                held = held + pltpu.roll(sum_ref[hp, h, i : i + 8, :], padded - i, 1)
            for bit in (1, 2, 4):
                held = jnp.where(
                    (rows // bit) % 2 == 1, pltpu.roll(held, padded - bit, 1), held
                )
            diagonal_ref[0, h] = held


def self_backward(qkv, bias, total, grad):
    pairs, length, width = qkv.shape
    width //= 3
    steps = width // LANES
    padded = -(-length // LANES) * LANES
    part = lambda c: pl.BlockSpec((1, length, LANES), lambda p, h: (p, 0, h + c * steps))
    return pl.pallas_call(
        self_backward_kernel,
        out_shape=(
            jax.ShapeDtypeStruct(qkv.shape, bf16),
            jax.ShapeDtypeStruct((steps, 2, 8, padded), f32),
        ),
        grid=(pairs, steps),
        in_specs=[
            part(0),
            part(1),
            part(2),
            pl.BlockSpec((2, length, length), lambda p, h: (h, 0, 0)),
            part(0),
            part(0),
        ],
        out_specs=[
            pl.BlockSpec((1, length, 3 * width), lambda p, h: (p, 0, 0)),
            pl.BlockSpec((1, 2, 8, padded), lambda p, h: (h, 0, 0, 0)),
        ],
        scratch_shapes=[pltpu.VMEM((steps, 2, length, padded), f32)],
        cost_estimate=cost(
            flops=pairs * HEADS * length * length * HEAD_DIM * 10,
            transcendentals=pairs * HEADS * length * length,
            bytes_accessed=pairs * length * width * 18,
        ),
        name="self_backward",
    )(qkv, qkv, qkv, bias, total, grad)


def dead_rows(live_rows, rows):
    places = lax.broadcasted_iota(jnp.int32, (1, rows), 1)
    return jnp.where(places < live_rows, 0.0, negative)


def cross_forward_kernel(pair, len_ref, q_ref, memory_ref, wk_ref, wv_ref, *refs):
    mixed_ref, total_ref, k_ref, v_ref = refs[-4:]
    rows = k_ref.shape[1]
    memory = memory_ref[...].reshape(rows, -1)
    kv = dot(memory, jnp.concatenate([wk_ref[...], wv_ref[...]], axis=1), NN).astype(bf16)
    k, v = kv[:, :LANES], kv[:, LANES:]
    k_ref[0], v_ref[0] = k, v
    scores = dot(stack_heads(q_ref[0]), k, NT) + dead_rows(len_ref[pair], rows)
    attend(scores, v, mixed_ref, total_ref)


def cross_forward(pair, query, memory, query_key, value_out, lens, before):
    pairs, length, width = query.shape
    sources, _, part, _ = memory.shape
    rows = sources * part
    steps = width // LANES
    target = pl.BlockSpec((1, length, LANES), lambda h, n: (pair, 0, h))
    source = pl.BlockSpec((1, rows, LANES), lambda h, n: (pair, 0, h))
    weight = lambda c: pl.BlockSpec((width, LANES), lambda h, n: (0, h + c * steps))
    return pl.pallas_call(
        functools.partial(cross_forward_kernel, pair),
        out_shape=(
            jax.ShapeDtypeStruct(query.shape, bf16),
            jax.ShapeDtypeStruct(query.shape, f32),
            jax.ShapeDtypeStruct((pairs, rows, width), bf16),
            jax.ShapeDtypeStruct((pairs, rows, width), bf16),
        ),
        grid_spec=pltpu.PrefetchScalarGridSpec(
            num_scalar_prefetch=1,
            grid=(steps,),
            in_specs=[
                target,
                pl.BlockSpec((sources, 1, part, width), lambda h, n: (0, pair, 0, 0)),
                weight(1),
                weight(0),
            ]
            + [pl.BlockSpec(memory_space=pl.ANY)] * len(before),
            out_specs=[target, target, source, source],
        ),
        input_output_aliases={5 + i: i for i in range(len(before))},
        cost_estimate=cost(
            flops=rows * width * (length * 4 + width * 4),
            transcendentals=HEADS * length * rows,
            bytes_accessed=length * width * 8 + rows * width * 6,
        ),
        name="cross_forward",
    )(lens, query, memory, query_key, value_out, *before)


def cross_backward_kernel(
    pair, last, len_ref, q_ref, k_ref, v_ref, total_ref, grad_ref, memory_ref, qk_ref, vo_ref, *refs
):
    *refs, grads_ref, held_ref, weight_ref, sems = refs
    hp, steps = pl.program_id(0), pl.num_programs(0)
    rows, width = k_ref.shape[1], weight_ref.shape[0]
    before = pair if last else 0
    before_refs, refs = refs[:before], refs[pair + 2 * (pair > 0) :]
    grad_query_ref, grad_memory_ref, *outs = refs

    moves = [
        (qk_ref.at[:, width:], weight_ref.at[:, :width]),
        (vo_ref.at[:, :width], weight_ref.at[:, width:]),
    ]
    if last:
        moves += [(memory_ref.at[:, p], held_ref.at[p]) for p in range(pair + 1)]
        moves += [(ref, grads_ref.at[p]) for p, ref in enumerate(before_refs)]
    copies = [pltpu.make_async_copy(*move, sems.at[i]) for i, move in enumerate(moves)]

    @pl.when(hp == 0)
    def _():
        for copy in copies:
            copy.start()

    q, grad, k = stack_heads(q_ref[0]), stack_heads(grad_ref[0]), k_ref[0]
    scores = dot(q, k, NT) + dead_rows(len_ref[pair], rows)
    probs, grad_scores = attend_back(scores, total_ref[0], grad, v_ref[0])
    grad_query_ref[0] = join_heads(dot(grad_scores, k, NN)).astype(bf16)
    for c, value in enumerate((dot(grad_scores, q, TN), dot(probs, grad, TN))):
        at = pl.ds(pl.multiple_of((hp + c * steps) * LANES, LANES), LANES)
        grads_ref[before, :, at] = value.astype(bf16)

    @pl.when(hp == steps - 1)
    def _():
        for copy in copies:
            copy.wait()
        back = dot(grads_ref[before], weight_ref[...], NT).astype(bf16)
        grad_memory_ref[...] = back.reshape(grad_memory_ref.shape)
        if last:
            d_kv = sum(
                dot(held_ref[p].reshape(rows, width), grads_ref[p], TN) for p in range(pair + 1)
            )
            outs[0][...] = d_kv[:, :width].astype(bf16)
            outs[1][...] = d_kv[:, width:].astype(bf16)
        else:
            outs[0][...] = grads_ref[0]


def cross_backward(
    pair, query, key, value, lens, total, grad, memory, query_key, value_out, before
):
    pairs, length, width = query.shape
    sources, _, part, _ = memory.shape
    rows = sources * part
    steps = width // LANES
    last = pair == pairs - 1
    held = pairs if last else 1
    target = pl.BlockSpec((1, length, LANES), lambda h, n: (pair, 0, h))
    source = pl.BlockSpec((1, rows, LANES), lambda h, n: (pair, 0, h))
    anywhere = pl.BlockSpec(memory_space=pl.ANY)
    whole = lambda *shape: pl.BlockSpec(shape, lambda h, n: (0,) * len(shape))
    out_shape = [
        jax.ShapeDtypeStruct(query.shape, bf16),
        jax.ShapeDtypeStruct(memory.shape, bf16),
    ]
    given = pl.BlockSpec((sources, 1, part, width), lambda h, n: (0, pair, 0, 0))
    if last:
        out_shape += [jax.ShapeDtypeStruct((width, width), bf16)] * 2
    else:
        out_shape += [jax.ShapeDtypeStruct((rows, 2 * width), bf16)]
    return pl.pallas_call(
        functools.partial(cross_backward_kernel, pair, last),
        out_shape=out_shape,
        grid_spec=pltpu.PrefetchScalarGridSpec(
            num_scalar_prefetch=1,
            grid=(steps,),
            in_specs=[target, source, source, target, target] + [anywhere] * (3 + len(before)),
            out_specs=[target, given] + [whole(*out.shape) for out in out_shape[2:]],
            scratch_shapes=[
                pltpu.VMEM((held, rows, 2 * width), bf16),
                pltpu.VMEM((held, sources, part, width), bf16),
                pltpu.VMEM((width, 2 * width), bf16),
                pltpu.SemaphoreType.DMA((2 + 2 * pairs,)),
            ],
        ),
        input_output_aliases={7 + len(before): 0, 8 + len(before): 1} if pair else {},
        cost_estimate=cost(
            flops=rows * width * (length * 10 + width * 8),
            transcendentals=HEADS * length * rows,
            bytes_accessed=length * width * 10 + rows * width * 8,
        ),
        name="cross_backward",
    )(lens, query, key, value, total, grad, memory, query_key, value_out, *before)


HIDDEN = 512
SLOPE = float(np.sqrt(2 / np.pi))
CUBIC = 0.044715


def feed_forward_kernel(
    own,
    second_ref,
    gain_ref,
    live_ref,
    cotangent_ref,
    down_ref,
    gate_low_ref,
    gate_high_ref,
    up_low_ref,
    up_high_ref,
    out_ref,
    grad_second_ref,
    d_gain_ref,
    grads_ref,
    normed_ref,
    turned_ref,
    branch_ref,
    third_ref,
    back_ref,
    d_gate_ref,
    d_up_ref,
    d_down_ref,
    sems,
):
    k, steps = pl.program_id(0), pl.num_programs(0)
    width = second_ref.shape[1]
    rows, stacked = d_down_ref.shape[1:]
    tall = HIDDEN // (rows // own)
    slot = k % 2

    def copies(step):
        at = step % 2
        gate = pl.multiple_of(stacked + step * HIDDEN, 256)
        up = pl.multiple_of(stacked + (steps + step) * HIDDEN, 256)
        first = pl.multiple_of(step * rows, 8)
        return [
            pltpu.make_async_copy(
                d_gate_ref.at[at], grads_ref.at[:, pl.ds(gate, HIDDEN)], sems.at[at, 0]
            ),
            pltpu.make_async_copy(
                d_up_ref.at[at], grads_ref.at[:, pl.ds(up, HIDDEN)], sems.at[at, 1]
            ),
            pltpu.make_async_copy(
                d_down_ref.at[at],
                grads_ref.at[pl.ds(first, rows), pl.ds(0, stacked)],
                sems.at[at, 2],
            ),
        ]

    @pl.when(k == 0)
    def _():
        second = second_ref[...]
        scale = lax.rsqrt(jnp.mean(second * second, axis=1, keepdims=True) + epsilon)
        normed = (second * scale * gain_ref[...]).astype(bf16)
        normed_ref[...] = normed
        turned_ref[...] = normed.T
        branch_ref[...] = (cotangent_ref[...].astype(f32) * live_ref[...]).astype(bf16)
        third_ref[...] = second
        back_ref[...] = jnp.zeros(back_ref.shape, f32)

    @pl.when(k >= 2)
    def _():
        for copy in copies(k - 2):
            copy.wait()

    packed = down_ref[...].astype(f32)
    pieces = []
    for i in range(rows // own):
        for c in range(stacked // width):
            high = min(own, tall - c * own)
            pieces.append(packed[i * own : i * own + high, c * width : (c + 1) * width])
    down = jnp.concatenate(pieces, axis=0).astype(bf16)
    gate_weight = jnp.concatenate([gate_low_ref[...], gate_high_ref[...]], axis=1)
    up_weight = jnp.concatenate([up_low_ref[...], up_high_ref[...]], axis=1)

    normed, branch = normed_ref[...], branch_ref[...]
    gate = dot(normed, gate_weight, NN)
    up = dot(normed, up_weight, NN)
    square = gate * gate
    bent = jnp.tanh(SLOPE * gate * (1.0 + CUBIC * square))
    half = 0.5 * (1.0 + bent)
    active = gate * half
    slope = half + 0.5 * gate * (1.0 - bent * bent) * (SLOPE * (1.0 + 3.0 * CUBIC * square))
    hidden = (active * up).astype(bf16)
    grad_hidden = dot(branch, down, NT)
    grad_gate = (grad_hidden * up * slope).astype(bf16)
    grad_up = (grad_hidden * active).astype(bf16)
    third_ref[...] += dot(hidden, down, NN)
    back_ref[...] += dot(grad_gate, gate_weight, NT) + dot(grad_up, up_weight, NT)
    d_gate_ref[slot] = dot(turned_ref[...], grad_gate, NN).astype(bf16)
    d_up_ref[slot] = dot(turned_ref[...], grad_up, NN).astype(bf16)
    d_down = dot(hidden, branch, TN)
    for i in range(rows // own):
        for c in range(stacked // width):
            high = min(own, tall - c * own)
            part = d_down[i * tall + c * own : i * tall + c * own + high].astype(bf16)
            at = i * own
            d_down_ref[slot, at : at + high, c * width : (c + 1) * width] = part
            if high < own:
                d_down_ref[slot, at + high : at + own, c * width : (c + 1) * width] = jnp.zeros(
                    (own - high, width), bf16
                )
    for copy in copies(k):
        copy.start()

    @pl.when(k == steps - 1)
    def _():
        second, back = second_ref[...], back_ref[...]
        out_ref[...] = (third_ref[...] * live_ref[...]).astype(bf16)
        scale = lax.rsqrt(jnp.mean(second * second, axis=1, keepdims=True) + epsilon)
        d_gain_ref[...] = jnp.sum(back * second * scale, axis=0, keepdims=True)
        back = back * gain_ref[...]
        inner = jnp.mean(back * second, axis=1, keepdims=True)
        back = scale * back - second * (scale * scale * scale * inner)
        grad_second_ref[...] = cotangent_ref[...].astype(f32) * live_ref[...] + back
        for step in (k - 1, k):
            for copy in copies(step):
                copy.wait()


def feed_forward(second, gain, live, cotangent, weights, inner, own):
    slots, width = second.shape
    steps = inner // HIDDEN
    stacked = weights.shape[1] - 2 * inner
    rows = weights.shape[0] // steps
    whole = lambda *shape: pl.BlockSpec(shape, lambda k: (0,) * len(shape))
    unit = HIDDEN // 2
    column = lambda first: pl.BlockSpec((width, unit), lambda k: (0, first + 2 * k))
    at = stacked // unit
    return pl.pallas_call(
        functools.partial(feed_forward_kernel, own),
        out_shape=(
            jax.ShapeDtypeStruct((slots, width), bf16),
            jax.ShapeDtypeStruct((slots, width), f32),
            jax.ShapeDtypeStruct((1, width), f32),
            jax.ShapeDtypeStruct(weights.shape, bf16),
        ),
        grid=(steps,),
        in_specs=[
            whole(slots, width),
            whole(1, width),
            whole(slots, 1),
            whole(slots, width),
            pl.BlockSpec((rows, stacked), lambda k: (k, 0)),
            column(at),
            column(at + 1),
            column(at + 2 * steps),
            column(at + 2 * steps + 1),
        ],
        out_specs=[
            whole(slots, width),
            whole(slots, width),
            whole(1, width),
            pl.BlockSpec(memory_space=pl.ANY),
        ],
        scratch_shapes=[
            pltpu.VMEM((slots, width), bf16),
            pltpu.VMEM((width, slots), bf16),
            pltpu.VMEM((slots, width), bf16),
            pltpu.VMEM((slots, width), f32),
            pltpu.VMEM((slots, width), f32),
            pltpu.VMEM((2, width, HIDDEN), bf16),
            pltpu.VMEM((2, width, HIDDEN), bf16),
            pltpu.VMEM((2, rows, stacked), bf16),
            pltpu.SemaphoreType.DMA((2, 3)),
        ],
        cost_estimate=cost(
            flops=18 * slots * width * inner,
            transcendentals=slots * inner,
            bytes_accessed=4 * weights.size + 16 * slots * width,
        ),
        name="feed_forward",
    )(second, gain.reshape(1, width), live, cotangent, weights, weights, weights, weights, weights)


class Cube:
    def __init__(self, narrow, wide):
        self.narrow, self.wide = narrow, wide
        self.size = narrow * wide
        self.bits = self.size.bit_length() - 1
        self.index = lax.axis_index(BOTH)

    def swap(self, value, mask):
        pairs = [(i, i ^ mask) for i in range(self.size)]
        return lax.ppermute(value, BOTH, pairs)

    def total(self, value, bits):
        for bit in bits:
            value = value + self.swap(value, 1 << bit)
        return value


def merge_four(cube, pieces, split):
    r, n = pieces[0].shape

    def kernel(place_ref, *refs):
        ins, (left_ref, right_ref) = refs[:4], refs[4:]
        for m, ref in enumerate(ins):
            at = place_ref[0] ^ m
            left_ref[at] = ref[:, :split]
            right_ref[at] = ref[:, split:]

    return pl.pallas_call(
        kernel,
        out_shape=(
            jax.ShapeDtypeStruct((4, r, split), bf16),
            jax.ShapeDtypeStruct((4, r, n - split), bf16),
        ),
        grid_spec=pltpu.PrefetchScalarGridSpec(
            num_scalar_prefetch=1,
            grid=(1,),
            in_specs=[pl.BlockSpec((r, n), lambda i, s: (0, 0))] * 4,
            out_specs=[
                pl.BlockSpec((4, r, split), lambda i, s: (0, 0, 0)),
                pl.BlockSpec((4, r, n - split), lambda i, s: (0, 0, 0)),
            ],
        ),
        cost_estimate=cost(flops=0, transcendentals=0, bytes_accessed=16 * r * n),
        name="merge_four",
    )(((cube.index >> 1) & 3).reshape(1), *pieces)


def merge_two(side, mine, come, chunks):
    a, rows, n = mine.shape
    piece = pl.BlockSpec((1, rows, n // chunks), lambda i, c, s: (i, 0, c))

    def kernel(side_ref, mine_ref, come_ref, out_ref):
        out_ref[0, side_ref[0]] = mine_ref[0]
        out_ref[0, 1 - side_ref[0]] = come_ref[0]

    return pl.pallas_call(
        kernel,
        out_shape=jax.ShapeDtypeStruct((a, 2, rows, n), bf16),
        grid_spec=pltpu.PrefetchScalarGridSpec(
            num_scalar_prefetch=1,
            grid=(a, chunks),
            in_specs=[piece, piece],
            out_specs=pl.BlockSpec((1, 2, rows, n // chunks), lambda i, c, s: (i, 0, 0, c)),
        ),
        cost_estimate=cost(
            flops=0, transcendentals=0, bytes_accessed=8 * a * rows * n
        ),
        name="merge_two",
    )(side.reshape(1), mine, come)


class Gather:
    def __init__(self, cube, shard, split):
        self.cube = cube
        pieces = [shard] + [cube.swap(shard, m << 1) for m in (1, 2, 3)]
        self.start = merge_four(cube, pieces, split)

    def half(self, filler):
        cube = self.cube
        one, two = self.start
        r = one.shape[1]
        come_one, come_two = cube.swap(one, 1), cube.swap(two.reshape(1, 4 * r, -1), 16)
        come_one, come_two, filler = tie(come_one, come_two, filler)
        one = merge_two(self.side(0), one, come_one, 1)
        two = merge_two(self.side(4), two.reshape(1, 4 * r, -1), come_two, 1)
        return one.reshape(1, 8 * r, -1), two.reshape(8, r, -1), filler

    def side(self, bit):
        return (self.cube.index >> bit) & 1

    def most(self, one, two):
        cube = self.cube
        r = two.shape[1]
        one = merge_two(self.side(4), one, cube.swap(one, 16), 2 - one.shape[2] // LANES % 2)
        two = merge_two(self.side(0), two, cube.swap(two, 1), 1)
        return [one.reshape(2, 8 * r, -1), two.reshape(2, 8 * r, -1)]

    def finish(self, values):
        core = self.side(3)
        chunks = lambda value: 2 - value.shape[2] // LANES % 2
        return [
            merge_two(core, value, self.cube.swap(value, 8), chunks(value)).reshape(
                -1, value.shape[2]
            )
            for value in values
        ]


class Scatter:
    def __init__(self, cube, grads):
        self.cube = cube
        self.shapes = [(grad.shape[0] // cube.size, grad.shape[1]) for grad in grads]
        self.own = self.shapes[0][0]
        self.flat = [i for i, (r, _) in enumerate(self.shapes) if r == self.own]
        self.tall = [i for i, (r, _) in enumerate(self.shapes) if r != self.own]
        self.grads = [
            grad.reshape(2, 2, cube.wide * r, n)
            for grad, (r, n) in zip(grads, self.shapes, strict=True)
        ]
        self.sides = jnp.stack([cube.index >> 4, (cube.index >> 3) & 1, cube.index & 1])
        self.groups = [(self.own, sum(self.shapes[i][1] for i in self.flat))]
        self.groups += [self.shapes[i] for i in self.tall]

    def message(self, come, own, places, lead=1, packed=0):
        wide = self.cube.wide
        split = 2
        n_grads, n_groups = len(self.grads), len(self.groups)
        n_ins = n_grads + len(come)
        widths = [n for _, n in self.groups]
        stack = [-(-r // self.own) for r, _ in self.groups]

        def kernel(sides_ref, *refs):
            ins, outs = refs[:n_ins], refs[n_ins:]
            flat = [ins[i][0, 0] for i in self.flat]
            values = [flat[0] if len(flat) == 1 else jnp.concatenate(flat, axis=1)]
            values += [ins[i][0, 0] for i in self.tall]
            for k, ref in enumerate(ins[n_grads:]):
                got = ref[...]
                got = got.reshape(got.shape[-2:])
                i = k % n_groups
                values[i] = values[i].astype(f32) + got.astype(f32)
            if not packed:
                for out_ref, value in zip(outs, values, strict=True):
                    out_ref[...] = value.astype(bf16).reshape(out_ref.shape)
                return
            at = 0
            for value, (r, n), high in zip(values, self.groups, stack, strict=True):
                value = value.astype(f32).reshape(wide // split, r, n)
                for c in range(high):
                    part = value[:, c * self.own : (c + 1) * self.own].astype(bf16)
                    if packed == 1:
                        outs[0][:, : part.shape[1], at : at + n] = part
                    else:
                        side = sides_ref[2]
                        for i in range(0, part.shape[0], 2):
                            for flip, out_ref in enumerate(outs):
                                out_ref[i // 2, : part.shape[1], at : at + n] = jnp.where(
                                    side == flip, part[i], part[i + 1]
                                )
                    at += n

        in_specs = [
            pl.BlockSpec((1, 1, wide * r // split, n), lambda i, j, s: (*own(i, s), j, 0))
            for r, n in self.shapes
        ]
        for k, value in enumerate(come):
            at = places[k // n_groups]
            r, n = self.groups[k % n_groups]
            in_specs.append(
                pl.BlockSpec(
                    (1,) * (value.ndim - 2) + (wide * r // split, n),
                    lambda i, j, s, at=at: (*at(s), j, 0),
                )
            )
        if packed:
            n = sum(w * high for w, high in zip(widths, stack, strict=True))
            high = wide // packed
            out_shape = [jax.ShapeDtypeStruct((high, self.own, n), bf16)] * packed
            out_specs = [
                pl.BlockSpec((high // split, self.own, n), lambda i, j, s: (j, 0, 0))
            ] * packed
        else:
            out_shape = [jax.ShapeDtypeStruct((lead, wide * r, n), bf16) for r, n in self.groups]
            out_specs = [
                pl.BlockSpec((1, wide * r // split, n), lambda i, j, s: (i, j, 0))
                for r, n in self.groups
            ]
        size = sum(int(np.prod(out.shape)) for out in out_shape)
        return pl.pallas_call(
            kernel,
            out_shape=out_shape,
            grid_spec=pltpu.PrefetchScalarGridSpec(
                num_scalar_prefetch=1,
                grid=(lead, split),
                in_specs=in_specs,
                out_specs=out_specs,
            ),
            cost_estimate=cost(
                flops=size, transcendentals=0, bytes_accessed=4 * size
            ),
            name="message",
        )(self.sides, *self.grads, *come)

    def swap(self, values, mask):
        return [self.cube.swap(value, mask) for value in values]

    def to_core(self):
        return self.message([], lambda i, s: (i, 1 - s[1]), [], lead=2)

    def to_x(self, one):
        return self.message(one, lambda i, s: (1 - s[0], s[1]), [lambda s: (1 - s[0],)])

    def to_wide(self, one, two, halved=False):
        places = [lambda s: (s[0],), lambda s: (0,)]
        return self.message(
            [*one, *two], lambda i, s: (s[0], s[1]), places, packed=1 + halved
        )

    def step(self, bit, mine, come):
        blocks, r, n = mine.shape

        def kernel(side_ref, *refs):
            keep_ref, send_ref = refs[-2:]
            side = side_ref[0]
            for i in range(blocks // 2):
                for out_ref, at in ((keep_ref, 2 * i + side), (send_ref, 2 * i + 1 - side)):
                    value = refs[0][at].astype(f32) + refs[1][at].astype(f32)
                    out_ref[i] = value.astype(bf16)

        whole = pl.BlockSpec(mine.shape, lambda i, s: (0, 0, 0))
        half = pl.BlockSpec((blocks // 2, r, n), lambda i, s: (0, 0, 0))
        return pl.pallas_call(
            kernel,
            out_shape=[jax.ShapeDtypeStruct((blocks // 2, r, n), bf16)] * 2,
            grid_spec=pltpu.PrefetchScalarGridSpec(
                num_scalar_prefetch=1,
                grid=(1,),
                in_specs=[whole, whole],
                out_specs=[half, half],
            ),
            cost_estimate=cost(
                flops=mine.size, transcendentals=0, bytes_accessed=6 * mine.size
            ),
            name="step",
        )(((self.cube.index >> bit) & 1).reshape(1), mine, come)

    def finish(self, *come):
        def kernel(*refs):
            ins, outs = refs[: len(come)], refs[len(come) :]
            blocks = [ref[i] for ref in ins for i in range(ref.shape[0])]
            value = blocks[0].astype(f32)
            for block in blocks[1:]:
                value = value + block.astype(f32)
            at = 0
            for i in self.flat:
                n = self.shapes[i][1]
                outs[i][...] = value[:, at : at + n]
                at += n
            for i in self.tall:
                r, n = self.shapes[i]
                for c in range(0, r, self.own):
                    high = min(self.own, r - c)
                    outs[i][c : c + high] = value[:high, at : at + n]
                    at += n

        size = sum(value.size for value in come)
        return pl.pallas_call(
            kernel,
            out_shape=tuple(jax.ShapeDtypeStruct(shape, f32) for shape in self.shapes),
            cost_estimate=cost(
                flops=size, transcendentals=0, bytes_accessed=4 * size
            ),
            name="finish",
        )(*come)


def tie(*values):
    return lax.optimization_barrier(values)


def pack_shards(parts, widths, rows):
    flat = [part for group in parts for part in group]

    def kernel(*refs):
        ins, outs = refs[: len(flat)], refs[len(flat) :]
        refs_of = iter(ins)
        for out_ref, group in zip(outs, parts, strict=True):
            at = 0
            for array, start, count in group:
                ref, n = next(refs_of), array.shape[1]
                out_ref[:count, at : at + n] = ref[start : start + count, :]
                if count < rows:
                    out_ref[count:, at : at + n] = jnp.zeros((rows - count, n), bf16)
                at += n

    return pl.pallas_call(
        kernel,
        out_shape=tuple(jax.ShapeDtypeStruct((rows, n), bf16) for n in widths),
        name="pack",
    )(*[part[0] for part in flat])


def rms_norm(value, gain):
    return value * lax.rsqrt(jnp.mean(value * value, axis=-1, keepdims=True) + epsilon) * gain


def gelu_tanh(value):
    return jax.nn.gelu(value, approximate=True)


def on_device(
    targets,
    memory,
    cotangent,
    target_len,
    memory_len,
    self_query,
    self_key,
    self_value,
    self_out,
    cross_query,
    cross_key,
    cross_value,
    cross_out,
    ff_gate,
    ff_up,
    ff_down,
    self_gain,
    cross_gain,
    ff_gain,
    position_bias,
    narrow,
    wide,
):
    cube = Cube(narrow, wide)
    pairs, length, width = targets.shape
    slots = pairs * length
    own, own_ff = self_query.shape[0], ff_down.shape[0]
    inner = ff_gate.shape[1]
    devices = cube.size
    stepped = narrow == 4 and wide == 8 and own % 8 == 0

    gains = jnp.stack([self_gain, cross_gain, ff_gain], axis=1)
    gains = jnp.pad(gains, ((0, 0), (0, LANES - 3)))
    stack = -(-own_ff // own)
    whole = lambda *arrays: [(array, 0, own) for array in arrays]
    self_shard, cross_shard, ff_shard = pack_shards(
        [
            whole(self_query, self_key, self_value, self_out, gains),
            whole(cross_query, cross_key, cross_value, cross_out),
            [(ff_down, c * own, min(own, own_ff - c * own)) for c in range(stack)]
            + whole(ff_gate, ff_up),
        ],
        [4 * width + LANES, 4 * width, 2 * inner + stack * width],
        own,
    )
    places = jnp.arange(length)
    apart = places[:, None] - places[None, :]
    bucket = bucket_of_distance(length, BUCKETS, REACH)
    starts = [int(np.argmax(bucket >= b)) for b in range(1, int(bucket[-1]) + 1)]
    bucket_matrix = sum((apart >= start).astype(jnp.int32) for start in starts)
    onehot = (bucket_matrix[:, :, None] == jnp.arange(BUCKETS)[None, None, :]).astype(bf16)
    bias = jnp.einsum("ijb,bh->hij", onehot, position_bias, preferred_element_type=f32)
    bias = jnp.where((apart >= 0)[None], bias, negative).astype(bf16)

    exchange = lambda value: lax.all_to_all(
        value, "wide", split_axis=0, concat_axis=0, tiled=True
    )
    gathered = lax.all_gather(self_shard, BOTH, axis=0, tiled=True)
    ff = lax.all_gather(ff_shard, BOTH, axis=0, tiled=True)
    if stepped:
        cross_gather = Gather(cube, cross_shard, 2 * width)
        one, two, bias = cross_gather.half(bias)
        most = cross_gather.most(one, two)
        memory, most[0] = tie(memory, most[0])
        gathered, *most = tie(gathered, *most)
        c_query_key, c_value_out = cross_gather.finish(most)
    else:
        cross = lax.all_gather(cross_shard, BOTH, axis=0, tiled=True)
        c_query_key, c_value_out = cross[:, : 2 * width], cross[:, 2 * width :]
    memory_rows = exchange(memory).reshape(wide, pairs, -1, width)
    w_qkv, s_out = gathered[:, : 3 * width], gathered[:, 3 * width : 4 * width]
    c_query, c_out = c_query_key[:, :width], c_value_out[:, width:]

    gains = gathered[:, 4 * width : 4 * width + 3].astype(f32).T
    gain_one, gain_two, gain_three = gains[0], gains[1], gains[2]
    live = (places[None, :] < target_len[:, None]).astype(f32).reshape(slots, 1)
    inputs = targets.astype(f32).reshape(slots, width)

    normed_one = rms_norm(inputs, gain_one).astype(bf16)
    cube_of = lambda value: value.reshape(pairs, length, -1)
    qkv_one = cube_of(dot(normed_one, w_qkv, NN).astype(bf16))
    mixed_one, total_one = self_forward(qkv_one, bias)
    mixed_one = mixed_one.reshape(slots, width)
    first = inputs + dot(mixed_one, s_out, NN)
    normed_two = rms_norm(first, gain_two).astype(bf16)
    query_two = cube_of(dot(normed_two, c_query, NN).astype(bf16))
    held = ()
    for p in range(pairs):
        held = cross_forward(
            p, query_two, memory_rows, c_query_key, c_value_out, memory_len, held
        )
    mixed_two, total_two, key_two, value_two = held
    mixed_two = mixed_two.reshape(slots, width)
    second = first + dot(mixed_two, c_out, NN)

    stacked = stack * width
    if stepped:
        layer_out, grad_second, d_gain_three, ff_grads = feed_forward(
            second, gain_three, live, cotangent.reshape(slots, width), ff, inner, own
        )
        d_gain_three = d_gain_three.reshape(width)
    else:
        f_gate, f_up = ff[:, stacked : stacked + inner], ff[:, stacked + inner :]
        f_down = ff[:, :stacked].reshape(devices, own, stack, width).swapaxes(1, 2)
        f_down = f_down.reshape(devices, -1, width)[:, :own_ff].reshape(inner, width)
        normed_three = rms_norm(second, gain_three).astype(bf16)
        gate = dot(normed_three, f_gate, NN)
        upward = dot(normed_three, f_up, NN)
        activated, gelu_pull = jax.vjp(gelu_tanh, gate)
        hidden = (activated * upward).astype(bf16)
        third = second + dot(hidden, f_down, NN)
        layer_out = (third * live).astype(bf16)
        grad_third = cotangent.astype(f32).reshape(slots, width) * live
        branch_ff = grad_third.astype(bf16)
        d_down = dot(hidden, branch_ff, TN).astype(bf16)
        grad_hidden = dot(branch_ff, f_down, NT)
        grad_gate = gelu_pull(grad_hidden * upward)[0].astype(bf16)
        grad_up = (grad_hidden * activated).astype(bf16)
        d_gate = dot(normed_three, grad_gate, TN).astype(bf16)
        d_up = dot(normed_three, grad_up, TN).astype(bf16)
        grad_normed_three = dot(grad_gate, f_gate, NT) + dot(grad_up, f_up, NT)
        d_down = d_down.reshape(devices, own_ff, width)
        d_down = jnp.pad(d_down, ((0, 0), (0, stack * own - own_ff), (0, 0)))
        d_down = d_down.reshape(devices, stack, own, width).swapaxes(1, 2)
        d_down = d_down.reshape(devices * own, stacked)
        ff_grads = jnp.concatenate([d_down, d_gate, d_up], axis=1)
        _, norm_three = jax.vjp(rms_norm, second, gain_three)
        back_three, d_gain_three = norm_three(grad_normed_three)
        grad_second = grad_third + back_three
    layer_out = layer_out.reshape(pairs, length, width)
    ff_grads = lax.psum_scatter(ff_grads, BOTH, scatter_dimension=0, tiled=True)

    branch_cross = grad_second.astype(bf16)
    d_cross_out = dot(mixed_two, branch_cross, TN).astype(bf16)
    grad_mixed_two = cube_of(dot(branch_cross, c_out, NT).astype(bf16))
    held = ()
    for p in range(pairs):
        grad_query_two, rows_grad, *found = cross_backward(
            p,
            query_two,
            key_two,
            value_two,
            memory_len,
            total_two,
            grad_mixed_two,
            memory_rows,
            c_query_key,
            c_value_out,
            held,
        )
        held = (*held[:-2], *found, grad_query_two, rows_grad)
    d_cross_key, d_cross_value = found
    grad_memory = exchange(rows_grad.reshape(memory.shape))
    grad_query_two = grad_query_two.reshape(slots, width)
    d_cross_query = dot(normed_two, grad_query_two, TN).astype(bf16)
    _, norm_two = jax.vjp(rms_norm, first, gain_two)
    back_two, d_gain_two = norm_two(dot(grad_query_two, c_query, NT))
    grad_first = grad_second + back_two

    branch_self = grad_first.astype(bf16)
    d_self_out = dot(mixed_one, branch_self, TN).astype(bf16)
    grad_mixed_one = cube_of(dot(branch_self, s_out, NT).astype(bf16))
    middle = [d_cross_query, d_cross_key, d_cross_value, d_cross_out, d_self_out]
    if stepped:
        middle_sum = Scatter(cube, middle)
        middle_one = middle_sum.swap(middle_sum.to_core(), 8)
        middle_send = middle_sum.to_x(middle_one)
        grad_mixed_one, *middle_send = tie(grad_mixed_one, *middle_send)
        middle_two = middle_sum.swap(middle_send, 16)
    grads_one, diagonals = self_backward(qkv_one, bias, total_one, grad_mixed_one)
    grads_one = grads_one.reshape(slots, 3 * width)
    d_qkv = dot(normed_one, grads_one, TN).astype(bf16)
    if stepped:
        last_sum = Scatter(cube, [d_qkv])
        last_send = last_sum.to_core()
        grads_one, diagonals, *tied = tie(grads_one, diagonals, *middle_two, *last_send)
        middle_two, last_send = tied[: len(middle_two)], tied[len(middle_two) :]
        last_one = last_sum.swap(last_send, 8)
        middle_keep, middle_send = middle_sum.to_wide(middle_one, middle_two, halved=True)
        grads_one, middle_send = tie(grads_one, middle_send)
        middle_come = cube.swap(middle_send, 1)
    grad_normed_one = dot(grads_one, w_qkv, NT)
    _, norm_one = jax.vjp(rms_norm, inputs, gain_one)
    back_one, d_gain_one = norm_one(grad_normed_one)
    if stepped:
        last_one[0], d_gain_one = tie(last_one[0], d_gain_one)
        last_send = last_sum.to_x(last_one)
        last_two = last_sum.swap(last_send, 16)
    grad_targets = (grad_first + back_one).reshape(pairs, length, width)
    if stepped:
        last_two[0], middle_come, grad_memory, grad_targets = tie(
            last_two[0], middle_come, grad_memory, grad_targets
        )
        middle_keep, middle_send = middle_sum.step(1, middle_keep, middle_come)
        middle_come = cube.swap(middle_send, 2)

    padded = diagonals.shape[-1]
    column = (padded - np.arange(length)) % padded
    to_bucket = np.zeros((padded, BUCKETS), np.float32)
    to_bucket[column, bucket] = 1.0
    diagonals = jnp.sum(diagonals, axis=2).reshape(HEADS, padded)
    d_position = jnp.einsum(
        "hc,cb->bh", diagonals, jnp.asarray(to_bucket), precision=lax.Precision.HIGHEST
    )
    small = jnp.concatenate(
        [d_gain_one, d_gain_two, d_gain_three, d_position.reshape(-1)]
    ).reshape(-1, LANES)
    small = jnp.pad(small, ((0, -small.shape[0] % 8), (0, 0)))
    near = range(wide.bit_length() - 1, cube.bits)
    far = range(wide.bit_length() - 1)
    small = cube.total(small, near)
    if stepped:
        last_two[0], small = tie(last_two[0], small)
        last_keep, last_send = last_sum.to_wide(last_one, last_two, halved=True)
        last_come = cube.swap(last_send, 1)
        middle_keep, middle_send = middle_sum.step(2, middle_keep, middle_come)
        middle_come = cube.swap(middle_send, 4)
        last_keep, last_send = last_sum.step(1, last_keep, last_come)
        last_come = cube.swap(last_send, 2)
        middle_grads = middle_sum.finish(middle_keep, middle_come)
        last_keep, last_send = last_sum.step(2, last_keep, last_come)
        last_come = cube.swap(last_send, 4)
        last_come, ff_grads = tie(last_come, ff_grads)
        (d_qkv,) = last_sum.finish(last_keep, last_come)
    else:
        scatter = lambda value: lax.psum_scatter(
            value, BOTH, scatter_dimension=0, tiled=True
        ).astype(f32)
        middle_grads = [scatter(value) for value in middle]
        d_qkv = scatter(d_qkv)
    small = cube.total(small, far).reshape(-1)
    gain_grads = small[: 3 * width].reshape(3, devices, width // devices)
    gain_grads = lax.dynamic_index_in_dim(gain_grads, cube.index, 1, keepdims=False)
    grad_position = small[3 * width : 3 * width + BUCKETS * HEADS].reshape(BUCKETS, HEADS)

    ff_grads = ff_grads.astype(f32)
    d_down = jnp.concatenate(
        [ff_grads[:, c * width : (c + 1) * width] for c in range(stack)], axis=0
    )[:own_ff]
    return (
        layer_out,
        grad_targets,
        grad_memory.astype(f32),
        d_qkv[:, :width],
        d_qkv[:, width : 2 * width],
        d_qkv[:, 2 * width :],
        middle_grads[4],
        *middle_grads[:4],
        ff_grads[:, stacked : stacked + inner],
        ff_grads[:, stacked + inner :],
        d_down,
        gain_grads[0],
        gain_grads[1],
        gain_grads[2],
        grad_position,
    )


def solution(mesh):
    rows = P(BOTH, None)
    slots = P(BOTH, None, None)
    one = P(BOTH)
    source = P("narrow", "wide", None)
    in_specs = (slots, source, slots, one, one) + (rows,) * 11 + (one,) * 3 + (P(),)
    out_specs = (slots, slots, source) + (rows,) * 11 + (one,) * 3 + (P(),)
    narrow, wide = mesh.shape["narrow"], mesh.shape["wide"]

    def body(*args):
        return on_device(*args, narrow=narrow, wide=wide)

    return jax.shard_map(body, mesh=mesh, in_specs=in_specs, out_specs=out_specs, check_vma=False)
```

```python
import functools

import jax
import jax.numpy as jnp
import numpy as np
from jax import lax
from jax.experimental import pallas as pl
from jax.experimental.pallas import tpu as pltpu
from jax.sharding import PartitionSpec as P

HEADS = 12
HEAD_DIM = 64
BUCKETS = 32
REACH = 128
LANES = 128
BOTH = ("narrow", "wide")
SHARE = 8

negative = -1e30
epsilon = 1e-06
bf16 = jnp.bfloat16
f32 = jnp.float32

NT = (((1,), (1,)), ((), ()))
NN = (((1,), (0,)), ((), ()))
TN = (((0,), (0,)), ((), ()))


def cost(flops=0, transcendentals=0, bytes_accessed=0):
    return pl.CostEstimate(
        flops=flops // SHARE,
        transcendentals=transcendentals // SHARE,
        bytes_accessed=bytes_accessed // SHARE,
    )


def dot(left, right, dims):
    return lax.dot_general(left, right, dims, preferred_element_type=f32)


def bucket_of_distance(length, buckets, reach):
    apart = np.arange(length)
    exact = buckets // 2
    safe = np.maximum(apart, 1)
    far = exact + (np.log(safe / exact) / np.log(reach / exact) * (buckets - exact)).astype(
        np.int64
    )
    far = np.minimum(far, buckets - 1)
    return np.where(apart < exact, apart, far).astype(np.int32)


def stack_heads(value):
    first = lax.broadcasted_iota(jnp.int32, value.shape, 1) < HEAD_DIM
    zero = jnp.zeros_like(value)
    return jnp.concatenate([jnp.where(first, value, zero), jnp.where(first, zero, value)], axis=0)


def join_heads(value):
    half = value.shape[0] // 2
    first = lax.broadcasted_iota(jnp.int32, (half, value.shape[1]), 1) < HEAD_DIM
    return jnp.where(first, value[:half], value[half:])


def stack_columns(total):
    return jnp.concatenate([total[:, :1], total[:, HEAD_DIM : HEAD_DIM + 1]], axis=0)


def attend(scores, v, mixed_ref, total_ref, pair=0):
    top = jnp.max(scores, axis=1, keepdims=True)
    grown = jnp.exp(scores - top)
    total = jnp.sum(grown, axis=1, keepdims=True)
    mixed = dot(grown.astype(bf16), v, NN) * (1.0 / total)
    mixed_ref[pair] = join_heads(mixed).astype(bf16)
    total_ref[pair] = join_heads(jnp.broadcast_to(top + jnp.log(total), mixed.shape))


def attend_back(scores, total, grad, v):
    probs = jnp.exp(scores - stack_columns(total))
    grad_probs = dot(grad, v, NT)
    inner = jnp.sum(probs * grad_probs, axis=1, keepdims=True)
    return probs.astype(bf16), (probs * (grad_probs - inner)).astype(bf16)


def self_forward_kernel(q_ref, k_ref, v_ref, bias_ref, mixed_ref, total_ref):
    pairs, length, _ = q_ref.shape
    bias = bias_ref[...].reshape(2 * length, length).astype(f32)
    for p in range(pairs):
        scores = dot(stack_heads(q_ref[p]), k_ref[p], NT) + bias
        attend(scores, v_ref[p], mixed_ref, total_ref, p)


def self_forward(qkv, bias):
    pairs, length, width = qkv.shape
    width //= 3
    steps = width // LANES
    part = lambda c: pl.BlockSpec((pairs, length, LANES), lambda h: (0, 0, h + c * steps))
    return pl.pallas_call(
        self_forward_kernel,
        out_shape=(
            jax.ShapeDtypeStruct((pairs, length, width), bf16),
            jax.ShapeDtypeStruct((pairs, length, width), f32),
        ),
        grid=(steps,),
        in_specs=[
            part(0),
            part(1),
            part(2),
            pl.BlockSpec((2, length, length), lambda h: (h, 0, 0)),
        ],
        out_specs=[part(0), part(0)],
        cost_estimate=cost(
            flops=pairs * HEADS * length * length * HEAD_DIM * 4,
            transcendentals=pairs * HEADS * length * length,
            bytes_accessed=pairs * length * width * 12,
        ),
        name="self_forward",
    )(qkv, qkv, qkv, bias)


def self_backward_kernel(
    q_ref, k_ref, v_ref, bias_ref, total_ref, grad_ref, grads_ref, diagonal_ref, sum_ref
):
    hp, steps = pl.program_id(0), pl.num_programs(0)
    pairs, length, _ = q_ref.shape
    padded = sum_ref.shape[-1]
    bias = bias_ref[...].reshape(2 * length, length).astype(f32)

    @pl.when(hp == 0)
    def _():
        sum_ref[...] = jnp.zeros(sum_ref.shape, f32)

    summed = 0.0
    for p in range(pairs):
        q, grad, k = stack_heads(q_ref[p]), stack_heads(grad_ref[p]), k_ref[p]
        scores = dot(q, k, NT) + bias
        probs, grad_scores = attend_back(scores, total_ref[p], grad, v_ref[p])
        summed = summed + grad_scores.astype(f32)
        found = join_heads(dot(grad_scores, k, NN)), dot(grad_scores, q, TN), dot(probs, grad, TN)
        for c in range(3):
            at = pl.ds(pl.multiple_of((hp + c * steps) * LANES, LANES), LANES)
            grads_ref[p, :, at] = found[c].astype(bf16)
    sum_ref[:, :, :length] = summed.reshape(2, length, length)

    rows = lax.broadcasted_iota(jnp.int32, (8, padded), 0)
    for h in range(2):
        held = sum_ref[h, 0:8, :]
        for i in range(8, length, 8):
            held = held + pltpu.roll(sum_ref[h, i : i + 8, :], padded - i, 1)
        for bit in (1, 2, 4):
            held = jnp.where((rows // bit) % 2 == 1, pltpu.roll(held, padded - bit, 1), held)
        diagonal_ref[0, h] = held


def self_backward(qkv, bias, total, grad):
    pairs, length, width = qkv.shape
    width //= 3
    steps = width // LANES
    padded = -(-length // LANES) * LANES
    part = lambda c: pl.BlockSpec((pairs, length, LANES), lambda h: (0, 0, h + c * steps))
    return pl.pallas_call(
        self_backward_kernel,
        out_shape=(
            jax.ShapeDtypeStruct(qkv.shape, bf16),
            jax.ShapeDtypeStruct((steps, 2, 8, padded), f32),
        ),
        grid=(steps,),
        in_specs=[
            part(0),
            part(1),
            part(2),
            pl.BlockSpec((2, length, length), lambda h: (h, 0, 0)),
            part(0),
            part(0),
        ],
        out_specs=[
            pl.BlockSpec((pairs, length, 3 * width), lambda h: (0, 0, 0)),
            pl.BlockSpec((1, 2, 8, padded), lambda h: (h, 0, 0, 0)),
        ],
        scratch_shapes=[pltpu.VMEM((2, length, padded), f32)],
        cost_estimate=cost(
            flops=pairs * HEADS * length * length * HEAD_DIM * 10,
            transcendentals=pairs * HEADS * length * length,
            bytes_accessed=pairs * length * width * 18,
        ),
        name="self_backward",
    )(qkv, qkv, qkv, bias, total, grad)


def dead_rows(live_rows, rows):
    places = lax.broadcasted_iota(jnp.int32, (1, rows), 1)
    return jnp.where(places < live_rows, 0.0, negative)


def cross_forward_kernel(pair, len_ref, q_ref, memory_ref, wk_ref, wv_ref, *refs):
    mixed_ref, total_ref, k_ref, v_ref = refs[-4:]
    rows = k_ref.shape[1]
    memory = memory_ref[...].reshape(rows, -1)
    kv = dot(memory, jnp.concatenate([wk_ref[...], wv_ref[...]], axis=1), NN).astype(bf16)
    k, v = kv[:, :LANES], kv[:, LANES:]
    k_ref[0], v_ref[0] = k, v
    scores = dot(stack_heads(q_ref[0]), k, NT) + dead_rows(len_ref[pair], rows)
    attend(scores, v, mixed_ref, total_ref)


def cross_forward(pair, query, memory, query_key, value_out, lens, before):
    pairs, length, width = query.shape
    sources, _, part, _ = memory.shape
    rows = sources * part
    steps = width // LANES
    target = pl.BlockSpec((1, length, LANES), lambda h, n: (pair, 0, h))
    source = pl.BlockSpec((1, rows, LANES), lambda h, n: (pair, 0, h))
    weight = lambda c: pl.BlockSpec((width, LANES), lambda h, n: (0, h + c * steps))
    return pl.pallas_call(
        functools.partial(cross_forward_kernel, pair),
        out_shape=(
            jax.ShapeDtypeStruct(query.shape, bf16),
            jax.ShapeDtypeStruct(query.shape, f32),
            jax.ShapeDtypeStruct((pairs, rows, width), bf16),
            jax.ShapeDtypeStruct((pairs, rows, width), bf16),
        ),
        grid_spec=pltpu.PrefetchScalarGridSpec(
            num_scalar_prefetch=1,
            grid=(steps,),
            in_specs=[
                target,
                pl.BlockSpec((sources, 1, part, width), lambda h, n: (0, pair, 0, 0)),
                weight(1),
                weight(0),
            ]
            + [pl.BlockSpec(memory_space=pl.ANY)] * len(before),
            out_specs=[target, target, source, source],
        ),
        input_output_aliases={5 + i: i for i in range(len(before))},
        cost_estimate=cost(
            flops=rows * width * (length * 4 + width * 4),
            transcendentals=HEADS * length * rows,
            bytes_accessed=length * width * 8 + rows * width * 6,
        ),
        name="cross_forward",
    )(lens, query, memory, query_key, value_out, *before)


def cross_backward_kernel(
    pair, last, len_ref, q_ref, k_ref, v_ref, total_ref, grad_ref, memory_ref, qk_ref, vo_ref, *refs
):
    *refs, grads_ref, held_ref, weight_ref, sems = refs
    hp, steps = pl.program_id(0), pl.num_programs(0)
    rows, width = k_ref.shape[1], weight_ref.shape[0]
    before = pair if last else 0
    before_refs, refs = refs[:before], refs[pair + 2 * (pair > 0) :]
    grad_query_ref, grad_memory_ref, *outs = refs

    moves = [
        (qk_ref.at[:, width:], weight_ref.at[:, :width]),
        (vo_ref.at[:, :width], weight_ref.at[:, width:]),
    ]
    if last:
        moves += [(memory_ref.at[:, p], held_ref.at[p]) for p in range(pair + 1)]
        moves += [(ref, grads_ref.at[p]) for p, ref in enumerate(before_refs)]
    copies = [pltpu.make_async_copy(*move, sems.at[i]) for i, move in enumerate(moves)]

    @pl.when(hp == 0)
    def _():
        for copy in copies:
            copy.start()

    q, grad, k = stack_heads(q_ref[0]), stack_heads(grad_ref[0]), k_ref[0]
    scores = dot(q, k, NT) + dead_rows(len_ref[pair], rows)
    probs, grad_scores = attend_back(scores, total_ref[0], grad, v_ref[0])
    grad_query_ref[0] = join_heads(dot(grad_scores, k, NN)).astype(bf16)
    for c, value in enumerate((dot(grad_scores, q, TN), dot(probs, grad, TN))):
        at = pl.ds(pl.multiple_of((hp + c * steps) * LANES, LANES), LANES)
        grads_ref[before, :, at] = value.astype(bf16)

    @pl.when(hp == steps - 1)
    def _():
        for copy in copies:
            copy.wait()
        back = dot(grads_ref[before], weight_ref[...], NT).astype(bf16)
        grad_memory_ref[...] = back.reshape(grad_memory_ref.shape)
        if last:
            d_kv = sum(
                dot(held_ref[p].reshape(rows, width), grads_ref[p], TN) for p in range(pair + 1)
            )
            outs[0][...] = d_kv[:, :width].astype(bf16)
            outs[1][...] = d_kv[:, width:].astype(bf16)
        else:
            outs[0][...] = grads_ref[0]


def cross_backward(
    pair, query, key, value, lens, total, grad, memory, query_key, value_out, before
):
    pairs, length, width = query.shape
    sources, _, part, _ = memory.shape
    rows = sources * part
    steps = width // LANES
    last = pair == pairs - 1
    held = pairs if last else 1
    target = pl.BlockSpec((1, length, LANES), lambda h, n: (pair, 0, h))
    source = pl.BlockSpec((1, rows, LANES), lambda h, n: (pair, 0, h))
    anywhere = pl.BlockSpec(memory_space=pl.ANY)
    whole = lambda *shape: pl.BlockSpec(shape, lambda h, n: (0,) * len(shape))
    out_shape = [
        jax.ShapeDtypeStruct(query.shape, bf16),
        jax.ShapeDtypeStruct(memory.shape, bf16),
    ]
    given = pl.BlockSpec((sources, 1, part, width), lambda h, n: (0, pair, 0, 0))
    if last:
        out_shape += [jax.ShapeDtypeStruct((width, width), bf16)] * 2
    else:
        out_shape += [jax.ShapeDtypeStruct((rows, 2 * width), bf16)]
    return pl.pallas_call(
        functools.partial(cross_backward_kernel, pair, last),
        out_shape=out_shape,
        grid_spec=pltpu.PrefetchScalarGridSpec(
            num_scalar_prefetch=1,
            grid=(steps,),
            in_specs=[target, source, source, target, target] + [anywhere] * (3 + len(before)),
            out_specs=[target, given] + [whole(*out.shape) for out in out_shape[2:]],
            scratch_shapes=[
                pltpu.VMEM((held, rows, 2 * width), bf16),
                pltpu.VMEM((held, sources, part, width), bf16),
                pltpu.VMEM((width, 2 * width), bf16),
                pltpu.SemaphoreType.DMA((2 + 2 * pairs,)),
            ],
        ),
        input_output_aliases={7 + len(before): 0, 8 + len(before): 1} if pair else {},
        cost_estimate=cost(
            flops=rows * width * (length * 10 + width * 8),
            transcendentals=HEADS * length * rows,
            bytes_accessed=length * width * 10 + rows * width * 8,
        ),
        name="cross_backward",
    )(lens, query, key, value, total, grad, memory, query_key, value_out, *before)


HIDDEN = 512
SLOPE = float(np.sqrt(2 / np.pi))
CUBIC = 0.044715


def feed_forward_kernel(
    own,
    second_ref,
    gain_ref,
    live_ref,
    cotangent_ref,
    down_ref,
    gate_low_ref,
    gate_high_ref,
    up_low_ref,
    up_high_ref,
    out_ref,
    grad_second_ref,
    d_gain_ref,
    grads_ref,
    normed_ref,
    turned_ref,
    branch_ref,
    third_ref,
    back_ref,
    d_gate_ref,
    d_up_ref,
    d_down_ref,
    sems,
):
    k, steps = pl.program_id(0), pl.num_programs(0)
    width = second_ref.shape[1]
    rows, stacked = d_down_ref.shape[1:]
    tall = HIDDEN // (rows // own)
    slot = k % 2

    def copies(step):
        at = step % 2
        gate = pl.multiple_of(stacked + step * HIDDEN, 256)
        up = pl.multiple_of(stacked + (steps + step) * HIDDEN, 256)
        first = pl.multiple_of(step * rows, 8)
        return [
            pltpu.make_async_copy(
                d_gate_ref.at[at], grads_ref.at[:, pl.ds(gate, HIDDEN)], sems.at[at, 0]
            ),
            pltpu.make_async_copy(
                d_up_ref.at[at], grads_ref.at[:, pl.ds(up, HIDDEN)], sems.at[at, 1]
            ),
            pltpu.make_async_copy(
                d_down_ref.at[at],
                grads_ref.at[pl.ds(first, rows), pl.ds(0, stacked)],
                sems.at[at, 2],
            ),
        ]

    @pl.when(k == 0)
    def _():
        second = second_ref[...]
        scale = lax.rsqrt(jnp.mean(second * second, axis=1, keepdims=True) + epsilon)
        normed = (second * scale * gain_ref[...]).astype(bf16)
        normed_ref[...] = normed
        turned_ref[...] = normed.T
        branch_ref[...] = (cotangent_ref[...].astype(f32) * live_ref[...]).astype(bf16)
        third_ref[...] = second
        back_ref[...] = jnp.zeros(back_ref.shape, f32)

    @pl.when(k >= 2)
    def _():
        for copy in copies(k - 2):
            copy.wait()

    packed = down_ref[...].astype(f32)
    pieces = []
    for i in range(rows // own):
        for c in range(stacked // width):
            high = min(own, tall - c * own)
            pieces.append(packed[i * own : i * own + high, c * width : (c + 1) * width])
    down = jnp.concatenate(pieces, axis=0).astype(bf16)
    gate_weight = jnp.concatenate([gate_low_ref[...], gate_high_ref[...]], axis=1)
    up_weight = jnp.concatenate([up_low_ref[...], up_high_ref[...]], axis=1)

    normed, branch = normed_ref[...], branch_ref[...]
    gate = dot(normed, gate_weight, NN)
    up = dot(normed, up_weight, NN)
    square = gate * gate
    bent = jnp.tanh(SLOPE * gate * (1.0 + CUBIC * square))
    half = 0.5 * (1.0 + bent)
    active = gate * half
    slope = half + 0.5 * gate * (1.0 - bent * bent) * (SLOPE * (1.0 + 3.0 * CUBIC * square))
    hidden = (active * up).astype(bf16)
    grad_hidden = dot(branch, down, NT)
    grad_gate = (grad_hidden * up * slope).astype(bf16)
    grad_up = (grad_hidden * active).astype(bf16)
    third_ref[...] += dot(hidden, down, NN)
    back_ref[...] += dot(grad_gate, gate_weight, NT) + dot(grad_up, up_weight, NT)
    d_gate_ref[slot] = dot(turned_ref[...], grad_gate, NN).astype(bf16)
    d_up_ref[slot] = dot(turned_ref[...], grad_up, NN).astype(bf16)
    d_down = dot(hidden, branch, TN)
    for i in range(rows // own):
        for c in range(stacked // width):
            high = min(own, tall - c * own)
            part = d_down[i * tall + c * own : i * tall + c * own + high].astype(bf16)
            at = i * own
            d_down_ref[slot, at : at + high, c * width : (c + 1) * width] = part
            if high < own:
                d_down_ref[slot, at + high : at + own, c * width : (c + 1) * width] = jnp.zeros(
                    (own - high, width), bf16
                )
    for copy in copies(k):
        copy.start()

    @pl.when(k == steps - 1)
    def _():
        second, back = second_ref[...], back_ref[...]
        out_ref[...] = (third_ref[...] * live_ref[...]).astype(bf16)
        scale = lax.rsqrt(jnp.mean(second * second, axis=1, keepdims=True) + epsilon)
        d_gain_ref[...] = jnp.sum(back * second * scale, axis=0, keepdims=True)
        back = back * gain_ref[...]
        inner = jnp.mean(back * second, axis=1, keepdims=True)
        back = scale * back - second * (scale * scale * scale * inner)
        grad_second_ref[...] = cotangent_ref[...].astype(f32) * live_ref[...] + back
        for step in (k - 1, k):
            for copy in copies(step):
                copy.wait()


def feed_forward(second, gain, live, cotangent, weights, inner, own):
    slots, width = second.shape
    steps = inner // HIDDEN
    stacked = weights.shape[1] - 2 * inner
    rows = weights.shape[0] // steps
    whole = lambda *shape: pl.BlockSpec(shape, lambda k: (0,) * len(shape))
    unit = HIDDEN // 2
    column = lambda first: pl.BlockSpec((width, unit), lambda k: (0, first + 2 * k))
    at = stacked // unit
    return pl.pallas_call(
        functools.partial(feed_forward_kernel, own),
        out_shape=(
            jax.ShapeDtypeStruct((slots, width), bf16),
            jax.ShapeDtypeStruct((slots, width), f32),
            jax.ShapeDtypeStruct((1, width), f32),
            jax.ShapeDtypeStruct(weights.shape, bf16),
        ),
        grid=(steps,),
        in_specs=[
            whole(slots, width),
            whole(1, width),
            whole(slots, 1),
            whole(slots, width),
            pl.BlockSpec((rows, stacked), lambda k: (k, 0)),
            column(at),
            column(at + 1),
            column(at + 2 * steps),
            column(at + 2 * steps + 1),
        ],
        out_specs=[
            whole(slots, width),
            whole(slots, width),
            whole(1, width),
            pl.BlockSpec(memory_space=pl.ANY),
        ],
        scratch_shapes=[
            pltpu.VMEM((slots, width), bf16),
            pltpu.VMEM((width, slots), bf16),
            pltpu.VMEM((slots, width), bf16),
            pltpu.VMEM((slots, width), f32),
            pltpu.VMEM((slots, width), f32),
            pltpu.VMEM((2, width, HIDDEN), bf16),
            pltpu.VMEM((2, width, HIDDEN), bf16),
            pltpu.VMEM((2, rows, stacked), bf16),
            pltpu.SemaphoreType.DMA((2, 3)),
        ],
        cost_estimate=cost(
            flops=18 * slots * width * inner,
            transcendentals=slots * inner,
            bytes_accessed=4 * weights.size + 16 * slots * width,
        ),
        name="feed_forward",
    )(second, gain.reshape(1, width), live, cotangent, weights, weights, weights, weights, weights)


class Cube:
    def __init__(self, narrow, wide):
        self.narrow, self.wide = narrow, wide
        self.size = narrow * wide
        self.bits = self.size.bit_length() - 1
        self.index = lax.axis_index(BOTH)

    def swap(self, value, mask):
        pairs = [(i, i ^ mask) for i in range(self.size)]
        return lax.ppermute(value, BOTH, pairs)

    def total(self, value, bits):
        for bit in bits:
            value = value + self.swap(value, 1 << bit)
        return value


def merge_four(cube, pieces, split):
    r, n = pieces[0].shape

    def kernel(place_ref, *refs):
        ins, (left_ref, right_ref) = refs[:4], refs[4:]
        for m, ref in enumerate(ins):
            at = place_ref[0] ^ m
            left_ref[at] = ref[:, :split]
            right_ref[at] = ref[:, split:]

    return pl.pallas_call(
        kernel,
        out_shape=(
            jax.ShapeDtypeStruct((4, r, split), bf16),
            jax.ShapeDtypeStruct((4, r, n - split), bf16),
        ),
        grid_spec=pltpu.PrefetchScalarGridSpec(
            num_scalar_prefetch=1,
            grid=(1,),
            in_specs=[pl.BlockSpec((r, n), lambda i, s: (0, 0))] * 4,
            out_specs=[
                pl.BlockSpec((4, r, split), lambda i, s: (0, 0, 0)),
                pl.BlockSpec((4, r, n - split), lambda i, s: (0, 0, 0)),
            ],
        ),
        cost_estimate=cost(flops=0, transcendentals=0, bytes_accessed=16 * r * n),
        name="merge_four",
    )(((cube.index >> 1) & 3).reshape(1), *pieces)


def merge_two(side, mine, come, chunks):
    a, rows, n = mine.shape
    piece = pl.BlockSpec((1, rows, n // chunks), lambda i, c, s: (i, 0, c))

    def kernel(side_ref, mine_ref, come_ref, out_ref):
        out_ref[0, side_ref[0]] = mine_ref[0]
        out_ref[0, 1 - side_ref[0]] = come_ref[0]

    return pl.pallas_call(
        kernel,
        out_shape=jax.ShapeDtypeStruct((a, 2, rows, n), bf16),
        grid_spec=pltpu.PrefetchScalarGridSpec(
            num_scalar_prefetch=1,
            grid=(a, chunks),
            in_specs=[piece, piece],
            out_specs=pl.BlockSpec((1, 2, rows, n // chunks), lambda i, c, s: (i, 0, 0, c)),
        ),
        cost_estimate=cost(
            flops=0, transcendentals=0, bytes_accessed=8 * a * rows * n
        ),
        name="merge_two",
    )(side.reshape(1), mine, come)


class Gather:
    def __init__(self, cube, shard, split):
        self.cube = cube
        pieces = [shard] + [cube.swap(shard, m << 1) for m in (1, 2, 3)]
        self.start = merge_four(cube, pieces, split)

    def half(self, filler):
        cube = self.cube
        one, two = self.start
        r = one.shape[1]
        come_one, come_two = cube.swap(one, 1), cube.swap(two.reshape(1, 4 * r, -1), 16)
        come_one, come_two, filler = tie(come_one, come_two, filler)
        one = merge_two(self.side(0), one, come_one, 1)
        two = merge_two(self.side(4), two.reshape(1, 4 * r, -1), come_two, 1)
        return one.reshape(1, 8 * r, -1), two.reshape(8, r, -1), filler

    def side(self, bit):
        return (self.cube.index >> bit) & 1

    def most(self, one, two):
        cube = self.cube
        r = two.shape[1]
        one = merge_two(self.side(4), one, cube.swap(one, 16), 2 - one.shape[2] // LANES % 2)
        two = merge_two(self.side(0), two, cube.swap(two, 1), 1)
        return [one.reshape(2, 8 * r, -1), two.reshape(2, 8 * r, -1)]

    def finish(self, values):
        core = self.side(3)
        chunks = lambda value: 2 - value.shape[2] // LANES % 2
        return [
            merge_two(core, value, self.cube.swap(value, 8), chunks(value)).reshape(
                -1, value.shape[2]
            )
            for value in values
        ]


class Scatter:
    def __init__(self, cube, grads):
        self.cube = cube
        self.shapes = [(grad.shape[0] // cube.size, grad.shape[1]) for grad in grads]
        self.own = self.shapes[0][0]
        self.flat = [i for i, (r, _) in enumerate(self.shapes) if r == self.own]
        self.tall = [i for i, (r, _) in enumerate(self.shapes) if r != self.own]
        self.grads = [
            grad.reshape(2, 2, cube.wide * r, n)
            for grad, (r, n) in zip(grads, self.shapes, strict=True)
        ]
        self.sides = jnp.stack([cube.index >> 4, (cube.index >> 3) & 1, cube.index & 1])
        self.groups = [(self.own, sum(self.shapes[i][1] for i in self.flat))]
        self.groups += [self.shapes[i] for i in self.tall]

    def message(self, come, own, places, lead=1, packed=0):
        wide = self.cube.wide
        split = 2
        n_grads, n_groups = len(self.grads), len(self.groups)
        n_ins = n_grads + len(come)
        widths = [n for _, n in self.groups]
        stack = [-(-r // self.own) for r, _ in self.groups]

        def kernel(sides_ref, *refs):
            ins, outs = refs[:n_ins], refs[n_ins:]
            flat = [ins[i][0, 0] for i in self.flat]
            values = [flat[0] if len(flat) == 1 else jnp.concatenate(flat, axis=1)]
            values += [ins[i][0, 0] for i in self.tall]
            for k, ref in enumerate(ins[n_grads:]):
                got = ref[...]
                got = got.reshape(got.shape[-2:])
                i = k % n_groups
                values[i] = values[i].astype(f32) + got.astype(f32)
            if not packed:
                for out_ref, value in zip(outs, values, strict=True):
                    out_ref[...] = value.astype(bf16).reshape(out_ref.shape)
                return
            at = 0
            for value, (r, n), high in zip(values, self.groups, stack, strict=True):
                value = value.astype(f32).reshape(wide // split, r, n)
                for c in range(high):
                    part = value[:, c * self.own : (c + 1) * self.own].astype(bf16)
                    if packed == 1:
                        outs[0][:, : part.shape[1], at : at + n] = part
                    else:
                        side = sides_ref[2]
                        for i in range(0, part.shape[0], 2):
                            for flip, out_ref in enumerate(outs):
                                out_ref[i // 2, : part.shape[1], at : at + n] = jnp.where(
                                    side == flip, part[i], part[i + 1]
                                )
                    at += n

        in_specs = [
            pl.BlockSpec((1, 1, wide * r // split, n), lambda i, j, s: (*own(i, s), j, 0))
            for r, n in self.shapes
        ]
        for k, value in enumerate(come):
            at = places[k // n_groups]
            r, n = self.groups[k % n_groups]
            in_specs.append(
                pl.BlockSpec(
                    (1,) * (value.ndim - 2) + (wide * r // split, n),
                    lambda i, j, s, at=at: (*at(s), j, 0),
                )
            )
        if packed:
            n = sum(w * high for w, high in zip(widths, stack, strict=True))
            high = wide // packed
            out_shape = [jax.ShapeDtypeStruct((high, self.own, n), bf16)] * packed
            out_specs = [
                pl.BlockSpec((high // split, self.own, n), lambda i, j, s: (j, 0, 0))
            ] * packed
        else:
            out_shape = [jax.ShapeDtypeStruct((lead, wide * r, n), bf16) for r, n in self.groups]
            out_specs = [
                pl.BlockSpec((1, wide * r // split, n), lambda i, j, s: (i, j, 0))
                for r, n in self.groups
            ]
        size = sum(int(np.prod(out.shape)) for out in out_shape)
        return pl.pallas_call(
            kernel,
            out_shape=out_shape,
            grid_spec=pltpu.PrefetchScalarGridSpec(
                num_scalar_prefetch=1,
                grid=(lead, split),
                in_specs=in_specs,
                out_specs=out_specs,
            ),
            cost_estimate=cost(
                flops=size, transcendentals=0, bytes_accessed=4 * size
            ),
            name="message",
        )(self.sides, *self.grads, *come)

    def swap(self, values, mask):
        return [self.cube.swap(value, mask) for value in values]

    def to_core(self):
        return self.message([], lambda i, s: (i, 1 - s[1]), [], lead=2)

    def to_x(self, one):
        return self.message(one, lambda i, s: (1 - s[0], s[1]), [lambda s: (1 - s[0],)])

    def to_wide(self, one, two, halved=False):
        places = [lambda s: (s[0],), lambda s: (0,)]
        return self.message(
            [*one, *two], lambda i, s: (s[0], s[1]), places, packed=1 + halved
        )

    def step(self, bit, mine, come):
        blocks, r, n = mine.shape

        def kernel(side_ref, *refs):
            keep_ref, send_ref = refs[-2:]
            side = side_ref[0]
            for i in range(blocks // 2):
                for out_ref, at in ((keep_ref, 2 * i + side), (send_ref, 2 * i + 1 - side)):
                    value = refs[0][at].astype(f32) + refs[1][at].astype(f32)
                    out_ref[i] = value.astype(bf16)

        whole = pl.BlockSpec(mine.shape, lambda i, s: (0, 0, 0))
        half = pl.BlockSpec((blocks // 2, r, n), lambda i, s: (0, 0, 0))
        return pl.pallas_call(
            kernel,
            out_shape=[jax.ShapeDtypeStruct((blocks // 2, r, n), bf16)] * 2,
            grid_spec=pltpu.PrefetchScalarGridSpec(
                num_scalar_prefetch=1,
                grid=(1,),
                in_specs=[whole, whole],
                out_specs=[half, half],
            ),
            cost_estimate=cost(
                flops=mine.size, transcendentals=0, bytes_accessed=6 * mine.size
            ),
            name="step",
        )(((self.cube.index >> bit) & 1).reshape(1), mine, come)

    def finish(self, *come):
        def kernel(*refs):
            ins, outs = refs[: len(come)], refs[len(come) :]
            blocks = [ref[i] for ref in ins for i in range(ref.shape[0])]
            value = blocks[0].astype(f32)
            for block in blocks[1:]:
                value = value + block.astype(f32)
            at = 0
            for i in self.flat:
                n = self.shapes[i][1]
                outs[i][...] = value[:, at : at + n]
                at += n
            for i in self.tall:
                r, n = self.shapes[i]
                for c in range(0, r, self.own):
                    high = min(self.own, r - c)
                    outs[i][c : c + high] = value[:high, at : at + n]
                    at += n

        size = sum(value.size for value in come)
        return pl.pallas_call(
            kernel,
            out_shape=tuple(jax.ShapeDtypeStruct(shape, f32) for shape in self.shapes),
            cost_estimate=cost(
                flops=size, transcendentals=0, bytes_accessed=4 * size
            ),
            name="finish",
        )(*come)


def tie(*values):
    return lax.optimization_barrier(values)


def pack_shards(parts, widths, rows):
    flat = [part for group in parts for part in group]

    def kernel(*refs):
        ins, outs = refs[: len(flat)], refs[len(flat) :]
        refs_of = iter(ins)
        for out_ref, group in zip(outs, parts, strict=True):
            at = 0
            for array, start, count in group:
                ref, n = next(refs_of), array.shape[1]
                out_ref[:count, at : at + n] = ref[start : start + count, :]
                if count < rows:
                    out_ref[count:, at : at + n] = jnp.zeros((rows - count, n), bf16)
                at += n

    return pl.pallas_call(
        kernel,
        out_shape=tuple(jax.ShapeDtypeStruct((rows, n), bf16) for n in widths),
        name="pack",
    )(*[part[0] for part in flat])


def rms_norm(value, gain):
    return value * lax.rsqrt(jnp.mean(value * value, axis=-1, keepdims=True) + epsilon) * gain


def gelu_tanh(value):
    return jax.nn.gelu(value, approximate=True)


def on_device(
    targets,
    memory,
    cotangent,
    target_len,
    memory_len,
    self_query,
    self_key,
    self_value,
    self_out,
    cross_query,
    cross_key,
    cross_value,
    cross_out,
    ff_gate,
    ff_up,
    ff_down,
    self_gain,
    cross_gain,
    ff_gain,
    position_bias,
    narrow,
    wide,
):
    cube = Cube(narrow, wide)
    pairs, length, width = targets.shape
    slots = pairs * length
    own, own_ff = self_query.shape[0], ff_down.shape[0]
    inner = ff_gate.shape[1]
    devices = cube.size
    stepped = narrow == 4 and wide == 8 and own % 8 == 0

    gains = jnp.stack([self_gain, cross_gain, ff_gain], axis=1)
    gains = jnp.pad(gains, ((0, 0), (0, LANES - 3)))
    stack = -(-own_ff // own)
    whole = lambda *arrays: [(array, 0, own) for array in arrays]
    self_shard, cross_shard, ff_shard = pack_shards(
        [
            whole(self_query, self_key, self_value, self_out, gains),
            whole(cross_query, cross_key, cross_value, cross_out),
            [(ff_down, c * own, min(own, own_ff - c * own)) for c in range(stack)]
            + whole(ff_gate, ff_up),
        ],
        [4 * width + LANES, 4 * width, 2 * inner + stack * width],
        own,
    )
    places = jnp.arange(length)
    apart = places[:, None] - places[None, :]
    bucket = bucket_of_distance(length, BUCKETS, REACH)
    starts = [int(np.argmax(bucket >= b)) for b in range(1, int(bucket[-1]) + 1)]
    bucket_matrix = sum((apart >= start).astype(jnp.int32) for start in starts)
    onehot = (bucket_matrix[:, :, None] == jnp.arange(BUCKETS)[None, None, :]).astype(bf16)
    bias = jnp.einsum("ijb,bh->hij", onehot, position_bias, preferred_element_type=f32)
    bias = jnp.where((apart >= 0)[None], bias, negative).astype(bf16)

    exchange = lambda value: lax.all_to_all(
        value, "wide", split_axis=0, concat_axis=0, tiled=True
    )
    gathered = lax.all_gather(self_shard, BOTH, axis=0, tiled=True)
    ff = lax.all_gather(ff_shard, BOTH, axis=0, tiled=True)
    if stepped:
        cross_gather = Gather(cube, cross_shard, 2 * width)
        one, two, bias = cross_gather.half(bias)
        most = cross_gather.most(one, two)
        memory, most[0] = tie(memory, most[0])
        gathered, *most = tie(gathered, *most)
        c_query_key, c_value_out = cross_gather.finish(most)
    else:
        cross = lax.all_gather(cross_shard, BOTH, axis=0, tiled=True)
        c_query_key, c_value_out = cross[:, : 2 * width], cross[:, 2 * width :]
    memory_rows = exchange(memory).reshape(wide, pairs, -1, width)
    w_qkv, s_out = gathered[:, : 3 * width], gathered[:, 3 * width : 4 * width]
    c_query, c_out = c_query_key[:, :width], c_value_out[:, width:]

    gains = gathered[:, 4 * width : 4 * width + 3].astype(f32).T
    gain_one, gain_two, gain_three = gains[0], gains[1], gains[2]
    live = (places[None, :] < target_len[:, None]).astype(f32).reshape(slots, 1)
    inputs = targets.astype(f32).reshape(slots, width)

    normed_one = rms_norm(inputs, gain_one).astype(bf16)
    cube_of = lambda value: value.reshape(pairs, length, -1)
    qkv_one = cube_of(dot(normed_one, w_qkv, NN).astype(bf16))
    mixed_one, total_one = self_forward(qkv_one, bias)
    mixed_one = mixed_one.reshape(slots, width)
    first = inputs + dot(mixed_one, s_out, NN)
    normed_two = rms_norm(first, gain_two).astype(bf16)
    query_two = cube_of(dot(normed_two, c_query, NN).astype(bf16))
    held = ()
    for p in range(pairs):
        held = cross_forward(
            p, query_two, memory_rows, c_query_key, c_value_out, memory_len, held
        )
    mixed_two, total_two, key_two, value_two = held
    mixed_two = mixed_two.reshape(slots, width)
    second = first + dot(mixed_two, c_out, NN)

    stacked = stack * width
    if stepped:
        layer_out, grad_second, d_gain_three, ff_grads = feed_forward(
            second, gain_three, live, cotangent.reshape(slots, width), ff, inner, own
        )
        d_gain_three = d_gain_three.reshape(width)
    else:
        f_gate, f_up = ff[:, stacked : stacked + inner], ff[:, stacked + inner :]
        f_down = ff[:, :stacked].reshape(devices, own, stack, width).swapaxes(1, 2)
        f_down = f_down.reshape(devices, -1, width)[:, :own_ff].reshape(inner, width)
        normed_three = rms_norm(second, gain_three).astype(bf16)
        gate = dot(normed_three, f_gate, NN)
        upward = dot(normed_three, f_up, NN)
        activated, gelu_pull = jax.vjp(gelu_tanh, gate)
        hidden = (activated * upward).astype(bf16)
        third = second + dot(hidden, f_down, NN)
        layer_out = (third * live).astype(bf16)
        grad_third = cotangent.astype(f32).reshape(slots, width) * live
        branch_ff = grad_third.astype(bf16)
        d_down = dot(hidden, branch_ff, TN).astype(bf16)
        grad_hidden = dot(branch_ff, f_down, NT)
        grad_gate = gelu_pull(grad_hidden * upward)[0].astype(bf16)
        grad_up = (grad_hidden * activated).astype(bf16)
        d_gate = dot(normed_three, grad_gate, TN).astype(bf16)
        d_up = dot(normed_three, grad_up, TN).astype(bf16)
        grad_normed_three = dot(grad_gate, f_gate, NT) + dot(grad_up, f_up, NT)
        d_down = d_down.reshape(devices, own_ff, width)
        d_down = jnp.pad(d_down, ((0, 0), (0, stack * own - own_ff), (0, 0)))
        d_down = d_down.reshape(devices, stack, own, width).swapaxes(1, 2)
        d_down = d_down.reshape(devices * own, stacked)
        ff_grads = jnp.concatenate([d_down, d_gate, d_up], axis=1)
        _, norm_three = jax.vjp(rms_norm, second, gain_three)
        back_three, d_gain_three = norm_three(grad_normed_three)
        grad_second = grad_third + back_three
    layer_out = layer_out.reshape(pairs, length, width)
    ff_grads = lax.psum_scatter(ff_grads, BOTH, scatter_dimension=0, tiled=True)

    branch_cross = grad_second.astype(bf16)
    d_cross_out = dot(mixed_two, branch_cross, TN).astype(bf16)
    grad_mixed_two = cube_of(dot(branch_cross, c_out, NT).astype(bf16))
    held = ()
    for p in range(pairs):
        grad_query_two, rows_grad, *found = cross_backward(
            p,
            query_two,
            key_two,
            value_two,
            memory_len,
            total_two,
            grad_mixed_two,
            memory_rows,
            c_query_key,
            c_value_out,
            held,
        )
        held = (*held[:-2], *found, grad_query_two, rows_grad)
    d_cross_key, d_cross_value = found
    grad_memory = exchange(rows_grad.reshape(memory.shape))
    grad_query_two = grad_query_two.reshape(slots, width)
    d_cross_query = dot(normed_two, grad_query_two, TN).astype(bf16)
    _, norm_two = jax.vjp(rms_norm, first, gain_two)
    back_two, d_gain_two = norm_two(dot(grad_query_two, c_query, NT))
    grad_first = grad_second + back_two

    branch_self = grad_first.astype(bf16)
    d_self_out = dot(mixed_one, branch_self, TN).astype(bf16)
    grad_mixed_one = cube_of(dot(branch_self, s_out, NT).astype(bf16))
    middle = [d_cross_query, d_cross_key, d_cross_value, d_cross_out, d_self_out]
    if stepped:
        middle_sum = Scatter(cube, middle)
        middle_one = middle_sum.swap(middle_sum.to_core(), 8)
        middle_send = middle_sum.to_x(middle_one)
        grad_mixed_one, *middle_send = tie(grad_mixed_one, *middle_send)
        middle_two = middle_sum.swap(middle_send, 16)
    grads_one, diagonals = self_backward(qkv_one, bias, total_one, grad_mixed_one)
    grads_one = grads_one.reshape(slots, 3 * width)
    d_qkv = dot(normed_one, grads_one, TN).astype(bf16)
    if stepped:
        last_sum = Scatter(cube, [d_qkv])
        last_send = last_sum.to_core()
        grads_one, diagonals, *tied = tie(grads_one, diagonals, *middle_two, *last_send)
        middle_two, last_send = tied[: len(middle_two)], tied[len(middle_two) :]
        last_one = last_sum.swap(last_send, 8)
        middle_keep, middle_send = middle_sum.to_wide(middle_one, middle_two, halved=True)
        grads_one, middle_send = tie(grads_one, middle_send)
        middle_come = cube.swap(middle_send, 1)
    if stepped:
        last_send = last_sum.to_x(last_one)
        grads_one, *last_send = tie(grads_one, *last_send)
        last_two = last_sum.swap(last_send, 16)
    grad_normed_one = dot(grads_one, w_qkv, NT)
    _, norm_one = jax.vjp(rms_norm, inputs, gain_one)
    back_one, d_gain_one = norm_one(grad_normed_one)
    grad_targets = (grad_first + back_one).reshape(pairs, length, width)
    if stepped:
        last_two[0], middle_come, grad_memory, grad_targets = tie(
            last_two[0], middle_come, grad_memory, grad_targets
        )
        middle_keep, middle_send = middle_sum.step(1, middle_keep, middle_come)
        middle_come = cube.swap(middle_send, 2)

    padded = diagonals.shape[-1]
    column = (padded - np.arange(length)) % padded
    to_bucket = np.zeros((padded, BUCKETS), np.float32)
    to_bucket[column, bucket] = 1.0
    diagonals = jnp.sum(diagonals, axis=2).reshape(HEADS, padded)
    d_position = jnp.einsum(
        "hc,cb->bh", diagonals, jnp.asarray(to_bucket), precision=lax.Precision.HIGHEST
    )
    small = jnp.concatenate(
        [d_gain_one, d_gain_two, d_gain_three, d_position.reshape(-1)]
    ).reshape(-1, LANES)
    small = jnp.pad(small, ((0, -small.shape[0] % 8), (0, 0)))
    near = range(wide.bit_length() - 1, cube.bits)
    far = range(wide.bit_length() - 1)
    small = cube.total(small, near)
    if stepped:
        last_two[0], small = tie(last_two[0], small)
        last_keep, last_send = last_sum.to_wide(last_one, last_two, halved=True)
        last_come = cube.swap(last_send, 1)
        middle_keep, middle_send = middle_sum.step(2, middle_keep, middle_come)
        middle_come = cube.swap(middle_send, 4)
        last_keep, last_send = last_sum.step(1, last_keep, last_come)
        last_come = cube.swap(last_send, 2)
        middle_grads = middle_sum.finish(middle_keep, middle_come)
        last_keep, last_send = last_sum.step(2, last_keep, last_come)
        last_come = cube.swap(last_send, 4)
        last_come, ff_grads = tie(last_come, ff_grads)
        (d_qkv,) = last_sum.finish(last_keep, last_come)
    else:
        scatter = lambda value: lax.psum_scatter(
            value, BOTH, scatter_dimension=0, tiled=True
        ).astype(f32)
        middle_grads = [scatter(value) for value in middle]
        d_qkv = scatter(d_qkv)
    small = cube.total(small, far).reshape(-1)
    gain_grads = small[: 3 * width].reshape(3, devices, width // devices)
    gain_grads = lax.dynamic_index_in_dim(gain_grads, cube.index, 1, keepdims=False)
    grad_position = small[3 * width : 3 * width + BUCKETS * HEADS].reshape(BUCKETS, HEADS)

    ff_grads = ff_grads.astype(f32)
    d_down = jnp.concatenate(
        [ff_grads[:, c * width : (c + 1) * width] for c in range(stack)], axis=0
    )[:own_ff]
    return (
        layer_out,
        grad_targets,
        grad_memory.astype(f32),
        d_qkv[:, :width],
        d_qkv[:, width : 2 * width],
        d_qkv[:, 2 * width :],
        middle_grads[4],
        *middle_grads[:4],
        ff_grads[:, stacked : stacked + inner],
        ff_grads[:, stacked + inner :],
        d_down,
        gain_grads[0],
        gain_grads[1],
        gain_grads[2],
        grad_position,
    )


def solution(mesh):
    rows = P(BOTH, None)
    slots = P(BOTH, None, None)
    one = P(BOTH)
    source = P("narrow", "wide", None)
    in_specs = (slots, source, slots, one, one) + (rows,) * 11 + (one,) * 3 + (P(),)
    out_specs = (slots, slots, source) + (rows,) * 11 + (one,) * 3 + (P(),)
    narrow, wide = mesh.shape["narrow"], mesh.shape["wide"]

    def body(*args):
        return on_device(*args, narrow=narrow, wide=wide)

    return jax.shard_map(body, mesh=mesh, in_specs=in_specs, out_specs=out_specs, check_vma=False)
```

```python
import functools

import jax
import jax.numpy as jnp
import numpy as np
from jax import lax
from jax.experimental import pallas as pl
from jax.experimental.pallas import tpu as pltpu
from jax.sharding import PartitionSpec as P

HEADS = 12
HEAD_DIM = 64
BUCKETS = 32
REACH = 128
LANES = 128
BOTH = ("narrow", "wide")
SHARE = 8

negative = -1e30
epsilon = 1e-06
bf16 = jnp.bfloat16
f32 = jnp.float32

NT = (((1,), (1,)), ((), ()))
NN = (((1,), (0,)), ((), ()))
TN = (((0,), (0,)), ((), ()))


def cost(flops=0, transcendentals=0, bytes_accessed=0):
    return pl.CostEstimate(
        flops=flops // SHARE,
        transcendentals=transcendentals // SHARE,
        bytes_accessed=bytes_accessed // SHARE,
    )


def dot(left, right, dims):
    return lax.dot_general(left, right, dims, preferred_element_type=f32)


def bucket_of_distance(length, buckets, reach):
    apart = np.arange(length)
    exact = buckets // 2
    safe = np.maximum(apart, 1)
    far = exact + (np.log(safe / exact) / np.log(reach / exact) * (buckets - exact)).astype(
        np.int64
    )
    far = np.minimum(far, buckets - 1)
    return np.where(apart < exact, apart, far).astype(np.int32)


def stack_heads(value):
    first = lax.broadcasted_iota(jnp.int32, value.shape, 1) < HEAD_DIM
    zero = jnp.zeros_like(value)
    return jnp.concatenate([jnp.where(first, value, zero), jnp.where(first, zero, value)], axis=0)


def join_heads(value):
    half = value.shape[0] // 2
    first = lax.broadcasted_iota(jnp.int32, (half, value.shape[1]), 1) < HEAD_DIM
    return jnp.where(first, value[:half], value[half:])


def stack_columns(total):
    return jnp.concatenate([total[:, :1], total[:, HEAD_DIM : HEAD_DIM + 1]], axis=0)


def attend(scores, v, mixed_ref, total_ref, pair=0):
    top = jnp.max(scores, axis=1, keepdims=True)
    grown = jnp.exp(scores - top)
    total = jnp.sum(grown, axis=1, keepdims=True)
    mixed = dot(grown.astype(bf16), v, NN) * (1.0 / total)
    mixed_ref[pair] = join_heads(mixed).astype(bf16)
    total_ref[pair] = join_heads(jnp.broadcast_to(top + jnp.log(total), mixed.shape))


def attend_back(scores, total, grad, v):
    probs = jnp.exp(scores - stack_columns(total))
    grad_probs = dot(grad, v, NT)
    inner = jnp.sum(probs * grad_probs, axis=1, keepdims=True)
    return probs.astype(bf16), (probs * (grad_probs - inner)).astype(bf16)


def self_forward_kernel(q_ref, k_ref, v_ref, bias_ref, mixed_ref, total_ref):
    pairs, length, _ = q_ref.shape
    bias = bias_ref[...].reshape(2 * length, length).astype(f32)
    for p in range(pairs):
        scores = dot(stack_heads(q_ref[p]), k_ref[p], NT) + bias
        attend(scores, v_ref[p], mixed_ref, total_ref, p)


def self_forward(qkv, bias):
    pairs, length, width = qkv.shape
    width //= 3
    steps = width // LANES
    part = lambda c: pl.BlockSpec((pairs, length, LANES), lambda h: (0, 0, h + c * steps))
    return pl.pallas_call(
        self_forward_kernel,
        out_shape=(
            jax.ShapeDtypeStruct((pairs, length, width), bf16),
            jax.ShapeDtypeStruct((pairs, length, width), f32),
        ),
        grid=(steps,),
        in_specs=[
            part(0),
            part(1),
            part(2),
            pl.BlockSpec((2, length, length), lambda h: (h, 0, 0)),
        ],
        out_specs=[part(0), part(0)],
        cost_estimate=cost(
            flops=pairs * HEADS * length * length * HEAD_DIM * 4,
            transcendentals=pairs * HEADS * length * length,
            bytes_accessed=pairs * length * width * 12,
        ),
        name="self_forward",
    )(qkv, qkv, qkv, bias)


def self_backward_kernel(
    q_ref, k_ref, v_ref, bias_ref, total_ref, grad_ref, grads_ref, diagonal_ref, sum_ref
):
    hp, steps = pl.program_id(0), pl.num_programs(0)
    pairs, length, _ = q_ref.shape
    padded = sum_ref.shape[-1]
    bias = bias_ref[...].reshape(2 * length, length).astype(f32)

    @pl.when(hp == 0)
    def _():
        sum_ref[...] = jnp.zeros(sum_ref.shape, f32)

    summed = 0.0
    for p in range(pairs):
        q, grad, k = stack_heads(q_ref[p]), stack_heads(grad_ref[p]), k_ref[p]
        scores = dot(q, k, NT) + bias
        probs, grad_scores = attend_back(scores, total_ref[p], grad, v_ref[p])
        summed = summed + grad_scores.astype(f32)
        found = join_heads(dot(grad_scores, k, NN)), dot(grad_scores, q, TN), dot(probs, grad, TN)
        for c in range(3):
            at = pl.ds(pl.multiple_of((hp + c * steps) * LANES, LANES), LANES)
            grads_ref[p, :, at] = found[c].astype(bf16)
    sum_ref[:, :, :length] = summed.reshape(2, length, length)

    rows = lax.broadcasted_iota(jnp.int32, (8, padded), 0)
    for h in range(2):
        held = sum_ref[h, 0:8, :]
        for i in range(8, length, 8):
            held = held + pltpu.roll(sum_ref[h, i : i + 8, :], padded - i, 1)
        for bit in (1, 2, 4):
            held = jnp.where((rows // bit) % 2 == 1, pltpu.roll(held, padded - bit, 1), held)
        diagonal_ref[0, h] = held


def self_backward(qkv, bias, total, grad):
    pairs, length, width = qkv.shape
    width //= 3
    steps = width // LANES
    padded = -(-length // LANES) * LANES
    part = lambda c: pl.BlockSpec((pairs, length, LANES), lambda h: (0, 0, h + c * steps))
    return pl.pallas_call(
        self_backward_kernel,
        out_shape=(
            jax.ShapeDtypeStruct(qkv.shape, bf16),
            jax.ShapeDtypeStruct((steps, 2, 8, padded), f32),
        ),
        grid=(steps,),
        in_specs=[
            part(0),
            part(1),
            part(2),
            pl.BlockSpec((2, length, length), lambda h: (h, 0, 0)),
            part(0),
            part(0),
        ],
        out_specs=[
            pl.BlockSpec((pairs, length, 3 * width), lambda h: (0, 0, 0)),
            pl.BlockSpec((1, 2, 8, padded), lambda h: (h, 0, 0, 0)),
        ],
        scratch_shapes=[pltpu.VMEM((2, length, padded), f32)],
        cost_estimate=cost(
            flops=pairs * HEADS * length * length * HEAD_DIM * 10,
            transcendentals=pairs * HEADS * length * length,
            bytes_accessed=pairs * length * width * 18,
        ),
        name="self_backward",
    )(qkv, qkv, qkv, bias, total, grad)


def dead_rows(live_rows, rows):
    places = lax.broadcasted_iota(jnp.int32, (1, rows), 1)
    return jnp.where(places < live_rows, 0.0, negative)


def cross_forward_kernel(pair, len_ref, q_ref, memory_ref, wk_ref, wv_ref, *refs):
    mixed_ref, total_ref, k_ref, v_ref = refs[-4:]
    rows = k_ref.shape[1]
    memory = memory_ref[...].reshape(rows, -1)
    kv = dot(memory, jnp.concatenate([wk_ref[...], wv_ref[...]], axis=1), NN).astype(bf16)
    k, v = kv[:, :LANES], kv[:, LANES:]
    k_ref[0], v_ref[0] = k, v
    scores = dot(stack_heads(q_ref[0]), k, NT) + dead_rows(len_ref[pair], rows)
    attend(scores, v, mixed_ref, total_ref)


def cross_forward(pair, query, memory, query_key, value_out, lens, before):
    pairs, length, width = query.shape
    sources, _, part, _ = memory.shape
    rows = sources * part
    steps = width // LANES
    target = pl.BlockSpec((1, length, LANES), lambda h, n: (pair, 0, h))
    source = pl.BlockSpec((1, rows, LANES), lambda h, n: (pair, 0, h))
    weight = lambda c: pl.BlockSpec((width, LANES), lambda h, n: (0, h + c * steps))
    return pl.pallas_call(
        functools.partial(cross_forward_kernel, pair),
        out_shape=(
            jax.ShapeDtypeStruct(query.shape, bf16),
            jax.ShapeDtypeStruct(query.shape, f32),
            jax.ShapeDtypeStruct((pairs, rows, width), bf16),
            jax.ShapeDtypeStruct((pairs, rows, width), bf16),
        ),
        grid_spec=pltpu.PrefetchScalarGridSpec(
            num_scalar_prefetch=1,
            grid=(steps,),
            in_specs=[
                target,
                pl.BlockSpec((sources, 1, part, width), lambda h, n: (0, pair, 0, 0)),
                weight(1),
                weight(0),
            ]
            + [pl.BlockSpec(memory_space=pl.ANY)] * len(before),
            out_specs=[target, target, source, source],
        ),
        input_output_aliases={5 + i: i for i in range(len(before))},
        cost_estimate=cost(
            flops=rows * width * (length * 4 + width * 4),
            transcendentals=HEADS * length * rows,
            bytes_accessed=length * width * 8 + rows * width * 6,
        ),
        name="cross_forward",
    )(lens, query, memory, query_key, value_out, *before)


def cross_backward_kernel(
    pair, last, len_ref, q_ref, k_ref, v_ref, total_ref, grad_ref, memory_ref, qk_ref, vo_ref, *refs
):
    *refs, grads_ref, held_ref, weight_ref, sems = refs
    hp, steps = pl.program_id(0), pl.num_programs(0)
    rows, width = k_ref.shape[1], weight_ref.shape[0]
    before = pair if last else 0
    before_refs, refs = refs[:before], refs[pair + 2 * (pair > 0) :]
    grad_query_ref, grad_memory_ref, *outs = refs

    moves = [
        (qk_ref.at[:, width:], weight_ref.at[:, :width]),
        (vo_ref.at[:, :width], weight_ref.at[:, width:]),
    ]
    if last:
        moves += [(memory_ref.at[:, p], held_ref.at[p]) for p in range(pair + 1)]
        moves += [(ref, grads_ref.at[p]) for p, ref in enumerate(before_refs)]
    copies = [pltpu.make_async_copy(*move, sems.at[i]) for i, move in enumerate(moves)]

    @pl.when(hp == 0)
    def _():
        for copy in copies:
            copy.start()

    q, grad, k = stack_heads(q_ref[0]), stack_heads(grad_ref[0]), k_ref[0]
    scores = dot(q, k, NT) + dead_rows(len_ref[pair], rows)
    probs, grad_scores = attend_back(scores, total_ref[0], grad, v_ref[0])
    grad_query_ref[0] = join_heads(dot(grad_scores, k, NN)).astype(bf16)
    for c, value in enumerate((dot(grad_scores, q, TN), dot(probs, grad, TN))):
        at = pl.ds(pl.multiple_of((hp + c * steps) * LANES, LANES), LANES)
        grads_ref[before, :, at] = value.astype(bf16)

    @pl.when(hp == steps - 1)
    def _():
        for copy in copies:
            copy.wait()
        back = dot(grads_ref[before], weight_ref[...], NT).astype(bf16)
        grad_memory_ref[...] = back.reshape(grad_memory_ref.shape)
        if last:
            d_kv = sum(
                dot(held_ref[p].reshape(rows, width), grads_ref[p], TN) for p in range(pair + 1)
            )
            outs[0][...] = d_kv[:, :width].astype(bf16)
            outs[1][...] = d_kv[:, width:].astype(bf16)
        else:
            outs[0][...] = grads_ref[0]


def cross_backward(
    pair, query, key, value, lens, total, grad, memory, query_key, value_out, before
):
    pairs, length, width = query.shape
    sources, _, part, _ = memory.shape
    rows = sources * part
    steps = width // LANES
    last = pair == pairs - 1
    held = pairs if last else 1
    target = pl.BlockSpec((1, length, LANES), lambda h, n: (pair, 0, h))
    source = pl.BlockSpec((1, rows, LANES), lambda h, n: (pair, 0, h))
    anywhere = pl.BlockSpec(memory_space=pl.ANY)
    whole = lambda *shape: pl.BlockSpec(shape, lambda h, n: (0,) * len(shape))
    out_shape = [
        jax.ShapeDtypeStruct(query.shape, bf16),
        jax.ShapeDtypeStruct(memory.shape, bf16),
    ]
    given = pl.BlockSpec((sources, 1, part, width), lambda h, n: (0, pair, 0, 0))
    if last:
        out_shape += [jax.ShapeDtypeStruct((width, width), bf16)] * 2
    else:
        out_shape += [jax.ShapeDtypeStruct((rows, 2 * width), bf16)]
    return pl.pallas_call(
        functools.partial(cross_backward_kernel, pair, last),
        out_shape=out_shape,
        grid_spec=pltpu.PrefetchScalarGridSpec(
            num_scalar_prefetch=1,
            grid=(steps,),
            in_specs=[target, source, source, target, target] + [anywhere] * (3 + len(before)),
            out_specs=[target, given] + [whole(*out.shape) for out in out_shape[2:]],
            scratch_shapes=[
                pltpu.VMEM((held, rows, 2 * width), bf16),
                pltpu.VMEM((held, sources, part, width), bf16),
                pltpu.VMEM((width, 2 * width), bf16),
                pltpu.SemaphoreType.DMA((2 + 2 * pairs,)),
            ],
        ),
        input_output_aliases={7 + len(before): 0, 8 + len(before): 1} if pair else {},
        cost_estimate=cost(
            flops=rows * width * (length * 10 + width * 8),
            transcendentals=HEADS * length * rows,
            bytes_accessed=length * width * 10 + rows * width * 8,
        ),
        name="cross_backward",
    )(lens, query, key, value, total, grad, memory, query_key, value_out, *before)


HIDDEN = 512
SLOPE = float(np.sqrt(2 / np.pi))
CUBIC = 0.044715


def feed_forward_kernel(
    own,
    second_ref,
    gain_ref,
    live_ref,
    cotangent_ref,
    down_ref,
    gate_low_ref,
    gate_high_ref,
    up_low_ref,
    up_high_ref,
    out_ref,
    grad_second_ref,
    d_gain_ref,
    grads_ref,
    normed_ref,
    turned_ref,
    branch_ref,
    third_ref,
    back_ref,
    d_gate_ref,
    d_up_ref,
    d_down_ref,
    sems,
):
    k, steps = pl.program_id(0), pl.num_programs(0)
    width = second_ref.shape[1]
    rows, stacked = d_down_ref.shape[1:]
    tall = HIDDEN // (rows // own)
    slot = k % 2

    def copies(step):
        at = step % 2
        gate = pl.multiple_of(stacked + step * HIDDEN, 256)
        up = pl.multiple_of(stacked + (steps + step) * HIDDEN, 256)
        first = pl.multiple_of(step * rows, 8)
        return [
            pltpu.make_async_copy(
                d_gate_ref.at[at], grads_ref.at[:, pl.ds(gate, HIDDEN)], sems.at[at, 0]
            ),
            pltpu.make_async_copy(
                d_up_ref.at[at], grads_ref.at[:, pl.ds(up, HIDDEN)], sems.at[at, 1]
            ),
            pltpu.make_async_copy(
                d_down_ref.at[at],
                grads_ref.at[pl.ds(first, rows), pl.ds(0, stacked)],
                sems.at[at, 2],
            ),
        ]

    @pl.when(k == 0)
    def _():
        second = second_ref[...]
        scale = lax.rsqrt(jnp.mean(second * second, axis=1, keepdims=True) + epsilon)
        normed = (second * scale * gain_ref[...]).astype(bf16)
        normed_ref[...] = normed
        turned_ref[...] = normed.T
        branch_ref[...] = (cotangent_ref[...].astype(f32) * live_ref[...]).astype(bf16)
        third_ref[...] = second
        back_ref[...] = jnp.zeros(back_ref.shape, f32)

    @pl.when(k >= 2)
    def _():
        for copy in copies(k - 2):
            copy.wait()

    packed = down_ref[...].astype(f32)
    pieces = []
    for i in range(rows // own):
        for c in range(stacked // width):
            high = min(own, tall - c * own)
            pieces.append(packed[i * own : i * own + high, c * width : (c + 1) * width])
    down = jnp.concatenate(pieces, axis=0).astype(bf16)
    gate_weight = jnp.concatenate([gate_low_ref[...], gate_high_ref[...]], axis=1)
    up_weight = jnp.concatenate([up_low_ref[...], up_high_ref[...]], axis=1)

    normed, branch = normed_ref[...], branch_ref[...]
    gate = dot(normed, gate_weight, NN)
    up = dot(normed, up_weight, NN)
    square = gate * gate
    bent = jnp.tanh(SLOPE * gate * (1.0 + CUBIC * square))
    half = 0.5 * (1.0 + bent)
    active = gate * half
    slope = half + 0.5 * gate * (1.0 - bent * bent) * (SLOPE * (1.0 + 3.0 * CUBIC * square))
    hidden = (active * up).astype(bf16)
    grad_hidden = dot(branch, down, NT)
    grad_gate = (grad_hidden * up * slope).astype(bf16)
    grad_up = (grad_hidden * active).astype(bf16)
    third_ref[...] += dot(hidden, down, NN)
    back_ref[...] += dot(grad_gate, gate_weight, NT) + dot(grad_up, up_weight, NT)
    d_gate_ref[slot] = dot(turned_ref[...], grad_gate, NN).astype(bf16)
    d_up_ref[slot] = dot(turned_ref[...], grad_up, NN).astype(bf16)
    d_down = dot(hidden, branch, TN)
    for i in range(rows // own):
        for c in range(stacked // width):
            high = min(own, tall - c * own)
            part = d_down[i * tall + c * own : i * tall + c * own + high].astype(bf16)
            at = i * own
            d_down_ref[slot, at : at + high, c * width : (c + 1) * width] = part
            if high < own:
                d_down_ref[slot, at + high : at + own, c * width : (c + 1) * width] = jnp.zeros(
                    (own - high, width), bf16
                )
    for copy in copies(k):
        copy.start()

    @pl.when(k == steps - 1)
    def _():
        second, back = second_ref[...], back_ref[...]
        out_ref[...] = (third_ref[...] * live_ref[...]).astype(bf16)
        scale = lax.rsqrt(jnp.mean(second * second, axis=1, keepdims=True) + epsilon)
        d_gain_ref[...] = jnp.sum(back * second * scale, axis=0, keepdims=True)
        back = back * gain_ref[...]
        inner = jnp.mean(back * second, axis=1, keepdims=True)
        back = scale * back - second * (scale * scale * scale * inner)
        grad_second_ref[...] = cotangent_ref[...].astype(f32) * live_ref[...] + back
        for step in (k - 1, k):
            for copy in copies(step):
                copy.wait()


def feed_forward(second, gain, live, cotangent, weights, inner, own):
    slots, width = second.shape
    steps = inner // HIDDEN
    stacked = weights.shape[1] - 2 * inner
    rows = weights.shape[0] // steps
    whole = lambda *shape: pl.BlockSpec(shape, lambda k: (0,) * len(shape))
    unit = HIDDEN // 2
    column = lambda first: pl.BlockSpec((width, unit), lambda k: (0, first + 2 * k))
    at = stacked // unit
    return pl.pallas_call(
        functools.partial(feed_forward_kernel, own),
        out_shape=(
            jax.ShapeDtypeStruct((slots, width), bf16),
            jax.ShapeDtypeStruct((slots, width), f32),
            jax.ShapeDtypeStruct((1, width), f32),
            jax.ShapeDtypeStruct(weights.shape, bf16),
        ),
        grid=(steps,),
        in_specs=[
            whole(slots, width),
            whole(1, width),
            whole(slots, 1),
            whole(slots, width),
            pl.BlockSpec((rows, stacked), lambda k: (k, 0)),
            column(at),
            column(at + 1),
            column(at + 2 * steps),
            column(at + 2 * steps + 1),
        ],
        out_specs=[
            whole(slots, width),
            whole(slots, width),
            whole(1, width),
            pl.BlockSpec(memory_space=pl.ANY),
        ],
        scratch_shapes=[
            pltpu.VMEM((slots, width), bf16),
            pltpu.VMEM((width, slots), bf16),
            pltpu.VMEM((slots, width), bf16),
            pltpu.VMEM((slots, width), f32),
            pltpu.VMEM((slots, width), f32),
            pltpu.VMEM((2, width, HIDDEN), bf16),
            pltpu.VMEM((2, width, HIDDEN), bf16),
            pltpu.VMEM((2, rows, stacked), bf16),
            pltpu.SemaphoreType.DMA((2, 3)),
        ],
        cost_estimate=cost(
            flops=18 * slots * width * inner,
            transcendentals=slots * inner,
            bytes_accessed=4 * weights.size + 16 * slots * width,
        ),
        name="feed_forward",
    )(second, gain.reshape(1, width), live, cotangent, weights, weights, weights, weights, weights)


class Cube:
    def __init__(self, narrow, wide):
        self.narrow, self.wide = narrow, wide
        self.size = narrow * wide
        self.bits = self.size.bit_length() - 1
        self.index = lax.axis_index(BOTH)

    def swap(self, value, mask):
        pairs = [(i, i ^ mask) for i in range(self.size)]
        return lax.ppermute(value, BOTH, pairs)

    def total(self, value, bits):
        for bit in bits:
            value = value + self.swap(value, 1 << bit)
        return value


def merge_four(cube, pieces, split):
    r, n = pieces[0].shape

    def kernel(place_ref, *refs):
        ins, (left_ref, right_ref) = refs[:4], refs[4:]
        for m, ref in enumerate(ins):
            at = place_ref[0] ^ m
            left_ref[at] = ref[:, :split]
            right_ref[at] = ref[:, split:]

    return pl.pallas_call(
        kernel,
        out_shape=(
            jax.ShapeDtypeStruct((4, r, split), bf16),
            jax.ShapeDtypeStruct((4, r, n - split), bf16),
        ),
        grid_spec=pltpu.PrefetchScalarGridSpec(
            num_scalar_prefetch=1,
            grid=(1,),
            in_specs=[pl.BlockSpec((r, n), lambda i, s: (0, 0))] * 4,
            out_specs=[
                pl.BlockSpec((4, r, split), lambda i, s: (0, 0, 0)),
                pl.BlockSpec((4, r, n - split), lambda i, s: (0, 0, 0)),
            ],
        ),
        cost_estimate=cost(flops=0, transcendentals=0, bytes_accessed=16 * r * n),
        name="merge_four",
    )(((cube.index >> 1) & 3).reshape(1), *pieces)


def merge_two(side, mine, come, chunks):
    a, rows, n = mine.shape
    piece = pl.BlockSpec((1, rows, n // chunks), lambda i, c, s: (i, 0, c))

    def kernel(side_ref, mine_ref, come_ref, out_ref):
        out_ref[0, side_ref[0]] = mine_ref[0]
        out_ref[0, 1 - side_ref[0]] = come_ref[0]

    return pl.pallas_call(
        kernel,
        out_shape=jax.ShapeDtypeStruct((a, 2, rows, n), bf16),
        grid_spec=pltpu.PrefetchScalarGridSpec(
            num_scalar_prefetch=1,
            grid=(a, chunks),
            in_specs=[piece, piece],
            out_specs=pl.BlockSpec((1, 2, rows, n // chunks), lambda i, c, s: (i, 0, 0, c)),
        ),
        cost_estimate=cost(
            flops=0, transcendentals=0, bytes_accessed=8 * a * rows * n
        ),
        name="merge_two",
    )(side.reshape(1), mine, come)


class Gather:
    def __init__(self, cube, shard, split):
        self.cube = cube
        pieces = [shard] + [cube.swap(shard, m << 1) for m in (1, 2, 3)]
        self.start = merge_four(cube, pieces, split)

    def half(self, filler):
        cube = self.cube
        one, two = self.start
        r = one.shape[1]
        come_one, come_two = cube.swap(one, 1), cube.swap(two.reshape(1, 4 * r, -1), 16)
        come_one, come_two, filler = tie(come_one, come_two, filler)
        one = merge_two(self.side(0), one, come_one, 1)
        two = merge_two(self.side(4), two.reshape(1, 4 * r, -1), come_two, 1)
        return one.reshape(1, 8 * r, -1), two.reshape(8, r, -1), filler

    def side(self, bit):
        return (self.cube.index >> bit) & 1

    def most(self, one, two):
        cube = self.cube
        r = two.shape[1]
        one = merge_two(self.side(4), one, cube.swap(one, 16), 2 - one.shape[2] // LANES % 2)
        two = merge_two(self.side(0), two, cube.swap(two, 1), 1)
        return [one.reshape(2, 8 * r, -1), two.reshape(2, 8 * r, -1)]

    def finish(self, values):
        core = self.side(3)
        chunks = lambda value: 2 - value.shape[2] // LANES % 2
        return [
            merge_two(core, value, self.cube.swap(value, 8), chunks(value)).reshape(
                -1, value.shape[2]
            )
            for value in values
        ]


class Scatter:
    def __init__(self, cube, grads):
        self.cube = cube
        self.shapes = [(grad.shape[0] // cube.size, grad.shape[1]) for grad in grads]
        self.own = self.shapes[0][0]
        self.flat = [i for i, (r, _) in enumerate(self.shapes) if r == self.own]
        self.tall = [i for i, (r, _) in enumerate(self.shapes) if r != self.own]
        self.grads = [
            grad.reshape(2, 2, cube.wide * r, n)
            for grad, (r, n) in zip(grads, self.shapes, strict=True)
        ]
        self.sides = jnp.stack([cube.index >> 4, (cube.index >> 3) & 1, cube.index & 1])
        self.groups = [(self.own, sum(self.shapes[i][1] for i in self.flat))]
        self.groups += [self.shapes[i] for i in self.tall]

    def message(self, come, own, places, lead=1, packed=0):
        wide = self.cube.wide
        split = 2
        n_grads, n_groups = len(self.grads), len(self.groups)
        n_ins = n_grads + len(come)
        widths = [n for _, n in self.groups]
        stack = [-(-r // self.own) for r, _ in self.groups]

        def kernel(sides_ref, *refs):
            ins, outs = refs[:n_ins], refs[n_ins:]
            flat = [ins[i][0, 0] for i in self.flat]
            values = [flat[0] if len(flat) == 1 else jnp.concatenate(flat, axis=1)]
            values += [ins[i][0, 0] for i in self.tall]
            for k, ref in enumerate(ins[n_grads:]):
                got = ref[...]
                got = got.reshape(got.shape[-2:])
                i = k % n_groups
                values[i] = values[i].astype(f32) + got.astype(f32)
            if not packed:
                for out_ref, value in zip(outs, values, strict=True):
                    out_ref[...] = value.astype(bf16).reshape(out_ref.shape)
                return
            at = 0
            for value, (r, n), high in zip(values, self.groups, stack, strict=True):
                value = value.astype(f32).reshape(wide // split, r, n)
                for c in range(high):
                    part = value[:, c * self.own : (c + 1) * self.own].astype(bf16)
                    if packed == 1:
                        outs[0][:, : part.shape[1], at : at + n] = part
                    else:
                        side = sides_ref[2]
                        for i in range(0, part.shape[0], 2):
                            for flip, out_ref in enumerate(outs):
                                out_ref[i // 2, : part.shape[1], at : at + n] = jnp.where(
                                    side == flip, part[i], part[i + 1]
                                )
                    at += n

        in_specs = [
            pl.BlockSpec((1, 1, wide * r // split, n), lambda i, j, s: (*own(i, s), j, 0))
            for r, n in self.shapes
        ]
        for k, value in enumerate(come):
            at = places[k // n_groups]
            r, n = self.groups[k % n_groups]
            in_specs.append(
                pl.BlockSpec(
                    (1,) * (value.ndim - 2) + (wide * r // split, n),
                    lambda i, j, s, at=at: (*at(s), j, 0),
                )
            )
        if packed:
            n = sum(w * high for w, high in zip(widths, stack, strict=True))
            high = wide // packed
            out_shape = [jax.ShapeDtypeStruct((high, self.own, n), bf16)] * packed
            out_specs = [
                pl.BlockSpec((high // split, self.own, n), lambda i, j, s: (j, 0, 0))
            ] * packed
        else:
            out_shape = [jax.ShapeDtypeStruct((lead, wide * r, n), bf16) for r, n in self.groups]
            out_specs = [
                pl.BlockSpec((1, wide * r // split, n), lambda i, j, s: (i, j, 0))
                for r, n in self.groups
            ]
        size = sum(int(np.prod(out.shape)) for out in out_shape)
        return pl.pallas_call(
            kernel,
            out_shape=out_shape,
            grid_spec=pltpu.PrefetchScalarGridSpec(
                num_scalar_prefetch=1,
                grid=(lead, split),
                in_specs=in_specs,
                out_specs=out_specs,
            ),
            cost_estimate=cost(
                flops=size, transcendentals=0, bytes_accessed=4 * size
            ),
            name="message",
        )(self.sides, *self.grads, *come)

    def swap(self, values, mask):
        return [self.cube.swap(value, mask) for value in values]

    def to_core(self):
        return self.message([], lambda i, s: (i, 1 - s[1]), [], lead=2)

    def to_x(self, one):
        return self.message(one, lambda i, s: (1 - s[0], s[1]), [lambda s: (1 - s[0],)])

    def to_wide(self, one, two, halved=False):
        places = [lambda s: (s[0],), lambda s: (0,)]
        return self.message(
            [*one, *two], lambda i, s: (s[0], s[1]), places, packed=1 + halved
        )

    def step(self, bit, mine, come):
        blocks, r, n = mine.shape

        def kernel(side_ref, *refs):
            keep_ref, send_ref = refs[-2:]
            side = side_ref[0]
            for i in range(blocks // 2):
                for out_ref, at in ((keep_ref, 2 * i + side), (send_ref, 2 * i + 1 - side)):
                    value = refs[0][at].astype(f32) + refs[1][at].astype(f32)
                    out_ref[i] = value.astype(bf16)

        whole = pl.BlockSpec(mine.shape, lambda i, s: (0, 0, 0))
        half = pl.BlockSpec((blocks // 2, r, n), lambda i, s: (0, 0, 0))
        return pl.pallas_call(
            kernel,
            out_shape=[jax.ShapeDtypeStruct((blocks // 2, r, n), bf16)] * 2,
            grid_spec=pltpu.PrefetchScalarGridSpec(
                num_scalar_prefetch=1,
                grid=(1,),
                in_specs=[whole, whole],
                out_specs=[half, half],
            ),
            cost_estimate=cost(
                flops=mine.size, transcendentals=0, bytes_accessed=6 * mine.size
            ),
            name="step",
        )(((self.cube.index >> bit) & 1).reshape(1), mine, come)

    def finish(self, *come):
        def kernel(*refs):
            ins, outs = refs[: len(come)], refs[len(come) :]
            blocks = [ref[i] for ref in ins for i in range(ref.shape[0])]
            value = blocks[0].astype(f32)
            for block in blocks[1:]:
                value = value + block.astype(f32)
            at = 0
            for i in self.flat:
                n = self.shapes[i][1]
                outs[i][...] = value[:, at : at + n]
                at += n
            for i in self.tall:
                r, n = self.shapes[i]
                for c in range(0, r, self.own):
                    high = min(self.own, r - c)
                    outs[i][c : c + high] = value[:high, at : at + n]
                    at += n

        size = sum(value.size for value in come)
        return pl.pallas_call(
            kernel,
            out_shape=tuple(jax.ShapeDtypeStruct(shape, f32) for shape in self.shapes),
            cost_estimate=cost(
                flops=size, transcendentals=0, bytes_accessed=4 * size
            ),
            name="finish",
        )(*come)


def tie(*values):
    return lax.optimization_barrier(values)


def pack_shards(parts, widths, rows):
    flat = [part for group in parts for part in group]

    def kernel(*refs):
        ins, outs = refs[: len(flat)], refs[len(flat) :]
        refs_of = iter(ins)
        for out_ref, group in zip(outs, parts, strict=True):
            at = 0
            for array, start, count in group:
                ref, n = next(refs_of), array.shape[1]
                out_ref[:count, at : at + n] = ref[start : start + count, :]
                if count < rows:
                    out_ref[count:, at : at + n] = jnp.zeros((rows - count, n), bf16)
                at += n

    return pl.pallas_call(
        kernel,
        out_shape=tuple(jax.ShapeDtypeStruct((rows, n), bf16) for n in widths),
        name="pack",
    )(*[part[0] for part in flat])


def rms_norm(value, gain):
    return value * lax.rsqrt(jnp.mean(value * value, axis=-1, keepdims=True) + epsilon) * gain


def gelu_tanh(value):
    return jax.nn.gelu(value, approximate=True)


def on_device(
    targets,
    memory,
    cotangent,
    target_len,
    memory_len,
    self_query,
    self_key,
    self_value,
    self_out,
    cross_query,
    cross_key,
    cross_value,
    cross_out,
    ff_gate,
    ff_up,
    ff_down,
    self_gain,
    cross_gain,
    ff_gain,
    position_bias,
    narrow,
    wide,
):
    cube = Cube(narrow, wide)
    pairs, length, width = targets.shape
    slots = pairs * length
    own, own_ff = self_query.shape[0], ff_down.shape[0]
    inner = ff_gate.shape[1]
    devices = cube.size
    stepped = narrow == 4 and wide == 8 and own % 8 == 0

    gains = jnp.stack([self_gain, cross_gain, ff_gain], axis=1)
    gains = jnp.pad(gains, ((0, 0), (0, LANES - 3)))
    stack = -(-own_ff // own)
    whole = lambda *arrays: [(array, 0, own) for array in arrays]
    self_shard, cross_shard, ff_shard = pack_shards(
        [
            whole(self_query, self_key, self_value, self_out, gains),
            whole(cross_query, cross_key, cross_value, cross_out),
            [(ff_down, c * own, min(own, own_ff - c * own)) for c in range(stack)]
            + whole(ff_gate, ff_up),
        ],
        [4 * width + LANES, 4 * width, 2 * inner + stack * width],
        own,
    )
    places = jnp.arange(length)
    apart = places[:, None] - places[None, :]
    bucket = bucket_of_distance(length, BUCKETS, REACH)
    starts = [int(np.argmax(bucket >= b)) for b in range(1, int(bucket[-1]) + 1)]
    bucket_matrix = sum((apart >= start).astype(jnp.int32) for start in starts)
    onehot = (bucket_matrix[:, :, None] == jnp.arange(BUCKETS)[None, None, :]).astype(bf16)
    bias = jnp.einsum("ijb,bh->hij", onehot, position_bias, preferred_element_type=f32)
    bias = jnp.where((apart >= 0)[None], bias, negative).astype(bf16)

    exchange = lambda value: lax.all_to_all(
        value, "wide", split_axis=0, concat_axis=0, tiled=True
    )
    gathered = lax.all_gather(self_shard, BOTH, axis=0, tiled=True)
    ff = lax.all_gather(ff_shard, BOTH, axis=0, tiled=True)
    if stepped:
        cross_gather = Gather(cube, cross_shard, 2 * width)
        one, two, bias = cross_gather.half(bias)
        most = cross_gather.most(one, two)
        memory, most[0] = tie(memory, most[0])
        gathered, *most = tie(gathered, *most)
        c_query_key, c_value_out = cross_gather.finish(most)
    else:
        cross = lax.all_gather(cross_shard, BOTH, axis=0, tiled=True)
        c_query_key, c_value_out = cross[:, : 2 * width], cross[:, 2 * width :]
    memory_rows = exchange(memory).reshape(wide, pairs, -1, width)
    w_qkv, s_out = gathered[:, : 3 * width], gathered[:, 3 * width : 4 * width]
    c_query, c_out = c_query_key[:, :width], c_value_out[:, width:]

    gains = gathered[:, 4 * width : 4 * width + 3].astype(f32).T
    gain_one, gain_two, gain_three = gains[0], gains[1], gains[2]
    live = (places[None, :] < target_len[:, None]).astype(f32).reshape(slots, 1)
    inputs = targets.astype(f32).reshape(slots, width)

    normed_one = rms_norm(inputs, gain_one).astype(bf16)
    cube_of = lambda value: value.reshape(pairs, length, -1)
    qkv_one = cube_of(dot(normed_one, w_qkv, NN).astype(bf16))
    mixed_one, total_one = self_forward(qkv_one, bias)
    mixed_one = mixed_one.reshape(slots, width)
    first = inputs + dot(mixed_one, s_out, NN)
    normed_two = rms_norm(first, gain_two).astype(bf16)
    query_two = cube_of(dot(normed_two, c_query, NN).astype(bf16))
    held = ()
    for p in range(pairs):
        held = cross_forward(
            p, query_two, memory_rows, c_query_key, c_value_out, memory_len, held
        )
    mixed_two, total_two, key_two, value_two = held
    mixed_two = mixed_two.reshape(slots, width)
    second = first + dot(mixed_two, c_out, NN)

    stacked = stack * width
    if stepped:
        layer_out, grad_second, d_gain_three, ff_grads = feed_forward(
            second, gain_three, live, cotangent.reshape(slots, width), ff, inner, own
        )
        d_gain_three = d_gain_three.reshape(width)
    else:
        f_gate, f_up = ff[:, stacked : stacked + inner], ff[:, stacked + inner :]
        f_down = ff[:, :stacked].reshape(devices, own, stack, width).swapaxes(1, 2)
        f_down = f_down.reshape(devices, -1, width)[:, :own_ff].reshape(inner, width)
        normed_three = rms_norm(second, gain_three).astype(bf16)
        gate = dot(normed_three, f_gate, NN)
        upward = dot(normed_three, f_up, NN)
        activated, gelu_pull = jax.vjp(gelu_tanh, gate)
        hidden = (activated * upward).astype(bf16)
        third = second + dot(hidden, f_down, NN)
        layer_out = (third * live).astype(bf16)
        grad_third = cotangent.astype(f32).reshape(slots, width) * live
        branch_ff = grad_third.astype(bf16)
        d_down = dot(hidden, branch_ff, TN).astype(bf16)
        grad_hidden = dot(branch_ff, f_down, NT)
        grad_gate = gelu_pull(grad_hidden * upward)[0].astype(bf16)
        grad_up = (grad_hidden * activated).astype(bf16)
        d_gate = dot(normed_three, grad_gate, TN).astype(bf16)
        d_up = dot(normed_three, grad_up, TN).astype(bf16)
        grad_normed_three = dot(grad_gate, f_gate, NT) + dot(grad_up, f_up, NT)
        d_down = d_down.reshape(devices, own_ff, width)
        d_down = jnp.pad(d_down, ((0, 0), (0, stack * own - own_ff), (0, 0)))
        d_down = d_down.reshape(devices, stack, own, width).swapaxes(1, 2)
        d_down = d_down.reshape(devices * own, stacked)
        ff_grads = jnp.concatenate([d_down, d_gate, d_up], axis=1)
        _, norm_three = jax.vjp(rms_norm, second, gain_three)
        back_three, d_gain_three = norm_three(grad_normed_three)
        grad_second = grad_third + back_three
    layer_out = layer_out.reshape(pairs, length, width)
    ff_grads = lax.psum_scatter(ff_grads, BOTH, scatter_dimension=0, tiled=True)

    branch_cross = grad_second.astype(bf16)
    d_cross_out = dot(mixed_two, branch_cross, TN).astype(bf16)
    grad_mixed_two = cube_of(dot(branch_cross, c_out, NT).astype(bf16))
    held = ()
    for p in range(pairs):
        grad_query_two, rows_grad, *found = cross_backward(
            p,
            query_two,
            key_two,
            value_two,
            memory_len,
            total_two,
            grad_mixed_two,
            memory_rows,
            c_query_key,
            c_value_out,
            held,
        )
        held = (*held[:-2], *found, grad_query_two, rows_grad)
    d_cross_key, d_cross_value = found
    grad_memory = exchange(rows_grad.reshape(memory.shape))
    grad_query_two = grad_query_two.reshape(slots, width)
    d_cross_query = dot(normed_two, grad_query_two, TN).astype(bf16)
    _, norm_two = jax.vjp(rms_norm, first, gain_two)
    back_two, d_gain_two = norm_two(dot(grad_query_two, c_query, NT))
    grad_first = grad_second + back_two

    branch_self = grad_first.astype(bf16)
    d_self_out = dot(mixed_one, branch_self, TN).astype(bf16)
    grad_mixed_one = cube_of(dot(branch_self, s_out, NT).astype(bf16))
    middle = [d_cross_query, d_cross_key, d_cross_value, d_cross_out, d_self_out]
    if stepped:
        middle_sum = Scatter(cube, middle)
        middle_one = middle_sum.swap(middle_sum.to_core(), 8)
        middle_send = middle_sum.to_x(middle_one)
        grad_mixed_one, *middle_send = tie(grad_mixed_one, *middle_send)
        middle_two = middle_sum.swap(middle_send, 16)
    grads_one, diagonals = self_backward(qkv_one, bias, total_one, grad_mixed_one)
    grads_one = grads_one.reshape(slots, 3 * width)
    d_qkv = dot(normed_one, grads_one, TN).astype(bf16)
    if stepped:
        last_sum = Scatter(cube, [d_qkv])
        last_send = last_sum.to_core()
        grads_one, diagonals, *tied = tie(grads_one, diagonals, *middle_two, *last_send)
        middle_two, last_send = tied[: len(middle_two)], tied[len(middle_two) :]
        last_one = last_sum.swap(last_send, 8)
        middle_keep, middle_send = middle_sum.to_wide(middle_one, middle_two, halved=True)
        grads_one, middle_send = tie(grads_one, middle_send)
        middle_come = cube.swap(middle_send, 1)
    if stepped:
        last_send = last_sum.to_x(last_one)
        grads_one, *last_send = tie(grads_one, *last_send)
        last_two = last_sum.swap(last_send, 16)
    grad_normed_one = dot(grads_one, w_qkv, NT)
    _, norm_one = jax.vjp(rms_norm, inputs, gain_one)
    back_one, d_gain_one = norm_one(grad_normed_one)
    grad_targets = (grad_first + back_one).reshape(pairs, length, width)
    if stepped:
        last_two[0], middle_come, grad_memory, grad_targets = tie(
            last_two[0], middle_come, grad_memory, grad_targets
        )
        middle_keep, middle_send = middle_sum.step(1, middle_keep, middle_come)
        middle_come = cube.swap(middle_send, 2)

    padded = diagonals.shape[-1]
    column = (padded - np.arange(length)) % padded
    to_bucket = np.zeros((padded, BUCKETS), np.float32)
    to_bucket[column, bucket] = 1.0
    diagonals = jnp.sum(diagonals, axis=2).reshape(HEADS, padded)
    d_position = jnp.einsum(
        "hc,cb->bh", diagonals, jnp.asarray(to_bucket), precision=lax.Precision.HIGHEST
    )
    small = jnp.concatenate(
        [d_gain_one, d_gain_two, d_gain_three, d_position.reshape(-1)]
    ).reshape(-1, LANES)
    small = jnp.pad(small, ((0, -small.shape[0] % 8), (0, 0)))
    near = range(wide.bit_length() - 1, cube.bits)
    far = range(wide.bit_length() - 1)
    small = cube.total(small, near)
    if stepped:
        last_two[0], small = tie(last_two[0], small)
        last_keep, last_send = last_sum.to_wide(last_one, last_two, halved=True)
        last_come = cube.swap(last_send, 1)
        middle_keep, middle_send = middle_sum.step(2, middle_keep, middle_come)
        middle_come = cube.swap(middle_send, 4)
        last_keep, last_send = last_sum.step(1, last_keep, last_come)
        last_come = cube.swap(last_send, 2)
        middle_grads = middle_sum.finish(middle_keep, middle_come)
        last_keep, last_send = last_sum.step(2, last_keep, last_come)
        last_send, ff_grads = tie(last_send, ff_grads)
        last_come = cube.swap(last_send, 4)
        (d_qkv,) = last_sum.finish(last_keep, last_come)
    else:
        scatter = lambda value: lax.psum_scatter(
            value, BOTH, scatter_dimension=0, tiled=True
        ).astype(f32)
        middle_grads = [scatter(value) for value in middle]
        d_qkv = scatter(d_qkv)
    small = cube.total(small, far).reshape(-1)
    gain_grads = small[: 3 * width].reshape(3, devices, width // devices)
    gain_grads = lax.dynamic_index_in_dim(gain_grads, cube.index, 1, keepdims=False)
    grad_position = small[3 * width : 3 * width + BUCKETS * HEADS].reshape(BUCKETS, HEADS)

    ff_grads = ff_grads.astype(f32)
    d_down = jnp.concatenate(
        [ff_grads[:, c * width : (c + 1) * width] for c in range(stack)], axis=0
    )[:own_ff]
    return (
        layer_out,
        grad_targets,
        grad_memory.astype(f32),
        d_qkv[:, :width],
        d_qkv[:, width : 2 * width],
        d_qkv[:, 2 * width :],
        middle_grads[4],
        *middle_grads[:4],
        ff_grads[:, stacked : stacked + inner],
        ff_grads[:, stacked + inner :],
        d_down,
        gain_grads[0],
        gain_grads[1],
        gain_grads[2],
        grad_position,
    )


def solution(mesh):
    rows = P(BOTH, None)
    slots = P(BOTH, None, None)
    one = P(BOTH)
    source = P("narrow", "wide", None)
    in_specs = (slots, source, slots, one, one) + (rows,) * 11 + (one,) * 3 + (P(),)
    out_specs = (slots, slots, source) + (rows,) * 11 + (one,) * 3 + (P(),)
    narrow, wide = mesh.shape["narrow"], mesh.shape["wide"]

    def body(*args):
        return on_device(*args, narrow=narrow, wide=wide)

    return jax.shard_map(body, mesh=mesh, in_specs=in_specs, out_specs=out_specs, check_vma=False)
```
